32 devices in a mesh: seq: 4 (over y, x), row: 8 (over z, core).
Axes of the slice: x: 2, y: 2, z: 4, core: 2. Of those that a mesh axis runs over, the one named last changes fastest.
Arguments:
- tokens: bfloat16 [16, 1024, 512], P('row', 'seq'), may hold values from -7.2 to 7.2
- cotangent: bfloat16 [16, 1024, 512], P('row', 'seq'), may hold values from -6 to 6
- contig_lengths: int32 [16, 8], P('row'), may hold values from 1 to 256, 1024 in all within a row
- conv_weight: float32 [9, 512, 512], P(None, 'row'), may hold values from -0.09375 to 0.09375
- inner_weight: float32 [512, 2048], P('row'), may hold values from -0.25 to 0.25
- outer_weight: float32 [2048, 512], P('row'), may hold values from -0.125 to 0.125
- vectors: float32 [10, 512], replicated, may hold values from -0.75 to 1.4, as said below
- conv_moments: float32 [2, 9, 512, 512], P(None, None, 'row'), may hold values from -0.00015623207 to 0.00015623207, as said below
- inner_moments: float32 [2, 512, 2048], P(None, 'row'), may hold values from -0.00015623207 to 0.00015623207, as said below
- outer_moments: float32 [2, 2048, 512], P(None, 'row'), may hold values from -0.00015623207 to 0.00015623207, as said below
- vector_moments: float32 [2, 10, 512], replicated, may hold values from -0.00015623207 to 0.00015623207, as said below
Outputs:
- layer_out: bfloat16 [16, 1024, 512], P('row', 'seq')
- input_grad: float32 [16, 1024, 512], P('row', 'seq')
- global_norm: float32 [], replicated
- new_conv: float32 [9, 512, 512], P(None, 'row')
- conv_first: float32 [9, 512, 512], P(None, 'row')
- new_inner: float32 [512, 2048], P('row')
- inner_first: float32 [512, 2048], P('row')
- new_outer: float32 [2048, 512], P('row')
- outer_first: float32 [2048, 512], P('row')
- new_vectors: float32 [10, 512], replicated
- vector_first: float32 [10, 512], replicated
- second_moments: float32 [512, 8714], P('row')
The draws below stay inside these ranges and needn't reach their ends.
Inputs may be any that keep to these rules, and one draw needn't show every extreme that they name: `contig_lengths`: each row's contig lengths sum to 1024; contigs lie one after another from base 0. `vectors`: rows 1 and 4 lie in 0.6 to 1.4. `conv_moments`: second moments are positive. `inner_moments`: second moments are positive. `outer_moments`: second moments are positive. `vector_moments`: second moments are positive.
All inputs are finite; a program needn't handle non-finite values.
Results may differ from the reference program's by a relative error of at most 0.0062.
Values may be sent and summed in bfloat16 or wider, within the bound.
No kernel may reach another device: no remote copies, remote signals or barrier semaphores. Data moves between devices by JAX's collectives and lax.ppermute only.
A program may use at most 128 MiB of HBM per device.

```python
import math
import jax
import jax.numpy as jnp
import numpy as np
from jax import lax

D = 512
FF = 2048
KERNEL_TAPS = 9
DILATION_STEP = 8
L = 1024
CONTIGS = 8
ROWS = 16


def draw_tokens(key, part):
    key = jax.random.fold_in(key, 101)
    channel = jnp.arange(D, dtype=jnp.float32) / D
    channel_ramp = 0.6 * 3.0 ** channel
    values = jax.random.truncated_normal(key, -4.0, 4.0, (ROWS, L, D), jnp.float32) * channel_ramp
    return values.astype(jnp.bfloat16)


def draw_vectors(key, part):
    key = jax.random.fold_in(key, 202)
    noise_key, gain_key = jax.random.split(key)
    shifts = 0.25 * jax.random.truncated_normal(noise_key, -3.0, 3.0, (10, D), jnp.float32)
    gains = jax.random.uniform(gain_key, (10, D), jnp.float32, 0.6, 1.4)
    row_index = jnp.arange(10)
    is_gain = (row_index == 1) | (row_index == 4)
    return jnp.where(is_gain[:, None], gains, shifts)


def moment_pair(key, tensor_shape):
    grad_scale = (KERNEL_TAPS * D * D + 2 * D * FF + 10 * D) ** (-0.5)
    first_key, second_key = jax.random.split(key)
    first_moment = 0.11 * grad_scale * jax.random.truncated_normal(first_key, -3.0, 3.0, tensor_shape, jnp.float32)
    second_moment = 0.001 * grad_scale * grad_scale * jnp.exp(jax.random.uniform(second_key, tensor_shape, jnp.float32, 0.0, math.log(4.0)))
    return jnp.stack([first_moment, second_moment])


def draw_conv_moments(key, part):
    return moment_pair(jax.random.fold_in(key, 303), (KERNEL_TAPS, D, D))


def draw_inner_moments(key, part):
    return moment_pair(jax.random.fold_in(key, 404), (D, FF))


def draw_outer_moments(key, part):
    return moment_pair(jax.random.fold_in(key, 505), (FF, D))


def draw_vector_moments(key, part):
    return moment_pair(jax.random.fold_in(key, 606), (10, D))


def steps_of(rng, extent, shards, low, largest):
    level = 1.0
    for dim, blocks in shards:
        draws = jax.random.uniform(jax.random.fold_in(jax.random.fold_in(rng, 6), dim), (blocks,), jnp.float32, low / len(shards), largest / len(shards))
        level = level * jnp.repeat(jnp.exp(draws), extent[dim] // blocks).reshape((-1,) + (1,) * (len(extent) - 1 - dim))
    return level


def split_up(count, total, most, slope):
    weights = [(1 << 20) // math.isqrt(rank ** slope) + 1 for rank in range(2, count + 1)]
    rest, given = total - most - (count - 1), [1] * (count - 1)
    while rest > 0:
        movable = [i for i in range(count - 1) if given[i] < most]
        mass, budget = sum([weights[i] for i in movable]), rest
        for i in movable:
            addition = min(most - given[i], max(1, budget * weights[i] // mass), rest)
            given[i] = given[i] + addition
            rest = rest - addition
    return np.array([most] + given)


def ragged_sizes(rng, amount, total, reach, skew):
    if amount == 2:
        one = jax.random.randint(rng, (), max(1, total - reach), min(reach, total - 1) + 1)
        return jnp.stack([one, total - one])
    lengths = jnp.asarray(split_up(amount, total, reach, skew), jnp.int32)
    pairs = (amount - 1) // 2
    donor, taker = lengths[1:1 + 2 * pairs:2], lengths[2:2 + 2 * pairs:2]
    slack = jnp.minimum(donor - 1, reach - taker)
    passed = jax.random.randint(jax.random.fold_in(rng, 1), (pairs,), 0, 1 << 20) % (slack + 1)
    lengths = lengths.at[1:1 + 2 * pairs:2].set(donor - passed).at[2:2 + 2 * pairs:2].set(taker + passed)
    return lengths[jax.random.permutation(jax.random.fold_in(rng, 2), amount)]


def noise(own_key, dims, spread, bound, shards=(), held_as=jnp.bfloat16):
    gain = steps_of(own_key, dims, shards, -0.22, 0.18) if shards else 1.0
    array = jax.random.normal(own_key, dims, jnp.float32) * spread * gain
    return jnp.minimum(jnp.maximum(array, -bound), bound).astype(held_as)


def setup_inputs(seed: int = 0) -> dict:
    arg_keys = jax.random.split(jax.random.key(seed), 12)
    tokens = draw_tokens(jax.random.fold_in(arg_keys[11], 71), 0)
    cotangent = noise(arg_keys[1], (ROWS, L, D), 1.0, 6.0, ((0, 8), (1, 4)))
    contig_lengths = jax.vmap(lambda own: ragged_sizes(own, CONTIGS, L, L // 4, 1))(jax.random.split(arg_keys[2], ROWS)).reshape((ROWS, CONTIGS)).astype(jnp.int32)
    conv_weight = noise(arg_keys[3], (KERNEL_TAPS, D, D), (KERNEL_TAPS * D) ** -0.5, 0.09375, ((1, 8),), jnp.float32)
    inner_weight = noise(arg_keys[4], (D, FF), D ** -0.5, 0.25, ((0, 8),), jnp.float32)
    outer_weight = noise(arg_keys[5], (FF, D), FF ** -0.5, 0.125, ((0, 8),), jnp.float32)
    vectors = draw_vectors(jax.random.fold_in(arg_keys[11], 71), 0)
    conv_moments = draw_conv_moments(jax.random.fold_in(arg_keys[11], 71), 0)
    inner_moments = draw_inner_moments(jax.random.fold_in(arg_keys[11], 71), 0)
    outer_moments = draw_outer_moments(jax.random.fold_in(arg_keys[11], 71), 0)
    vector_moments = draw_vector_moments(jax.random.fold_in(arg_keys[11], 71), 0)
    return dict(tokens=tokens, cotangent=cotangent, contig_lengths=contig_lengths, conv_weight=conv_weight, inner_weight=inner_weight, outer_weight=outer_weight, vectors=vectors, conv_moments=conv_moments, inner_moments=inner_moments, outer_moments=outer_moments, vector_moments=vector_moments)


@jax.custom_vjp
def low(v):
    return lax.optimization_barrier(v.astype(jnp.bfloat16)).astype(jnp.float32)

@jax.custom_vjp
def low_back(v):
    return v

def low_keep(v):
    return (low(v), None)

def low_pass(kept, grad):
    return (grad,)

def back_keep(v):
    return (v, None)

def back_low(kept, grad):
    return (low(grad),)
low.defvjp(low_keep, low_pass)
low_back.defvjp(back_keep, back_low)
highest = lax.Precision.HIGHEST
beta_one = 0.9
beta_two = 0.999
adam_eps = 1e-08
weight_decay = 0.1
matrix_rate = 0.03
vector_rate = 0.3
clip_level = 1.0
step_count = 10
norm_eps = 1e-05

def layer_norm(feature, gain_row, shift_row):
    average = lax.optimization_barrier(jnp.mean(feature, axis=-1, keepdims=True))
    centered = feature - average
    variance = lax.optimization_barrier(jnp.mean(centered * centered, axis=-1, keepdims=True))
    return centered * lax.rsqrt(variance + norm_eps) * gain_row + shift_row

def gelu_exact(preact):
    return jax.nn.gelu(preact, approximate=False)

def tap_masks(contig_lengths, row_length):
    half_span_width = DILATION_STEP * (KERNEL_TAPS // 2)
    starts = jnp.cumsum(contig_lengths, axis=1)[:, :-1]
    position = jnp.arange(row_length + 2 * half_span_width, dtype=jnp.int32) - half_span_width
    contig_of = lax.optimization_barrier(jnp.sum((position[None, :, None] >= starts[:, None, :]).astype(jnp.int32), axis=2))
    inside = (position >= 0) & (position < row_length)
    centre = contig_of[:, half_span_width:half_span_width + row_length]
    mask_list = []
    for kernel_tap_index in range(KERNEL_TAPS):
        begin_position = kernel_tap_index * DILATION_STEP
        mask_list.append((contig_of[:, begin_position:begin_position + row_length] == centre) & inside[None, begin_position:begin_position + row_length])
    return mask_list

def forward(tokens, conv_weight, inner_weight, outer_weight, vectors, mask_list):
    row_length = tokens.shape[1]
    half_span_width = DILATION_STEP * (KERNEL_TAPS // 2)
    conv_low = low(conv_weight)
    inner_low = low(inner_weight)
    outer_low = low(outer_weight)
    padded = jnp.pad(tokens, ((0, 0), (half_span_width, half_span_width), (0, 0)))
    conv_pre = vectors[0]
    for kernel_tap_index in range(KERNEL_TAPS):
        begin_position = kernel_tap_index * DILATION_STEP
        product = jnp.einsum('rld,de->rle', padded[:, begin_position:begin_position + row_length], conv_low[kernel_tap_index], precision=highest)
        conv_pre = conv_pre + jnp.where(mask_list[kernel_tap_index][:, :, None], product, 0.0)
    conv_pre = low_back(conv_pre)
    after_conv = tokens + layer_norm(gelu_exact(conv_pre), vectors[1], vectors[2])
    inner_pre = jnp.einsum('rld,df->rlf', low(after_conv), inner_low, precision=highest) + vectors[6:].reshape(-1)
    inner_pre = low_back(inner_pre)
    hidden = low(gelu_exact(inner_pre))
    outer_pre = jnp.einsum('rlf,fd->rld', hidden, outer_low, precision=highest) + vectors[3]
    outer_pre = low_back(outer_pre)
    return after_conv + layer_norm(outer_pre, vectors[4], vectors[5])

def adamw(weight, moments, gradient, clip_scale, step_rate, decay_rate):
    clipped = gradient * clip_scale
    first_moment = beta_one * moments[0] + (1.0 - beta_one) * clipped
    second_moment = beta_two * moments[1] + (1.0 - beta_two) * clipped * clipped
    first_hat = first_moment / (1.0 - beta_one ** step_count)
    second_hat = second_moment / (1.0 - beta_two ** step_count)
    updated = weight - step_rate * (first_hat / (jnp.sqrt(second_hat) + adam_eps) + decay_rate * weight)
    return (updated, first_moment, second_moment)

def reference(tokens, cotangent, contig_lengths, conv_weight, inner_weight, outer_weight, vectors, conv_moments, inner_moments, outer_moments, vector_moments):
    group_rows = math.gcd(ROWS, max(1, 4096 // L))
    group_count = ROWS // group_rows
    token_groups = tokens.astype(jnp.float32).reshape(group_count, group_rows, L, D)
    back_groups = cotangent.astype(jnp.float32).reshape(group_count, group_rows, L, D)
    length_groups = contig_lengths.reshape(group_count, group_rows, CONTIGS)

    def one_group(running, pieces):
        rows_in, rows_back, rows_len = pieces
        mask_list = tap_masks(rows_len, L)

        def wrapped(token_part, conv_part, inner_part, outer_part, vector_part):
            return forward(token_part, conv_part, inner_part, outer_part, vector_part, mask_list)
        result, pullback = jax.vjp(wrapped, rows_in, conv_weight, inner_weight, outer_weight, vectors)
        gradients = pullback(rows_back)
        running = tuple((so_far + addend for so_far, addend in zip(running, gradients[1:])))
        return (running, (result.astype(jnp.bfloat16), gradients[0]))
    start_sums = (jnp.zeros(conv_weight.shape, jnp.float32), jnp.zeros(inner_weight.shape, jnp.float32), jnp.zeros(outer_weight.shape, jnp.float32), jnp.zeros(vectors.shape, jnp.float32))
    sums, (outputs, input_grads) = lax.scan(one_group, start_sums, (token_groups, back_groups, length_groups))
    conv_grad, inner_grad, outer_grad, vector_grad = sums
    squares = jnp.sum(conv_grad * conv_grad) + jnp.sum(inner_grad * inner_grad) + jnp.sum(outer_grad * outer_grad) + jnp.sum(vector_grad * vector_grad)
    global_norm = jnp.sqrt(squares)
    clip_scale = clip_level / jnp.maximum(global_norm, clip_level)
    new_conv, conv_first, conv_second = adamw(conv_weight, conv_moments, conv_grad, clip_scale, matrix_rate, weight_decay)
    new_inner, inner_first, inner_second = adamw(inner_weight, inner_moments, inner_grad, clip_scale, matrix_rate, weight_decay)
    new_outer, outer_first, outer_second = adamw(outer_weight, outer_moments, outer_grad, clip_scale, matrix_rate, weight_decay)
    new_vectors, vector_first, vector_second = adamw(vectors, vector_moments, vector_grad, clip_scale, vector_rate, 0.0)
    second_moments = jnp.concatenate([jnp.transpose(conv_second, (1, 0, 2)).reshape(D, KERNEL_TAPS * D), inner_second, outer_second.reshape(D, FF), jnp.transpose(vector_second)], axis=1)
    return (outputs.reshape(ROWS, L, D), input_grads.reshape(ROWS, L, D), global_norm, new_conv, conv_first, new_inner, inner_first, new_outer, outer_first, new_vectors, vector_first, second_moments)
```

```python
import functools

import jax
import jax.numpy as jnp
from jax import lax
from jax.experimental import pallas as pl
from jax.experimental.pallas import tpu as pltpu
from jax.sharding import PartitionSpec as P

DILATION_STEP = 8

beta_one = 0.9
beta_two = 0.999
adam_eps = 1e-08
weight_decay = 0.1
matrix_rate = 0.03
vector_rate = 0.3
clip_level = 1.0
step_count = 10
norm_eps = 1e-05

F32 = jnp.float32
BF = jnp.bfloat16
VEC_PAD = 16
LANES = 128
SQRT_HALF = 0.7071067811865476
PDF_SCALE = 0.3989422804014327


def exchange(value, axis, mask):
    size = lax.axis_size(axis)
    return lax.ppermute(value, axis, [(i, i ^ mask) for i in range(size)])


def shift_along(value, axis, step):
    size = lax.axis_size(axis)
    pairs = [(i, i + step) for i in range(size) if 0 <= i + step < size]
    return lax.ppermute(value, axis, pairs)


def gelu_parts(v):
    cdf = 0.5 + 0.5 * lax.erf(v * SQRT_HALF)
    return v * cdf, cdf


def gelu_slope(v, cdf):
    return cdf + v * (jnp.exp(-0.5 * v * v) * PDF_SCALE)


def mean_of(v):
    return jnp.mean(v, axis=-1, keepdims=True)


def normalized(v):
    centred = v - mean_of(v)
    scale = lax.rsqrt(mean_of(centred * centred) + norm_eps)
    return centred * scale, scale


def fold_rows(v):
    rows, cols = v.shape
    return jnp.sum(v.reshape(rows // 8, 8, cols), axis=0)


def column_sum(acc):
    return jnp.sum(acc, axis=0, keepdims=True)


def loop_rows(total, step, body, init=0):
    return lax.fori_loop(
        0, total // step, lambda i, carry: body(pl.multiple_of(i * step, step), carry), init
    )


def dot(a, b):
    return jnp.dot(a, b, preferred_element_type=F32)


def dot_nt(a, b):
    return lax.dot_general(a, b, (((1,), (1,)), ((), ())), preferred_element_type=F32)


def dot_tn(a, b):
    return lax.dot_general(a, b, (((0,), (0,)), ((), ())), preferred_element_type=F32)


def place():
    seq_at = lax.axis_index("seq")
    row_at = lax.axis_index("row")
    return seq_at, row_at // 2, row_at % 2


def at(index, step):
    return pl.ds(pl.multiple_of(index * step, step), step)


def vmem_call(kernel, outs, scratch=(), smem=0, inputs=0, flops=0, nbytes=0, **kw):
    return pl.pallas_call(
        kernel,
        out_shape=[jax.ShapeDtypeStruct(shape, dtype) for shape, dtype in outs],
        in_specs=[pl.BlockSpec(memory_space=pltpu.SMEM)] * smem
        + [pl.BlockSpec(memory_space=pltpu.VMEM)] * inputs,
        out_specs=[pl.BlockSpec(memory_space=pltpu.VMEM)] * len(outs),
        scratch_shapes=list(scratch),
        cost_estimate=pl.CostEstimate(flops=flops, bytes_accessed=nbytes, transcendentals=0),
        compiler_params=pltpu.CompilerParams(vmem_limit_bytes=60 * 1024 * 1024),
        **kw,
    )


def contigs(lens_ref, row, positions, row_length):
    found = jnp.zeros(positions.shape, jnp.int32)
    start = jnp.int32(0)
    for j in range(lens_ref.shape[1] - 1):
        start = start + lens_ref[row, j]
        found = found + (positions >= start).astype(jnp.int32)
    found = jnp.where(positions < 0, -1, found)
    return jnp.where(positions >= row_length, lens_ref.shape[1], found)


def masked_taps(src, cid, length, taps, half, store):
    centre = cid[pl.ds(half, length), :]

    def body(tap, carry):
        begin = pl.multiple_of(tap * DILATION_STEP, DILATION_STEP)
        keep = cid[pl.ds(begin, length), :] == centre
        for a in range(src.shape[1] // LANES):
            part = src[pl.ds(begin, length), a * LANES : (a + 1) * LANES]
            store(tap, a, jnp.where(keep, part, 0.0).astype(BF))
        return carry

    lax.fori_loop(0, taps, body, 0)


def conv_kernel(taps, nz, ns, *refs):
    lens, tok, left, right, vec, own, other = refs[:7]
    pieces = (refs[7 : 7 + ns], refs[7 + ns : 7 + 2 * ns])
    pre, after, full, ext, cid, cat = refs[7 + 2 * ns :]
    seq_at, z_at, core_at = place()
    rows, length, width = tok.shape
    in_rows = own.shape[1]
    quarter = width // ns
    half = DILATION_STEP * (taps // 2)
    for i, whole in enumerate((own, other)):
        block = z_at * 2 + (core_at ^ i)
        for t in range(taps):
            full[t, at(block, in_rows), :] = whole[t]
        for j in range(1, nz):
            block = (z_at ^ j) * 2 + (core_at ^ i)
            for k in range(ns):
                for t in range(taps):
                    full[t, at(block, in_rows), at(seq_at ^ k, quarter)] = pieces[i][k][j - 1, t]
    span = length + 2 * half
    base = seq_at * length - half
    positions = base + lax.broadcasted_iota(jnp.int32, (span, LANES), 0)
    for r in range(rows):
        ext[0:half, :] = left[r].astype(F32)
        ext[half : half + length, :] = tok[r].astype(F32)
        ext[half + length :, :] = right[r].astype(F32)
        cid[...] = contigs(lens, r, positions, length * ns)

        def store(tap, a, value, r=r):
            cat[r * length : (r + 1) * length, at(tap * (width // LANES) + a, LANES)] = value

        masked_taps(ext, cid, length, taps, half, store)
    weights = full.reshape(taps * width, width)

    def product(r, carry):
        where = at(r, length)
        pre[where, :] = dot(cat[where, :], weights[...]) + vec[0:1, :]
        return carry

    lax.fori_loop(0, rows, product, 0)

    for r in range(rows):

        def norm(begin, carry, r=r):
            where = pl.ds(r * length + begin, 32)
            active, _ = gelu_parts(pre[where, :])
            unit, _ = normalized(active)
            after[where, :] = (
                tok[r, pl.ds(begin, 32), :].astype(F32) + unit * vec[1:2, :] + vec[2:3, :]
            )
            return carry

        loop_rows(length, 32, norm)


def ffn_kernel(nz, ns, *refs):
    pre, after, cot, vec, inner_own, outer_own, inner_other, outer_other = refs[:8]
    pieces = (refs[8 : 8 + ns], refs[8 + ns : 8 + 2 * ns])
    rest = refs[8 + 2 * ns :]
    layer, after_grad, conv_grad = rest[:3]
    sends = rest[3 : 3 + ns]
    low, hidden, outer_grad, inner_grad, inner, outer, slope, tmp, sums = rest[3 + ns :]
    seq_at, z_at, core_at = place()
    count, width = pre.shape
    in_rows, hid = inner_own.shape
    out_rows = outer_own.shape[0]
    part = out_rows // ns
    quarter = hid // ns
    blocks = hid // width
    for i, (one, two) in enumerate(((inner_own, outer_own), (inner_other, outer_other))):
        block = z_at * 2 + (core_at ^ i)
        inner[at(block, in_rows), :] = one[...]
        outer[at(block, out_rows), :] = two[...]
        for j in range(1, nz):
            block = (z_at ^ j) * 2 + (core_at ^ i)
            for k in range(ns):
                inner[at(block, in_rows), at(seq_at ^ k, quarter)] = pieces[i][k][j - 1, :in_rows]
                outer[at(block * ns + (seq_at ^ k), part), :] = pieces[i][k][j - 1, in_rows:]

    def lower(begin, carry):
        where = pl.ds(begin, 64)
        low[where, :] = after[where, :].astype(BF)
        return carry

    loop_rows(count, 64, lower)

    def up(b, carry):
        cols = at(b, width)
        tmp[...] = dot(low[...], inner[:, cols]) + vec[pl.ds(6 + b, 1), :]

        def act(begin, inside):
            where = pl.ds(begin, 32)
            v = tmp[where, :]
            active, cdf = gelu_parts(v)
            hidden[where, cols] = active.astype(BF)
            slope[where, cols] = gelu_slope(v, cdf)
            return inside

        loop_rows(count, 32, act)
        return carry

    lax.fori_loop(0, blocks, up, 0)
    tmp[...] = dot(hidden[...], outer[...]) + vec[3:4, :]
    zero = jnp.zeros((8, width), F32)

    def second(begin, carry):
        bias_sum, gain_sum, shift_sum = carry
        where = pl.ds(begin, 32)
        unit, scale = normalized(tmp[where, :])
        gain = vec[4:5, :]
        layer[where, :] = (after[where, :] + unit * gain + vec[5:6, :]).astype(BF)
        dy = cot[where, :].astype(F32)
        u = dy * gain
        grad = (scale * (u - mean_of(u) - unit * mean_of(u * unit))).astype(BF)
        outer_grad[where, :] = grad
        return (
            bias_sum + fold_rows(grad.astype(F32)),
            gain_sum + fold_rows(dy * unit),
            shift_sum + fold_rows(dy),
        )

    totals = loop_rows(count, 32, second, (zero, zero, zero))
    sums[...] = jnp.zeros(sums.shape, F32)
    for i, total in enumerate(totals):
        sums[3 + i : 4 + i, :] = column_sum(total)

    def down(b, carry):
        cols = at(b, width)
        tmp[...] = dot_nt(outer_grad[...], outer[cols, :])

        def act(begin, total):
            where = pl.ds(begin, 32)
            grad = (tmp[where, :] * slope[where, cols]).astype(BF)
            inner_grad[where, cols] = grad
            return total + fold_rows(grad.astype(F32))

        total = loop_rows(count, 32, act, zero)
        sums[pl.ds(6 + b, 1), :] = column_sum(total)
        return carry

    lax.fori_loop(0, blocks, down, 0)
    tmp[...] = dot_nt(inner_grad[...], inner[...])

    def first(begin, carry):
        bias_sum, gain_sum, shift_sum = carry
        where = pl.ds(begin, 32)
        upstream = cot[where, :].astype(F32) + tmp[where, :]
        after_grad[where, :] = upstream
        v = pre[where, :]
        active, cdf = gelu_parts(v)
        unit, scale = normalized(active)
        u = upstream * vec[1:2, :]
        grad = scale * (u - mean_of(u) - unit * mean_of(u * unit))
        grad = (grad * gelu_slope(v, cdf)).astype(BF)
        conv_grad[where, :] = grad
        return (
            bias_sum + fold_rows(grad.astype(F32)),
            gain_sum + fold_rows(upstream * unit),
            shift_sum + fold_rows(upstream),
        )

    totals = loop_rows(count, 32, first, (zero, zero, zero))
    for i, total in enumerate(totals):
        sums[i : i + 1, :] = column_sum(total)
    span = width // ns
    for k in range(ns):
        sends[k][0:count, :] = conv_grad[:, at(seq_at ^ k, span)]
        encode(sends[k], count, spread(sums[...]))


def spread(v):
    return jnp.concatenate(
        [v[:, a * LANES : (a + 1) * LANES] for a in range(v.shape[1] // LANES)], axis=0
    )


def gathered(v):
    return jnp.concatenate(
        [v[a * VEC_PAD : (a + 1) * VEC_PAD, :] for a in range(v.shape[0] // VEC_PAD)], axis=1
    )


def encode(ref, begin, v):
    rows = v.shape[0]
    high = v.astype(BF)
    ref[begin : begin + rows, :] = high
    ref[begin + rows : begin + 2 * rows, :] = (v - high.astype(F32)).astype(BF)


def decode(ref, begin, rows):
    high = ref[begin : begin + rows, :].astype(F32)
    return high + ref[begin + rows : begin + 2 * rows, :].astype(F32)


def tree_sum(values):
    values = list(values)
    while len(values) > 1:
        values = [values[i] + values[i + 1] for i in range(0, len(values), 2)]
    return values[0]


def ffn_weight_kernel(nz, ns, in_rows, out_rows, *refs):
    low, hidden, outer_grad, inner_grad, mine, theirs, outer_sum, inner_sum = refs
    seq_at, z_at, core_at = place()
    width = low.shape[1]
    hid = hidden.shape[1]
    part = out_rows // ns
    quarter = hid // ns

    def product(b, carry):
        cols = at(b, width)
        outer_sum[cols, :] = dot_tn(hidden[:, cols], outer_grad[...]).astype(BF)
        inner_sum[:, cols] = dot_tn(low[...], inner_grad[:, cols]).astype(BF)
        return carry

    lax.fori_loop(0, hid // width, product, 0)
    for i, out in enumerate((mine, theirs)):
        for k in range(ns):
            for j in range(nz):
                block = (z_at ^ j) * 2 + (core_at ^ i)
                out[k, j, :in_rows] = inner_sum[at(block, in_rows), at(seq_at ^ k, quarter)]
                out[k, j, in_rows:] = outer_sum[at(block * ns + (seq_at ^ k), part), :]


def conv_weight_kernel(taps, nz, ns, in_rows, *refs):
    lens = refs[0]
    toks = refs[1 : 1 + ns]
    grads = refs[1 + ns : 1 + 2 * ns]
    mine, theirs, padded, cid, cat, total = refs[1 + 2 * ns :]
    seq_at, z_at, core_at = place()
    rows, length, width = toks[0].shape
    span = width // ns
    half = DILATION_STEP * (taps // 2)
    row_length = ns * length
    count = rows * length
    positions = lax.broadcasted_iota(jnp.int32, (row_length + 2 * half, LANES), 0) - half
    edge = jnp.zeros((half, span), F32)
    for r in range(rows):
        padded[0:half, :] = edge
        padded[half + row_length :, :] = edge
        cid[...] = contigs(lens, r, positions, row_length)
        for k in range(ns):
            padded[pl.ds(half + (seq_at ^ k) * length, length), :] = grads[k][
                r * length : (r + 1) * length, :
            ].astype(F32)
        for k in range(ns):
            base = (seq_at ^ k) * length
            centre = cid[pl.ds(pl.multiple_of(base + half, 8), length), :]
            for t in range(taps):
                begin = pl.multiple_of(base + DILATION_STEP * (taps - 1 - t), 8)
                keep = cid[pl.ds(begin, length), :] == centre
                value = jnp.where(keep, padded[pl.ds(begin, length), :], 0.0)
                low_row = k * count + r * length
                cat[low_row : low_row + length, t * span : (t + 1) * span] = value.astype(BF)
    for k in range(ns):
        value = tree_sum(
            [
                dot_tn(toks[k][r], cat[k * count + r * length : k * count + (r + 1) * length, :])
                for r in range(rows)
            ]
        )
        if k == 0:
            total[...] = value
        else:
            total[...] += value
    for i, out in enumerate((mine, theirs)):
        for j in range(nz):
            block = (z_at ^ j) * 2 + (core_at ^ i)
            for t in range(taps):
                begin = (j * taps + t) * in_rows
                out[begin : begin + in_rows, :] = total[
                    at(block, in_rows), t * span : (t + 1) * span
                ].astype(BF)
    vec_rows = (grads[0].shape[0] - count) // 2
    summed = tree_sum([decode(g, count, vec_rows) for g in grads])
    for out in (mine, theirs):
        encode(out, nz * taps * in_rows, summed)


def input_grad_kernel(taps, ns, *refs):
    lens, grad, left, right, after_grad, full, out, ext, cid, cat = refs
    seq_at = lax.axis_index("seq")
    rows, half, width = left.shape
    length = grad.shape[0] // rows
    base = seq_at * length - half
    positions = base + lax.broadcasted_iota(jnp.int32, (length + 2 * half, LANES), 0)
    for r in range(rows):
        ext[0:half, :] = left[r].astype(F32)
        ext[half : half + length, :] = grad[r * length : (r + 1) * length, :].astype(F32)
        ext[half + length :, :] = right[r].astype(F32)
        cid[...] = contigs(lens, r, positions, length * ns)

        def store(tap, a, value, r=r):
            flipped = taps - 1 - tap
            cat[
                flipped, r * length : (r + 1) * length, a * LANES : (a + 1) * LANES
            ] = value

        masked_taps(ext, cid, length, taps, half, store)

    out[...] = after_grad[...]

    def product(t, carry):
        out[...] += dot_nt(cat[t], full[t])
        return carry

    lax.fori_loop(0, taps, product, 0)


def split_sum_kernel(count, *refs):
    ins, outs = refs[:count], refs[count:]
    rows = outs[0].shape[0]
    for p, out in enumerate(outs):

        def body(begin, carry, p=p, out=out):
            where = pl.ds(p * rows + begin, 64)
            out[pl.ds(begin, 64), :] = tree_sum([v[where, :].astype(F32) for v in ins]).astype(BF)
            return carry

        loop_rows(rows, 64, body)


def split_sum(ins, parts):
    rows, cols = ins[0].shape
    return vmem_call(
        functools.partial(split_sum_kernel, len(ins)),
        [((rows // parts, cols), BF)] * parts,
        inputs=len(ins),
        flops=rows * cols * len(ins),
        nbytes=2 * rows * cols * (len(ins) + 1),
    )(*ins)


def conv_core_kernel(rows, mine, got, *outs):
    vec_rows = (mine.shape[0] - rows * len(outs)) // 2
    begin_vec = rows * len(outs)
    summed = decode(mine, begin_vec, vec_rows) + decode(got, begin_vec, vec_rows)
    for p, out in enumerate(outs):

        def body(begin, carry, p=p, out=out):
            where = pl.ds(p * rows + begin, 64)
            out[pl.ds(begin, 64), :] = (mine[where, :].astype(F32) + got[where, :].astype(F32)).astype(
                BF
            )
            return carry

        loop_rows(rows, 64, body)
        encode(out, rows, summed)


def final_kernel(count, vec_rows, *refs):
    ins, outs = refs[:count], refs[count:]
    out, square = outs[:2]
    rows = out.shape[0]

    def body(begin, carry):
        where = pl.ds(begin, 64)
        value = tree_sum([v[where, :].astype(F32) for v in ins]).astype(BF)
        out[where, :] = value
        wide = value.astype(F32)
        folded = fold_rows(wide * wide)
        return carry + sum(
            folded[:, a * LANES : (a + 1) * LANES] for a in range(folded.shape[1] // LANES)
        )

    square[...] = loop_rows(rows, 64, body, jnp.zeros((8, LANES), F32))
    if vec_rows:
        outs[2][...] = gathered(tree_sum([decode(v, rows, vec_rows) for v in ins]))


def adam_math(weight, first, second, gradient, clip, rate, decay):
    clipped = gradient * clip
    first = beta_one * first + (1.0 - beta_one) * clipped
    second = beta_two * second + (1.0 - beta_two) * clipped * clipped
    first_hat = first / (1.0 - beta_one**step_count)
    second_hat = second / (1.0 - beta_two**step_count)
    weight = weight - rate * (first_hat / (jnp.sqrt(second_hat) + adam_eps) + decay * weight)
    return weight, first, second


def adam_kernel(taps, ns, *refs):
    conv_grads, ffn_grads = refs[:ns], refs[ns : 2 * ns]
    vec_sum, squares, conv, inner, outer, vec, conv_m, inner_m, outer_m, vec_m = refs[
        2 * ns : 2 * ns + 10
    ]
    (
        norm,
        new_conv,
        conv_first,
        new_inner,
        inner_first,
        new_outer,
        outer_first,
        new_vec,
        vec_first,
        second,
        outer_second,
        vec_second,
    ) = refs[2 * ns + 10 :]
    seq_at, z_at, core_at = place()
    in_rows, width = conv.shape[1:]
    hid = inner.shape[1]
    out_rows = outer.shape[0]
    span = width // ns
    quarter = hid // ns
    part = out_rows // ns
    vec_count = vec.shape[0]
    vec_grad = vec_sum[0:vec_count, :]
    total = jnp.sum(squares[...]) + jnp.sum(vec_grad * vec_grad)
    value = jnp.sqrt(jnp.full((1, 1), total, F32))
    norm[...] = value
    clip = clip_level / jnp.maximum(value, clip_level)

    for k in range(ns):
        cols = at(seq_at ^ k, span)

        def conv_step(t, carry, k=k, cols=cols):
            w, m, v = adam_math(
                conv[t, :, cols],
                conv_m[0, t, :, cols],
                conv_m[1, t, :, cols],
                conv_grads[k][at(t, in_rows), :].astype(F32),
                clip,
                matrix_rate,
                weight_decay,
            )
            new_conv[t, :, cols] = w
            conv_first[t, :, cols] = m
            second[:, at(t * ns + (seq_at ^ k), span)] = v
            return carry

        lax.fori_loop(0, taps, conv_step, 0)
        for a in range(quarter // LANES):
            lanes = pl.ds(pl.multiple_of((seq_at ^ k) * quarter + a * LANES, LANES), LANES)
            w, m, v = adam_math(
                inner[:, lanes],
                inner_m[0, :, lanes],
                inner_m[1, :, lanes],
                ffn_grads[k][0:in_rows, a * LANES : (a + 1) * LANES].astype(F32),
                clip,
                matrix_rate,
                weight_decay,
            )
            new_inner[:, lanes] = w
            inner_first[:, lanes] = m
            second[
                :, pl.ds(pl.multiple_of(taps * width + (seq_at ^ k) * quarter + a * LANES, LANES), LANES)
            ] = v
        where = at(seq_at ^ k, part)
        for a in range(width // LANES):
            lanes = slice(a * LANES, (a + 1) * LANES)
            w, m, v = adam_math(
                outer[where, lanes],
                outer_m[0, where, lanes],
                outer_m[1, where, lanes],
                ffn_grads[k][in_rows:, lanes].astype(F32),
                clip,
                matrix_rate,
                weight_decay,
            )
            new_outer[where, lanes] = w
            outer_first[where, lanes] = m
            outer_second[a, where, :] = v
    ratio = out_rows // in_rows
    base = taps * width + hid
    for e in range(ratio):
        for a in range(width // LANES):
            begin = base + e * width + a * LANES
            second[:, begin : begin + LANES] = outer_second[a, pl.ds(e, in_rows, stride=ratio), :]
    w, m, v = adam_math(vec[...], vec_m[0], vec_m[1], vec_grad, clip, vector_rate, 0.0)
    new_vec[...] = w
    vec_first[...] = m
    v = jnp.concatenate([v, jnp.zeros((LANES - vec_count, width), F32)], axis=0)
    vec_second[...] = jnp.transpose(v)
    begin = base + ratio * width
    block = z_at * 2 + core_at
    second[:, begin : begin + vec_count] = vec_second[at(block, in_rows), :][:, 0:vec_count]


def per_device(
    tokens,
    cotangent,
    contig_lengths,
    conv_weight,
    inner_weight,
    outer_weight,
    vectors,
    conv_moments,
    inner_moments,
    outer_moments,
    vector_moments,
):
    ns = lax.axis_size("seq")
    nr = lax.axis_size("row")
    nz = nr // 2
    seq_at = lax.axis_index("seq")
    rows, length, width = tokens.shape
    taps, in_rows, _ = conv_weight.shape
    hid = inner_weight.shape[1]
    out_rows = outer_weight.shape[0]
    count = rows * length
    half = DILATION_STEP * (taps // 2)
    span = width // ns
    quarter = hid // ns
    part = out_rows // ns

    left = shift_along(tokens[:, length - half :], "seq", 1)
    right = shift_along(tokens[:, :half], "seq", -1)

    conv_own = conv_weight.astype(BF)
    conv_part = lax.dynamic_slice_in_dim(conv_weight, seq_at * span, span, 2).astype(BF)
    got = [exchange(conv_part, "row", 2 * j) for j in range(1, nz)]
    got = jnp.stack(got)
    conv_pieces = [got] + [exchange(got, "seq", k) for k in range(1, ns)]
    conv_other = exchange(conv_own, "row", 1)
    conv_other_pieces = [exchange(p, "row", 1) for p in conv_pieces]

    inner_own = inner_weight.astype(BF)
    outer_own = outer_weight.astype(BF)
    ffn_part = jnp.concatenate(
        [
            lax.dynamic_slice_in_dim(inner_weight, seq_at * quarter, quarter, 1),
            lax.dynamic_slice_in_dim(outer_weight, seq_at * part, part, 0),
        ],
        axis=0,
    ).astype(BF)
    got = jnp.stack([exchange(ffn_part, "row", 2 * j) for j in range(1, nz)])
    ffn_pieces = [got] + [exchange(got, "seq", k) for k in range(1, ns)]
    inner_other = exchange(inner_own, "row", 1)
    outer_other = exchange(outer_own, "row", 1)
    ffn_other_pieces = [exchange(p, "row", 1) for p in ffn_pieces]

    pre, after, conv_full = vmem_call(
        functools.partial(conv_kernel, taps, nz, ns),
        [((count, width), F32), ((count, width), F32), ((taps, width, width), BF)],
        [
            pltpu.VMEM((length + 2 * half, width), F32),
            pltpu.VMEM((length + 2 * half, LANES), jnp.int32),
            pltpu.VMEM((count, taps * width), BF),
        ],
        smem=1,
        inputs=6 + 2 * ns,
        flops=2 * count * taps * width * width,
        nbytes=4 * taps * width * width,
    )(
        contig_lengths,
        tokens,
        left,
        right,
        vectors,
        conv_own,
        conv_other,
        *conv_pieces,
        *conv_other_pieces,
    )

    tokens_late, _ = lax.optimization_barrier((tokens, ffn_pieces[-1]))
    token_pieces = [tokens] + [exchange(tokens_late, "seq", k) for k in range(1, ns)]

    results = vmem_call(
        functools.partial(ffn_kernel, nz, ns),
        [((count, width), BF), ((count, width), F32), ((count, width), BF)]
        + [((count + 2 * VEC_PAD * width // LANES, span), BF)] * ns
        + [((count, width), BF), ((count, hid), BF), ((count, width), BF), ((count, hid), BF)],
        [
            pltpu.VMEM((width, hid), BF),
            pltpu.VMEM((hid, width), BF),
            pltpu.VMEM((count, hid), F32),
            pltpu.VMEM((count, width), F32),
            pltpu.VMEM((VEC_PAD, width), F32),
        ],
        inputs=8 + 2 * ns,
        flops=8 * count * width * hid,
        nbytes=20 * width * hid,
    )(
        pre,
        after,
        cotangent.reshape(count, width),
        vectors,
        inner_own,
        outer_own,
        inner_other,
        outer_other,
        *ffn_pieces,
        *ffn_other_pieces,
    )
    layer_out, after_grad, conv_grad = results[:3]
    grad_pieces = list(results[3 : 3 + ns])
    low, hidden, outer_grad, inner_grad = results[3 + ns :]
    grad_pieces = grad_pieces[:1] + [exchange(grad_pieces[k], "seq", k) for k in range(1, ns)]

    conv_grad_rows = conv_grad.reshape(rows, length, width)
    grad_left = shift_along(conv_grad_rows[:, length - half :], "seq", 1)
    grad_right = shift_along(conv_grad_rows[:, :half], "seq", -1)

    ffn_rows = in_rows + part
    mine, theirs = vmem_call(
        functools.partial(ffn_weight_kernel, nz, ns, in_rows, out_rows),
        [((ns, nz, ffn_rows, width), BF)] * 2,
        [pltpu.VMEM((hid, width), BF), pltpu.VMEM((width, hid), BF)],
        inputs=4,
        flops=4 * count * width * hid,
        nbytes=8 * width * hid,
    )(low, hidden, outer_grad, inner_grad)
    arrived = exchange(theirs, "row", 1)
    flat = (ns * nz * ffn_rows, width)
    sums = split_sum([mine.reshape(flat), arrived.reshape(flat)], ns)
    sums = [sums[0]] + [exchange(sums[k], "seq", k) for k in range(1, ns)]
    sums = split_sum(sums, nz)
    sums = [sums[0]] + [exchange(sums[j], "row", 2 * j) for j in range(1, nz)]
    ffn_sum, ffn_square = vmem_call(
        functools.partial(final_kernel, nz, 0),
        [((ffn_rows, width), BF), ((8, LANES), F32)],
        inputs=nz,
        flops=ffn_rows * width * nz,
        nbytes=2 * ffn_rows * width * nz,
    )(*sums)
    ffn_sums = [ffn_sum] + [exchange(ffn_sum, "seq", k) for k in range(1, ns)]

    vec_rows = VEC_PAD * width // LANES
    conv_rows = taps * in_rows
    mine, theirs = vmem_call(
        functools.partial(conv_weight_kernel, taps, nz, ns, in_rows),
        [((nz * conv_rows + 2 * vec_rows, span), BF)] * 2,
        [
            pltpu.VMEM((ns * length + 2 * half, span), F32),
            pltpu.VMEM((ns * length + 2 * half, LANES), jnp.int32),
            pltpu.VMEM((ns * count, taps * span), BF),
            pltpu.VMEM((width, taps * span), F32),
        ],
        smem=1,
        inputs=2 * ns,
        flops=2 * ns * count * width * taps * span,
        nbytes=8 * count * width * ns,
    )(contig_lengths, *token_pieces, *grad_pieces)
    arrived = exchange(theirs, "row", 1)
    sums = vmem_call(
        functools.partial(conv_core_kernel, conv_rows),
        [((conv_rows + 2 * vec_rows, span), BF)] * nz,
        inputs=2,
        flops=4 * conv_rows * nz * span,
        nbytes=8 * conv_rows * nz * span,
    )(mine, arrived)
    sums = [sums[0]] + [exchange(sums[j], "row", 2 * j) for j in range(1, nz)]
    conv_sum, conv_square, vec_sum = vmem_call(
        functools.partial(final_kernel, nz, vec_rows),
        [((conv_rows, span), BF), ((8, LANES), F32), ((VEC_PAD, width), F32)],
        inputs=nz,
        flops=conv_rows * span * nz,
        nbytes=2 * conv_rows * span * nz,
    )(*sums)
    conv_sums = [conv_sum] + [exchange(conv_sum, "seq", k) for k in range(1, ns)]
    square = conv_square + ffn_square
    squares = lax.all_to_all(
        jnp.broadcast_to(square[None], (ns * nr, 8, LANES)), ("seq", "row"), 0, 0
    )

    (input_grad,) = vmem_call(
        functools.partial(input_grad_kernel, taps, ns),
        [((count, width), F32)],
        [
            pltpu.VMEM((length + 2 * half, width), F32),
            pltpu.VMEM((length + 2 * half, LANES), jnp.int32),
            pltpu.VMEM((taps, count, width), BF),
        ],
        smem=1,
        inputs=5,
        flops=2 * count * taps * width * width,
        nbytes=2 * taps * width * width,
    )(contig_lengths, conv_grad, grad_left, grad_right, after_grad, conv_full)

    second_width = taps * width + hid + (out_rows // in_rows) * width + vectors.shape[0]
    (
        norm,
        new_conv,
        conv_first,
        new_inner,
        inner_first,
        new_outer,
        outer_first,
        new_vectors,
        vector_first,
        second_moments,
    ) = vmem_call(
        functools.partial(adam_kernel, taps, ns),
        [
            ((1, 1), F32),
            (conv_weight.shape, F32),
            (conv_weight.shape, F32),
            (inner_weight.shape, F32),
            (inner_weight.shape, F32),
            (outer_weight.shape, F32),
            (outer_weight.shape, F32),
            (vectors.shape, F32),
            (vectors.shape, F32),
            ((in_rows, second_width), F32),
        ],
        [
            pltpu.VMEM((width // LANES, out_rows, LANES), F32),
            pltpu.VMEM((width, LANES), F32),
        ],
        inputs=2 * ns + 10,
        flops=20 * in_rows * second_width,
        nbytes=28 * in_rows * second_width,
    )(
        *conv_sums,
        *ffn_sums,
        vec_sum,
        squares,
        conv_weight,
        inner_weight,
        outer_weight,
        vectors,
        conv_moments,
        inner_moments,
        outer_moments,
        vector_moments,
    )
    return (
        layer_out.reshape(tokens.shape),
        input_grad.reshape(tokens.shape),
        norm.reshape(()),
        new_conv,
        conv_first,
        new_inner,
        inner_first,
        new_outer,
        outer_first,
        new_vectors,
        vector_first,
        second_moments,
    )


def solution(mesh):
    in_specs = (
        P("row", "seq", None),
        P("row", "seq", None),
        P("row", None),
        P(None, "row", None),
        P("row", None),
        P("row", None),
        P(),
        P(None, None, "row", None),
        P(None, "row", None),
        P(None, "row", None),
        P(),
    )
    out_specs = (
        P("row", "seq", None),
        P("row", "seq", None),
        P(),
        P(None, "row", None),
        P(None, "row", None),
        P("row", None),
        P("row", None),
        P("row", None),
        P("row", None),
        P(),
        P(),
        P("row", None),
    )
    return jax.shard_map(
        per_device, mesh=mesh, in_specs=in_specs, out_specs=out_specs, check_vma=False
    )
```

```python
import functools

import jax
import jax.numpy as jnp
from jax import lax
from jax.experimental import pallas as pl
from jax.experimental.pallas import tpu as pltpu
from jax.sharding import PartitionSpec as P

DILATION_STEP = 8

beta_one = 0.9
beta_two = 0.999
adam_eps = 1e-08
weight_decay = 0.1
matrix_rate = 0.03
vector_rate = 0.3
clip_level = 1.0
step_count = 10
norm_eps = 1e-05

F32 = jnp.float32
BF = jnp.bfloat16
VEC_PAD = 16
LANES = 128
SQRT_HALF = 0.7071067811865476
PDF_SCALE = 0.3989422804014327


def exchange(value, axis, mask):
    size = lax.axis_size(axis)
    return lax.ppermute(value, axis, [(i, i ^ mask) for i in range(size)])


def shift_along(value, axis, step):
    size = lax.axis_size(axis)
    pairs = [(i, i + step) for i in range(size) if 0 <= i + step < size]
    return lax.ppermute(value, axis, pairs)


def gelu_parts(v):
    cdf = 0.5 + 0.5 * lax.erf(v * SQRT_HALF)
    return v * cdf, cdf


def gelu_slope(v, cdf):
    return cdf + v * (jnp.exp(-0.5 * v * v) * PDF_SCALE)


def mean_of(v):
    return jnp.mean(v, axis=-1, keepdims=True)


def normalized(v):
    centred = v - mean_of(v)
    scale = lax.rsqrt(mean_of(centred * centred) + norm_eps)
    return centred * scale, scale


def fold_rows(v):
    rows, cols = v.shape
    return jnp.sum(v.reshape(rows // 8, 8, cols), axis=0)


def column_sum(acc):
    return jnp.sum(acc, axis=0, keepdims=True)


def loop_rows(total, step, body, init=0):
    return lax.fori_loop(
        0, total // step, lambda i, carry: body(pl.multiple_of(i * step, step), carry), init
    )


def dot(a, b):
    return jnp.dot(a, b, preferred_element_type=F32)


def dot_nt(a, b):
    return lax.dot_general(a, b, (((1,), (1,)), ((), ())), preferred_element_type=F32)


def dot_tn(a, b):
    return lax.dot_general(a, b, (((0,), (0,)), ((), ())), preferred_element_type=F32)


def place():
    seq_at = lax.axis_index("seq")
    row_at = lax.axis_index("row")
    return seq_at, row_at // 2, row_at % 2


def at(index, step):
    return pl.ds(pl.multiple_of(index * step, step), step)


def size_of(shape, dtype):
    total = jnp.dtype(dtype).itemsize
    for n in shape:
        total *= n
    return total


def vmem_call(kernel, outs, scratch=(), smem=0, loose=(), kept=(), left=(), slack=6):
    space = pl.BlockSpec(memory_space=pltpu.VMEM)
    anywhere = pl.BlockSpec(memory_space=pl.ANY)
    grant = slack * 1024 * 1024
    grant += sum(size_of(v.shape, v.dtype) for v in scratch if hasattr(v, "shape") and v.dtype in (F32, BF, jnp.int32))
    grant += sum(size_of(*outs[i]) for i in kept)

    def call(*args):
        fixed = [
            a
            if i < smem or i in loose
            else pltpu.with_memory_space_constraint(a, pltpu.VMEM)
            for i, a in enumerate(args)
        ]
        return pl.pallas_call(
            kernel,
            out_shape=[
                jax.ShapeDtypeStruct(shape, dtype) if i in kept or i in left else pltpu.VMEM(shape, dtype)
                for i, (shape, dtype) in enumerate(outs)
            ],
            in_specs=[
                pl.BlockSpec(memory_space=pltpu.SMEM) if i < smem else anywhere if i in loose else space
                for i in range(len(args))
            ],
            out_specs=[anywhere if i in left else space for i in range(len(outs))],
            scratch_shapes=list(scratch),
            cost_estimate=pl.CostEstimate(flops=1, bytes_accessed=1, transcendentals=0),
            compiler_params=pltpu.CompilerParams(vmem_limit_bytes=grant),
        )(*fixed)

    return call


def begin_copies(pairs, sems):
    copies = [pltpu.make_async_copy(src, dst, sems.at[i]) for i, (src, dst) in enumerate(pairs)]
    for copy in copies:
        copy.start()
    return copies


def end_copies(copies):
    for copy in copies:
        copy.wait()


def contigs(lens_ref, row, positions, row_length):
    found = jnp.zeros(positions.shape, jnp.int32)
    start = jnp.int32(0)
    for j in range(lens_ref.shape[1] - 1):
        start = start + lens_ref[row, j]
        found = found + (positions >= start).astype(jnp.int32)
    found = jnp.where(positions < 0, -1, found)
    return jnp.where(positions >= row_length, lens_ref.shape[1], found)


def masked_taps(src, cid, length, taps, half, store):
    centre = cid[pl.ds(half, length), :]

    def body(tap, carry):
        begin = pl.multiple_of(tap * DILATION_STEP, DILATION_STEP)
        keep = cid[pl.ds(begin, length), :] == centre
        for a in range(src.shape[1] // LANES):
            part = src[pl.ds(begin, length), a * LANES : (a + 1) * LANES]
            store(tap, a, jnp.where(keep, part, 0.0).astype(BF))
        return carry

    lax.fori_loop(0, taps, body, 0)


def cut_kernel(ns, conv, tok, part, left_edge, right_edge):
    seq_at = lax.axis_index("seq")
    half = left_edge.shape[1]
    part[...] = conv[:, :, at(seq_at, conv.shape[2] // ns)].astype(BF)
    left_edge[...] = tok[:, :half, :]
    right_edge[...] = tok[:, tok.shape[1] - half :, :]


def round_kernel(ns, conv, inner, outer, vec_m, conv_own, ffn_own, ffn_part, vec_m_near):
    seq_at = lax.axis_index("seq")
    in_rows, hid = inner.shape
    quarter = hid // ns
    part = outer.shape[0] // ns
    conv_own[...] = conv[...].astype(BF)
    for k in range(ns):
        ffn_own[k * in_rows : (k + 1) * in_rows, :] = inner[
            :, k * quarter : (k + 1) * quarter
        ].astype(BF)
    ffn_own[ns * in_rows :, :] = outer[...].astype(BF)
    ffn_part[:in_rows, :] = inner[:, at(seq_at, quarter)].astype(BF)
    ffn_part[in_rows:, :] = outer[at(seq_at, part), :].astype(BF)
    vec_m_near[...] = vec_m[...]


def stack_kernel(*refs):
    for i, ref in enumerate(refs[:-1]):
        refs[-1][i] = ref[...]


def conv_kernel(taps, nz, ns, lens, vec, tok, left, right, own, other, *rest):
    pieces = (rest[:ns], rest[ns : 2 * ns])
    pre, after, full, ext, cid, cat, sems = rest[2 * ns :]
    seq_at, z_at, core_at = place()
    rows, length, width = tok.shape
    quarter = width // ns
    half = DILATION_STEP * (taps // 2)
    pairs = []
    for i, whole in enumerate((own, other)):
        core = core_at ^ i
        pairs.append((whole, full.at[:, z_at, core]))
        for k in range(ns):
            for j in range(1, nz):
                cols = at(seq_at ^ k, quarter)
                pairs.append((pieces[i][k].at[j - 1], full.at[:, z_at ^ j, core, :, cols]))
    copies = begin_copies(pairs, sems)
    span = length + 2 * half
    base = seq_at * length - half
    positions = base + lax.broadcasted_iota(jnp.int32, (span, LANES), 0)
    for r in range(rows):
        ext[0:half, :] = left[r].astype(F32)
        ext[half : half + length, :] = tok[r].astype(F32)
        ext[half + length :, :] = right[r].astype(F32)
        cid[...] = contigs(lens, r, positions, length * ns)

        def store(tap, a, value, r=r):
            cat[r * length : (r + 1) * length, at(tap * (width // LANES) + a, LANES)] = value

        masked_taps(ext, cid, length, taps, half, store)
    end_copies(copies)
    weights = full.reshape(taps * width, width)

    def product(r, carry):
        where = at(r, length)
        pre[where, :] = dot(cat[where, :], weights[...]) + vec[0:1, :]
        return carry

    lax.fori_loop(0, rows, product, 0)

    for r in range(rows):

        def norm(begin, carry, r=r):
            where = pl.ds(r * length + begin, 32)
            active, _ = gelu_parts(pre[where, :])
            unit, _ = normalized(active)
            after[where, :] = (
                tok[r, pl.ds(begin, 32), :].astype(F32) + unit * vec[1:2, :] + vec[2:3, :]
            )
            return carry

        loop_rows(length, 32, norm)


def ffn_kernel(nz, ns, *refs):
    after, cot, vec = refs[:3]
    wholes = refs[3:5]
    pieces = (refs[5 : 5 + ns], refs[5 + ns : 5 + 2 * ns])
    rest = refs[5 + 2 * ns :]
    layer, low, hidden, outer_grad, inner_grad, inner_full, sums, outer_full, slope, tmp, sems = rest
    seq_at, z_at, core_at = place()
    count, width = after.shape
    hid = inner_full.shape[3]
    in_rows = inner_full.shape[2]
    quarter = hid // ns
    blocks = hid // width
    inner = inner_full.reshape(width, hid)
    outer = outer_full.reshape(hid, width)
    part = outer_full.shape[3]
    pairs = []
    for i, whole in enumerate(wholes):
        core = core_at ^ i
        for q in range(ns):
            pairs.append(
                (
                    whole.at[q * in_rows : (q + 1) * in_rows],
                    inner_full.at[z_at, core, :, q * quarter : (q + 1) * quarter],
                )
            )
            pairs.append(
                (
                    whole.at[ns * in_rows + q * part : ns * in_rows + (q + 1) * part],
                    outer_full.at[z_at, core, q],
                )
            )
        for k in range(ns):
            piece = pieces[i][k]
            q = seq_at ^ k
            for j in range(1, nz):
                z = z_at ^ j
                pairs.append((piece.at[j - 1, :in_rows], inner_full.at[z, core, :, at(q, quarter)]))
                pairs.append((piece.at[j - 1, in_rows:], outer_full.at[z, core, q]))
    copies = begin_copies(pairs, sems)

    def lower(begin, carry):
        where = pl.ds(begin, 64)
        low[where, :] = after[where, :].astype(BF)
        return carry

    loop_rows(count, 64, lower)
    end_copies(copies)

    def up(b, carry):
        cols = at(b, width)
        tmp[...] = dot(low[...], inner[:, cols]) + vec[pl.ds(6 + b, 1), :]

        def act(begin, inside):
            where = pl.ds(begin, 32)
            v = tmp[where, :]
            active, cdf = gelu_parts(v)
            hidden[where, cols] = active.astype(BF)
            slope[where, cols] = gelu_slope(v, cdf)
            return inside

        loop_rows(count, 32, act)
        return carry

    lax.fori_loop(0, blocks, up, 0)
    tmp[...] = dot(hidden[...], outer[...]) + vec[3:4, :]
    zero = jnp.zeros((8, width), F32)

    def second(begin, carry):
        bias_sum, gain_sum, shift_sum = carry
        where = pl.ds(begin, 32)
        unit, scale = normalized(tmp[where, :])
        gain = vec[4:5, :]
        layer[where, :] = (after[where, :] + unit * gain + vec[5:6, :]).astype(BF)
        dy = cot[where, :].astype(F32)
        u = dy * gain
        grad = (scale * (u - mean_of(u) - unit * mean_of(u * unit))).astype(BF)
        outer_grad[where, :] = grad
        return (
            bias_sum + fold_rows(grad.astype(F32)),
            gain_sum + fold_rows(dy * unit),
            shift_sum + fold_rows(dy),
        )

    totals = loop_rows(count, 32, second, (zero, zero, zero))
    sums[...] = jnp.zeros(sums.shape, F32)
    for i, total in enumerate(totals):
        sums[3 + i : 4 + i, :] = column_sum(total)

    def down(b, carry):
        cols = at(b, width)
        tmp[...] = dot_nt(outer_grad[...], outer[cols, :])

        def act(begin, total):
            where = pl.ds(begin, 32)
            grad = (tmp[where, :] * slope[where, cols]).astype(BF)
            inner_grad[where, cols] = grad
            return total + fold_rows(grad.astype(F32))

        total = loop_rows(count, 32, act, zero)
        sums[pl.ds(6 + b, 1), :] = column_sum(total)
        return carry

    lax.fori_loop(0, blocks, down, 0)


def back_kernel(ns, *refs):
    pre, cot, vec, inner_grad, inner_full, partial_sums, after_grad, conv_grad = refs[:8]
    inner = inner_full.reshape(pre.shape[1], inner_grad.shape[1])
    sends = refs[8 : 8 + ns]
    tmp, sums = refs[8 + ns :]
    seq_at = lax.axis_index("seq")
    count, width = pre.shape
    zero = jnp.zeros((8, width), F32)
    sums[...] = partial_sums[...]
    tmp[...] = dot_nt(inner_grad[...], inner[...])

    def first(begin, carry):
        bias_sum, gain_sum, shift_sum = carry
        where = pl.ds(begin, 32)
        upstream = cot[where, :].astype(F32) + tmp[where, :]
        after_grad[where, :] = upstream
        v = pre[where, :]
        active, cdf = gelu_parts(v)
        unit, scale = normalized(active)
        u = upstream * vec[1:2, :]
        grad = scale * (u - mean_of(u) - unit * mean_of(u * unit))
        grad = (grad * gelu_slope(v, cdf)).astype(BF)
        conv_grad[where, :] = grad
        return (
            bias_sum + fold_rows(grad.astype(F32)),
            gain_sum + fold_rows(upstream * unit),
            shift_sum + fold_rows(upstream),
        )

    totals = loop_rows(count, 32, first, (zero, zero, zero))
    for i, total in enumerate(totals):
        sums[i : i + 1, :] = column_sum(total)
    span = width // ns
    for k in range(ns):
        sends[k][0:count, :] = conv_grad[:, at(seq_at ^ k, span)]
        encode(sends[k], count, spread(sums[...]))


def spread(v):
    return jnp.concatenate(
        [v[:, a * LANES : (a + 1) * LANES] for a in range(v.shape[1] // LANES)], axis=0
    )


def gathered(v):
    return jnp.concatenate(
        [v[a * VEC_PAD : (a + 1) * VEC_PAD, :] for a in range(v.shape[0] // VEC_PAD)], axis=1
    )


def encode(ref, begin, v):
    rows = v.shape[0]
    high = v.astype(BF)
    ref[begin : begin + rows, :] = high
    ref[begin + rows : begin + 2 * rows, :] = (v - high.astype(F32)).astype(BF)


def decode(ref, begin, rows):
    high = ref[begin : begin + rows, :].astype(F32)
    return high + ref[begin + rows : begin + 2 * rows, :].astype(F32)


def tree_sum(values):
    values = list(values)
    while len(values) > 1:
        values = [values[i] + values[i + 1] for i in range(0, len(values), 2)]
    return values[0]


def ffn_weight_kernel(nz, ns, in_rows, out_rows, *refs):
    low, hidden, outer_grad, inner_grad, mine, theirs, outer_sum, inner_sum = refs
    seq_at, z_at, core_at = place()
    width = low.shape[1]
    hid = hidden.shape[1]
    part = out_rows // ns
    quarter = hid // ns

    def product(b, carry):
        cols = at(b, width)
        outer_sum[cols, :] = dot_tn(hidden[:, cols], outer_grad[...]).astype(BF)
        inner_sum[:, cols] = dot_tn(low[...], inner_grad[:, cols]).astype(BF)
        return carry

    lax.fori_loop(0, hid // width, product, 0)
    for i, out in enumerate((mine, theirs)):
        for k in range(ns):
            for j in range(nz):
                block = (z_at ^ j) * 2 + (core_at ^ i)
                out[k, j, :in_rows] = inner_sum[at(block, in_rows), at(seq_at ^ k, quarter)]
                out[k, j, in_rows:] = outer_sum[at(block * ns + (seq_at ^ k), part), :]


def conv_weight_kernel(taps, nz, ns, in_rows, *refs):
    lens = refs[0]
    far = refs[1 : 1 + ns]
    grads = refs[1 + ns : 1 + 2 * ns]
    mine, theirs, padded, cid, cat, total, toks, sems = refs[1 + 2 * ns :]
    copies = begin_copies([(far[k], toks.at[k]) for k in range(ns)], sems)
    seq_at, z_at, core_at = place()
    _, rows, length, width = toks.shape
    span = width // ns
    half = DILATION_STEP * (taps // 2)
    row_length = ns * length
    count = rows * length
    positions = lax.broadcasted_iota(jnp.int32, (row_length + 2 * half, LANES), 0) - half
    edge = jnp.zeros((half, span), F32)
    for r in range(rows):
        padded[0:half, :] = edge
        padded[half + row_length :, :] = edge
        cid[...] = contigs(lens, r, positions, row_length)
        for k in range(ns):
            padded[pl.ds(half + (seq_at ^ k) * length, length), :] = grads[k][
                r * length : (r + 1) * length, :
            ].astype(F32)
        for k in range(ns):
            base = (seq_at ^ k) * length
            centre = cid[pl.ds(pl.multiple_of(base + half, 8), length), :]
            for t in range(taps):
                begin = pl.multiple_of(base + DILATION_STEP * (taps - 1 - t), 8)
                keep = cid[pl.ds(begin, length), :] == centre
                value = jnp.where(keep, padded[pl.ds(begin, length), :], 0.0)
                low_row = k * count + r * length
                cat[low_row : low_row + length, t * span : (t + 1) * span] = value.astype(BF)
    end_copies(copies)
    for k in range(ns):
        value = tree_sum(
            [
                dot_tn(toks[k, r], cat[k * count + r * length : k * count + (r + 1) * length, :])
                for r in range(rows)
            ]
        )
        if k == 0:
            total[...] = value
        else:
            total[...] += value
    for i, out in enumerate((mine, theirs)):
        for j in range(nz):
            block = (z_at ^ j) * 2 + (core_at ^ i)
            for t in range(taps):
                begin = (j * taps + t) * in_rows
                out[begin : begin + in_rows, :] = total[
                    at(block, in_rows), t * span : (t + 1) * span
                ].astype(BF)
    vec_rows = (grads[0].shape[0] - count) // 2
    summed = tree_sum([decode(g, count, vec_rows) for g in grads])
    for out in (mine, theirs):
        encode(out, nz * taps * in_rows, summed)


def input_grad_kernel(taps, ns, *refs):
    lens, grad, left, right, after_grad, full_blocks, out, ext, cid, cat = refs
    full = full_blocks.reshape(taps, grad.shape[1], grad.shape[1])
    seq_at = lax.axis_index("seq")
    rows, half, width = left.shape
    length = grad.shape[0] // rows
    base = seq_at * length - half
    positions = base + lax.broadcasted_iota(jnp.int32, (length + 2 * half, LANES), 0)
    for r in range(rows):
        ext[0:half, :] = left[r].astype(F32)
        ext[half : half + length, :] = grad[r * length : (r + 1) * length, :].astype(F32)
        ext[half + length :, :] = right[r].astype(F32)
        cid[...] = contigs(lens, r, positions, length * ns)

        def store(tap, a, value, r=r):
            flipped = taps - 1 - tap
            cat[
                flipped, r * length : (r + 1) * length, a * LANES : (a + 1) * LANES
            ] = value

        masked_taps(ext, cid, length, taps, half, store)

    out[...] = after_grad[...]

    def product(t, carry):
        out[...] += dot_nt(cat[t], full[t])
        return carry

    lax.fori_loop(0, taps, product, 0)


def split_sum_kernel(count, *refs):
    ins, outs = refs[:count], refs[count:]
    rows = outs[0].shape[0]
    for p, out in enumerate(outs):

        def body(begin, carry, p=p, out=out):
            where = pl.ds(p * rows + begin, 64)
            out[pl.ds(begin, 64), :] = tree_sum([v[where, :].astype(F32) for v in ins]).astype(BF)
            return carry

        loop_rows(rows, 64, body)


def split_sum(ins, parts):
    rows, cols = ins[0].shape
    return vmem_call(
        functools.partial(split_sum_kernel, len(ins)),
        [((rows // parts, cols), BF)] * parts,
        slack=2,
    )(*ins)


def conv_core_kernel(rows, mine, got, *outs):
    vec_rows = (mine.shape[0] - rows * len(outs)) // 2
    begin_vec = rows * len(outs)
    summed = decode(mine, begin_vec, vec_rows) + decode(got, begin_vec, vec_rows)
    for p, out in enumerate(outs):

        def body(begin, carry, p=p, out=out):
            where = pl.ds(p * rows + begin, 64)
            out[pl.ds(begin, 64), :] = (mine[where, :].astype(F32) + got[where, :].astype(F32)).astype(
                BF
            )
            return carry

        loop_rows(rows, 64, body)
        encode(out, rows, summed)


def conv_final_kernel(count, vec_rows, *refs):
    ins, (out, square, vec_sum) = refs[:count], refs[count:]
    square[...] = summed_square(ins, out)
    vec_sum[...] = gathered(tree_sum([decode(v, out.shape[0], vec_rows) for v in ins]))


def summed_square(ins, out):
    def body(begin, carry):
        where = pl.ds(begin, 64)
        value = tree_sum([v[where, :].astype(F32) for v in ins]).astype(BF)
        out[where, :] = value
        wide = value.astype(F32)
        return carry + lane_fold(fold_rows(wide * wide))

    rows = ins[0].shape[0] // 64 * 64 if out.shape[0] % 64 else out.shape[0]
    return loop_rows(min(rows, out.shape[0]), 64, body, jnp.zeros((8, LANES), F32))


def lane_fold(v):
    return sum(v[:, a * LANES : (a + 1) * LANES] for a in range(v.shape[1] // LANES))


def ffn_final_kernel(count, *refs):
    ins, (conv_square, out) = refs[:count], refs[count:]
    rows = ins[0].shape[0]
    square = summed_square(ins, out.at[0:rows]) + conv_square[...]
    high = square.astype(BF)
    low = (square - high.astype(F32)).astype(BF)
    zero = jnp.zeros(high.shape, BF)
    tail = jnp.concatenate([high, low] + [zero] * (out.shape[1] // LANES - 2), axis=1)
    out[rows : rows + VEC_PAD, :] = jnp.concatenate([tail, jnp.zeros(tail.shape, BF)], axis=0)


def square_kernel(count, *refs):
    ins, out = refs[:count], refs[count]
    rows = ins[0].shape[0] - VEC_PAD
    parts = []
    for v in ins:
        tail = v[rows : rows + VEC_PAD, :].astype(F32)
        parts.append(tail[:8, :LANES] + tail[:8, LANES : 2 * LANES])
    out[...] = tree_sum(parts)


def small_sum_kernel(*refs):
    refs[-1][...] = tree_sum([v[...] for v in refs[:-1]])


def adam_math(weight, first, second, gradient, clip, rate, decay):
    clipped = gradient * clip
    first = beta_one * first + (1.0 - beta_one) * clipped
    second = beta_two * second + (1.0 - beta_two) * clipped * clipped
    first_hat = first / (1.0 - beta_one**step_count)
    second_hat = second / (1.0 - beta_two**step_count)
    weight = weight - rate * (first_hat / (jnp.sqrt(second_hat) + adam_eps) + decay * weight)
    return weight, first, second


def adam_kernel(taps, ns, *refs):
    conv_grads = refs[:ns]
    ffn_grads = refs[ns : 2 * ns]
    vec_sum, one, two, conv, inner, outer, vec, conv_m, inner_m, outer_m, vec_m = refs[
        2 * ns : 2 * ns + 11
    ]
    norm, new_vec, vec_first = refs[2 * ns + 11 : 2 * ns + 14]
    outs = refs[2 * ns + 14 : 2 * ns + 21]
    new_conv, conv_first, new_inner, inner_first, new_outer, outer_first, second = refs[
        2 * ns + 21 : 2 * ns + 28
    ]
    outer_second, vec_second, sems = refs[2 * ns + 28 :]
    seq_at, z_at, core_at = place()
    in_rows, width = conv.shape[1:]
    hid = inner.shape[1]
    out_rows = outer.shape[0]
    span = width // ns
    quarter = hid // ns
    part = out_rows // ns
    vec_count = vec.shape[0]
    vec_grad = vec_sum[0:vec_count, :]
    total = jnp.sum(one[...] + two[...]) + jnp.sum(vec_grad * vec_grad)
    value = jnp.sqrt(jnp.full((1, 1), total, F32))
    norm[...] = value
    clip = clip_level / jnp.maximum(value, clip_level)
    going = []

    def send(index, src, dst):
        copy = pltpu.make_async_copy(src, dst, sems.at[index])
        copy.start()
        going.append(copy)

    def conv_step(t, carry):
        for k in range(ns):
            cols = at(seq_at ^ k, span)
            w, m, v = adam_math(
                conv[t, :, cols],
                conv_m[0, t, :, cols],
                conv_m[1, t, :, cols],
                conv_grads[k][at(t, in_rows), :].astype(F32),
                clip,
                matrix_rate,
                weight_decay,
            )
            new_conv[t, :, cols] = w
            conv_first[t, :, cols] = m
            second[:, at(t * ns + (seq_at ^ k), span)] = v
        return carry

    lax.fori_loop(0, taps, conv_step, 0)
    send(0, new_conv, outs[0])
    send(1, conv_first, outs[1])
    send(2, second.at[:, : taps * width], outs[6].at[:, : taps * width])
    chunks = quarter // LANES

    for k in range(ns):

        def inner_step(a, carry, k=k):
            lanes = at((seq_at ^ k) * chunks + a, LANES)
            w, m, v = adam_math(
                inner[:, lanes],
                inner_m[0, :, lanes],
                inner_m[1, :, lanes],
                ffn_grads[k][0:in_rows, at(a, LANES)].astype(F32),
                clip,
                matrix_rate,
                weight_decay,
            )
            new_inner[:, lanes] = w
            inner_first[:, lanes] = m
            second[:, at(taps * width // LANES + (seq_at ^ k) * chunks + a, LANES)] = v
            return carry

        lax.fori_loop(0, chunks, inner_step, 0)
    send(3, new_inner, outs[2])
    send(4, inner_first, outs[3])
    for k in range(ns):
        where = at(seq_at ^ k, part)

        def outer_step(a, carry, k=k, where=where):
            lanes = at(a, LANES)
            w, m, v = adam_math(
                outer[where, lanes],
                outer_m[0, where, lanes],
                outer_m[1, where, lanes],
                ffn_grads[k][in_rows : in_rows + part, lanes].astype(F32),
                clip,
                matrix_rate,
                weight_decay,
            )
            new_outer[where, lanes] = w
            outer_first[where, lanes] = m
            outer_second[a, where, :] = v
            return carry

        lax.fori_loop(0, width // LANES, outer_step, 0)
    send(5, new_outer, outs[4])
    send(6, outer_first, outs[5])
    ratio = out_rows // in_rows
    base = taps * width + hid
    for e in range(ratio):
        for a in range(width // LANES):
            begin = base + e * width + a * LANES
            second[:, begin : begin + LANES] = outer_second[a, pl.ds(e, in_rows, stride=ratio), :]
    w, m, v = adam_math(vec[...], vec_m[0], vec_m[1], vec_grad, clip, vector_rate, 0.0)
    new_vec[...] = w
    vec_first[...] = m
    v = jnp.concatenate([v, jnp.zeros((LANES - vec_count, width), F32)], axis=0)
    vec_second[...] = jnp.transpose(v)
    begin = base + ratio * width
    block = z_at * 2 + core_at
    second[:, begin : begin + vec_count] = vec_second[at(block, in_rows), :][:, 0:vec_count]
    send(7, second.at[:, taps * width :], outs[6].at[:, taps * width :])
    end_copies(going)


def per_device(
    tokens,
    cotangent,
    contig_lengths,
    conv_weight,
    inner_weight,
    outer_weight,
    vectors,
    conv_moments,
    inner_moments,
    outer_moments,
    vector_moments,
):
    ns = lax.axis_size("seq")
    nr = lax.axis_size("row")
    nz = nr // 2
    seq_at = lax.axis_index("seq")
    rows, length, width = tokens.shape
    taps, in_rows, _ = conv_weight.shape
    hid = inner_weight.shape[1]
    out_rows = outer_weight.shape[0]
    count = rows * length
    half = DILATION_STEP * (taps // 2)
    span = width // ns
    quarter = hid // ns
    part = out_rows // ns

    ffn_rows = in_rows + part
    vec_rows = VEC_PAD * width // LANES
    conv_rows = taps * in_rows
    cot = cotangent.reshape(count, width)

    conv_part, left_edge, right_edge = vmem_call(
        functools.partial(cut_kernel, ns),
        [((taps, in_rows, span), BF), ((rows, half, width), BF), ((rows, half, width), BF)],
        slack=2,
    )(conv_weight, tokens)
    got = [exchange(conv_part, "row", 2 * j) for j in range(1, nz)]
    left = shift_along(right_edge, "seq", 1)
    right = shift_along(left_edge, "seq", -1)
    conv_own, ffn_own, ffn_part, vector_near = vmem_call(
        functools.partial(round_kernel, ns),
        [
            (conv_weight.shape, BF),
            ((ns * ffn_rows, width), BF),
            ((ffn_rows, width), BF),
            (vector_moments.shape, F32),
        ],
        slack=2,
    )(conv_weight, inner_weight, outer_weight, vector_moments)
    conv_other = exchange(conv_own, "row", 1)
    ffn_other = exchange(ffn_own, "row", 1)
    got[0], left, right = lax.optimization_barrier((got[0], left, right))
    (got,) = vmem_call(stack_kernel, [((nz - 1, taps, in_rows, span), BF)], slack=2)(*got)
    conv_pieces = [got] + [exchange(got, "seq", k) for k in range(1, ns)]
    ffn_part, conv_pieces[1] = lax.optimization_barrier((ffn_part, conv_pieces[1]))
    ffn_got = [exchange(ffn_part, "row", 2 * j) for j in range(1, nz)]
    conv_other_pieces = [exchange(p, "row", 1) for p in conv_pieces]
    (ffn_got,) = vmem_call(stack_kernel, [((nz - 1, ffn_rows, width), BF)], slack=2)(*ffn_got)
    ffn_pieces = [ffn_got] + [exchange(ffn_got, "seq", k) for k in range(1, ns)]

    pre, after, conv_full = vmem_call(
        functools.partial(conv_kernel, taps, nz, ns),
        [((count, width), F32), ((count, width), F32), ((taps, nz, 2, in_rows, width), BF)],
        [
            pltpu.VMEM((length + 2 * half, width), F32),
            pltpu.VMEM((length + 2 * half, LANES), jnp.int32),
            pltpu.VMEM((count, taps * width), BF),
            pltpu.SemaphoreType.DMA((2 * (1 + ns * (nz - 1)),)),
        ],
        smem=1,
        loose=range(5, 7 + 2 * ns),
    )(
        contig_lengths,
        vectors,
        tokens,
        left,
        right,
        conv_own,
        conv_other,
        *conv_pieces,
        *conv_other_pieces,
    )

    late = lax.optimization_barrier((pre, tokens, *ffn_pieces))
    ffn_pieces = late[2:]
    token_pieces = [tokens] + [exchange(late[1], "seq", k) for k in range(1, ns)]
    ffn_other_pieces = [exchange(p, "row", 1) for p in ffn_pieces]

    layer_out, low, hidden, outer_grad, inner_grad, inner_full, vec_sums = vmem_call(
        functools.partial(ffn_kernel, nz, ns),
        [
            ((count, width), BF),
            ((count, width), BF),
            ((count, hid), BF),
            ((count, width), BF),
            ((count, hid), BF),
            ((nz, 2, in_rows, hid), BF),
            ((VEC_PAD, width), F32),
        ],
        [
            pltpu.VMEM((nz, 2, ns, part, width), BF),
            pltpu.VMEM((count, hid), F32),
            pltpu.VMEM((count, width), F32),
            pltpu.SemaphoreType.DMA((4 * ns * nz,)),
        ],
        kept=(0,),
        loose=range(3, 5 + 2 * ns),
    )(after, cot, vectors, ffn_own, ffn_other, *ffn_pieces, *ffn_other_pieces)

    mine, theirs = vmem_call(
        functools.partial(ffn_weight_kernel, nz, ns, in_rows, out_rows),
        [((ns, nz, ffn_rows, width), BF)] * 2,
        [pltpu.VMEM((hid, width), BF), pltpu.VMEM((width, hid), BF)],
    )(low, hidden, outer_grad, inner_grad)

    late = lax.optimization_barrier((inner_grad, mine, *token_pieces))
    inner_grad, mine, token_pieces = late[0], late[1], late[2:]
    results = vmem_call(
        functools.partial(back_kernel, ns),
        [((count, width), F32), ((count, width), BF)]
        + [((count + 2 * vec_rows, span), BF)] * ns,
        [pltpu.VMEM((count, width), F32), pltpu.VMEM((VEC_PAD, width), F32)],
    )(pre, cot, vectors, inner_grad, inner_full, vec_sums)
    after_grad, conv_grad = results[:2]
    grad_pieces = list(results[2:])
    theirs, conv_grad = lax.optimization_barrier((theirs, conv_grad))
    arrived = exchange(theirs, "row", 1)
    grad_pieces = grad_pieces[:1] + [exchange(grad_pieces[k], "seq", k) for k in range(1, ns)]
    grad_rows = conv_grad.reshape(rows, length, width)
    grad_left = shift_along(grad_rows[:, length - half :], "seq", 1)
    grad_right = shift_along(grad_rows[:, :half], "seq", -1)
    grad_pieces[0], grad_left, grad_right = lax.optimization_barrier(
        (grad_pieces[0], grad_left, grad_right)
    )

    mine, grad_pieces[1] = lax.optimization_barrier((mine, grad_pieces[1]))
    flat = (ns * nz * ffn_rows, width)
    ffn_sums = split_sum([mine.reshape(flat), arrived.reshape(flat)], ns)
    ffn_sums = [ffn_sums[0]] + [exchange(ffn_sums[k], "seq", k) for k in range(1, ns)]

    mine, theirs = vmem_call(
        functools.partial(conv_weight_kernel, taps, nz, ns, in_rows),
        [((nz * conv_rows + 2 * vec_rows, span), BF)] * 2,
        [
            pltpu.VMEM((ns * length + 2 * half, span), F32),
            pltpu.VMEM((ns * length + 2 * half, LANES), jnp.int32),
            pltpu.VMEM((ns * count, taps * span), BF),
            pltpu.VMEM((width, taps * span), F32),
            pltpu.VMEM((ns, rows, length, width), BF),
            pltpu.SemaphoreType.DMA((ns,)),
        ],
        smem=1,
        loose=range(1, 1 + ns),
    )(contig_lengths, *token_pieces, *grad_pieces)
    arrived = exchange(theirs, "row", 1)
    sums = vmem_call(
        functools.partial(conv_core_kernel, conv_rows),
        [((conv_rows + 2 * vec_rows, span), BF)] * nz,
        slack=2,
    )(mine, arrived)
    sums = [sums[0]] + [exchange(sums[j], "row", 2 * j) for j in range(1, nz)]

    (input_grad,) = vmem_call(
        functools.partial(input_grad_kernel, taps, ns),
        [((count, width), F32)],
        [
            pltpu.VMEM((length + 2 * half, width), F32),
            pltpu.VMEM((length + 2 * half, LANES), jnp.int32),
            pltpu.VMEM((taps, count, width), BF),
        ],
        smem=1,
        kept=(0,),
    )(contig_lengths, conv_grad, grad_left, grad_right, after_grad, conv_full)
    sums[0], input_grad = lax.optimization_barrier((sums[0], input_grad))

    conv_sum, conv_square, vec_sum = vmem_call(
        functools.partial(conv_final_kernel, nz, vec_rows),
        [((conv_rows, span), BF), ((8, LANES), F32), ((VEC_PAD, width), F32)],
        slack=2,
    )(*sums)
    conv_sums = [conv_sum] + [exchange(conv_sum, "seq", k) for k in range(1, ns)]

    ffn_sums = split_sum(ffn_sums, nz)
    ffn_sums = [ffn_sums[0]] + [exchange(ffn_sums[j], "row", 2 * j) for j in range(1, nz)]
    ffn_sums[0], conv_sums[-1] = lax.optimization_barrier((ffn_sums[0], conv_sums[-1]))
    (ffn_sum,) = vmem_call(
        functools.partial(ffn_final_kernel, nz), [((ffn_rows + VEC_PAD, width), BF)], slack=2
    )(*ffn_sums, conv_square)
    ffn_sums = [ffn_sum] + [exchange(ffn_sum, "seq", k) for k in range(1, ns)]
    (square,) = vmem_call(
        functools.partial(square_kernel, ns), [((8, LANES), F32)], slack=2
    )(*ffn_sums)
    squares = [square] + [exchange(square, "row", 2 * j) for j in range(1, nz)]
    (square,) = vmem_call(small_sum_kernel, [((8, LANES), F32)], slack=2)(*squares)
    squares = [square, exchange(square, "row", 1)]

    second_width = taps * width + hid + (out_rows // in_rows) * width + vectors.shape[0]
    results = [
        (conv_weight.shape, F32),
        (conv_weight.shape, F32),
        (inner_weight.shape, F32),
        (inner_weight.shape, F32),
        (outer_weight.shape, F32),
        (outer_weight.shape, F32),
        ((in_rows, second_width), F32),
    ]
    (
        norm,
        new_vectors,
        vector_first,
        new_conv,
        conv_first,
        new_inner,
        inner_first,
        new_outer,
        outer_first,
        second_moments,
    ) = vmem_call(
        functools.partial(adam_kernel, taps, ns),
        [((1, 1), F32), (vectors.shape, F32), (vectors.shape, F32), *results],
        [pltpu.VMEM(shape, dtype) for shape, dtype in results]
        + [
            pltpu.VMEM((width // LANES, out_rows, LANES), F32),
            pltpu.VMEM((width, LANES), F32),
            pltpu.SemaphoreType.DMA((8,)),
        ],
        kept=range(3),
        left=range(3, 10),
        slack=3,
    )(
        *conv_sums,
        *ffn_sums,
        vec_sum,
        *squares,
        conv_weight,
        inner_weight,
        outer_weight,
        vectors,
        conv_moments,
        inner_moments,
        outer_moments,
        vector_near,
    )
    return (
        layer_out.reshape(tokens.shape),
        input_grad.reshape(tokens.shape),
        norm.reshape(()),
        new_conv,
        conv_first,
        new_inner,
        inner_first,
        new_outer,
        outer_first,
        new_vectors,
        vector_first,
        second_moments,
    )


def solution(mesh):
    in_specs = (
        P("row", "seq", None),
        P("row", "seq", None),
        P("row", None),
        P(None, "row", None),
        P("row", None),
        P("row", None),
        P(),
        P(None, None, "row", None),
        P(None, "row", None),
        P(None, "row", None),
        P(),
    )
    out_specs = (
        P("row", "seq", None),
        P("row", "seq", None),
        P(),
        P(None, "row", None),
        P(None, "row", None),
        P("row", None),
        P("row", None),
        P("row", None),
        P("row", None),
        P(),
        P(),
        P("row", None),
    )
    return jax.shard_map(
        per_device, mesh=mesh, in_specs=in_specs, out_specs=out_specs, check_vma=False
    )
```

```python
import functools

import jax
import jax.numpy as jnp
from jax import lax
from jax.experimental import pallas as pl
from jax.experimental.pallas import tpu as pltpu
from jax.sharding import PartitionSpec as P

DILATION_STEP = 8

beta_one = 0.9
beta_two = 0.999
adam_eps = 1e-08
weight_decay = 0.1
matrix_rate = 0.03
vector_rate = 0.3
clip_level = 1.0
step_count = 10
norm_eps = 1e-05

F32 = jnp.float32
BF = jnp.bfloat16
VEC_PAD = 16
LANES = 128
SQRT_HALF = 0.7071067811865476
PDF_SCALE = 0.3989422804014327


def exchange(value, axis, mask):
    size = lax.axis_size(axis)
    return lax.ppermute(value, axis, [(i, i ^ mask) for i in range(size)])


def shift_along(value, axis, step):
    size = lax.axis_size(axis)
    pairs = [(i, i + step) for i in range(size) if 0 <= i + step < size]
    return lax.ppermute(value, axis, pairs)


def gelu_parts(v):
    cdf = 0.5 + 0.5 * lax.erf(v * SQRT_HALF)
    return v * cdf, cdf


def gelu_slope(v, cdf):
    return cdf + v * (jnp.exp(-0.5 * v * v) * PDF_SCALE)


def mean_of(v):
    return jnp.mean(v, axis=-1, keepdims=True)


def normalized(v):
    centred = v - mean_of(v)
    scale = lax.rsqrt(mean_of(centred * centred) + norm_eps)
    return centred * scale, scale


def fold_rows(v):
    rows, cols = v.shape
    return jnp.sum(v.reshape(rows // 8, 8, cols), axis=0)


def column_sum(acc):
    return jnp.sum(acc, axis=0, keepdims=True)


def loop_rows(total, step, body, init=0):
    return lax.fori_loop(
        0, total // step, lambda i, carry: body(pl.multiple_of(i * step, step), carry), init
    )


def dot(a, b):
    return jnp.dot(a, b, preferred_element_type=F32)


def dot_nt(a, b):
    return lax.dot_general(a, b, (((1,), (1,)), ((), ())), preferred_element_type=F32)


def dot_tn(a, b):
    return lax.dot_general(a, b, (((0,), (0,)), ((), ())), preferred_element_type=F32)


def place():
    seq_at = lax.axis_index("seq")
    row_at = lax.axis_index("row")
    return seq_at, row_at // 2, row_at % 2


def at(index, step):
    return pl.ds(pl.multiple_of(index * step, step), step)


def size_of(shape, dtype):
    total = jnp.dtype(dtype).itemsize
    for n in shape:
        total *= n
    return total


def vmem_call(kernel, outs, scratch=(), smem=0, loose=(), far=(), kept=(), left=(), slack=6):
    space = pl.BlockSpec(memory_space=pltpu.VMEM)
    anywhere = pl.BlockSpec(memory_space=pl.ANY)
    grant = slack * 1024 * 1024
    grant += sum(size_of(v.shape, v.dtype) for v in scratch if hasattr(v, "shape") and v.dtype in (F32, BF, jnp.int32))
    grant += sum(size_of(*outs[i]) for i in kept)

    def call(*args):
        fixed = [
            a
            if i < smem or i in loose
            else pltpu.with_memory_space_constraint(a, pltpu.HBM if i in far else pltpu.VMEM)
            for i, a in enumerate(args)
        ]
        return pl.pallas_call(
            kernel,
            out_shape=[
                jax.ShapeDtypeStruct(shape, dtype) if i in kept or i in left else pltpu.VMEM(shape, dtype)
                for i, (shape, dtype) in enumerate(outs)
            ],
            in_specs=[
                pl.BlockSpec(memory_space=pltpu.SMEM)
                if i < smem
                else pl.BlockSpec(memory_space=pltpu.HBM)
                if i in far
                else anywhere
                if i in loose
                else space
                for i in range(len(args))
            ],
            out_specs=[anywhere if i in left else space for i in range(len(outs))],
            scratch_shapes=list(scratch),
            cost_estimate=pl.CostEstimate(flops=1, bytes_accessed=1, transcendentals=0),
            compiler_params=pltpu.CompilerParams(vmem_limit_bytes=grant),
        )(*fixed)

    return call


def begin_copies(pairs, sems):
    copies = [pltpu.make_async_copy(src, dst, sems.at[i]) for i, (src, dst) in enumerate(pairs)]
    for copy in copies:
        copy.start()
    return copies


def end_copies(copies):
    for copy in copies:
        copy.wait()


def contigs(lens_ref, row, positions, row_length):
    found = jnp.zeros(positions.shape, jnp.int32)
    start = jnp.int32(0)
    for j in range(lens_ref.shape[1] - 1):
        start = start + lens_ref[row, j]
        found = found + (positions >= start).astype(jnp.int32)
    found = jnp.where(positions < 0, -1, found)
    return jnp.where(positions >= row_length, lens_ref.shape[1], found)


def masked_taps(src, cid, length, taps, half, store):
    centre = cid[pl.ds(half, length), :]

    def body(tap, carry):
        begin = pl.multiple_of(tap * DILATION_STEP, DILATION_STEP)
        keep = cid[pl.ds(begin, length), :] == centre
        for a in range(src.shape[1] // LANES):
            part = src[pl.ds(begin, length), a * LANES : (a + 1) * LANES]
            store(tap, a, jnp.where(keep, part, 0.0).astype(BF))
        return carry

    lax.fori_loop(0, taps, body, 0)


def round_kernel(ns, conv_far, inner_far, outer_far, tok_far, *refs):
    conv_part, left_edge, right_edge, conv_own, ffn_own, ffn_part = refs[:6]
    conv, inner, outer, sems = refs[6:]
    half = left_edge.shape[1]
    copies = begin_copies(
        [
            (conv_far, conv),
            (inner_far, inner),
            (outer_far, outer),
            (tok_far.at[:, :half], left_edge),
            (tok_far.at[:, tok_far.shape[1] - half :], right_edge),
        ],
        sems,
    )
    seq_at = lax.axis_index("seq")
    in_rows, hid = inner.shape
    quarter = hid // ns
    part = outer.shape[0] // ns
    span = conv.shape[2] // ns
    copies[0].wait()
    for t in range(conv.shape[0]):
        conv_own[t] = conv[t].astype(BF)
        conv_part[t] = conv[t, :, at(seq_at, span)].astype(BF)
    end_copies(copies[1:])
    for k in range(ns):
        ffn_own[k * in_rows : (k + 1) * in_rows, :] = inner[
            :, k * quarter : (k + 1) * quarter
        ].astype(BF)
    ffn_own[ns * in_rows :, :] = outer[...].astype(BF)
    ffn_part[:in_rows, :] = inner[:, at(seq_at, quarter)].astype(BF)
    ffn_part[in_rows:, :] = outer[at(seq_at, part), :].astype(BF)


def stack_kernel(count, *refs):
    ins, rest = refs[:count], refs[count:]
    out = rest[len(rest) // 2]
    for i, ref in enumerate(ins):
        out[i] = ref[...]
    if len(rest) > 1:
        rest[2][...] = rest[0][...]


def conv_kernel(taps, nz, ns, lens, vec, tok, left, right, own, other, *rest):
    pieces = (rest[:ns], rest[ns : 2 * ns])
    pre, after, full, ext, cid, cat, sems = rest[2 * ns :]
    seq_at, z_at, core_at = place()
    rows, length, width = tok.shape
    quarter = width // ns
    half = DILATION_STEP * (taps // 2)
    pairs = []
    for i, whole in enumerate((own, other)):
        core = core_at ^ i
        pairs.append((whole, full.at[:, z_at, core]))
        for k in range(ns):
            for j in range(1, nz):
                cols = at(seq_at ^ k, quarter)
                pairs.append((pieces[i][k].at[j - 1], full.at[:, z_at ^ j, core, :, cols]))
    copies = begin_copies(pairs, sems)
    span = length + 2 * half
    base = seq_at * length - half
    positions = base + lax.broadcasted_iota(jnp.int32, (span, LANES), 0)
    for r in range(rows):
        ext[0:half, :] = left[r].astype(F32)
        ext[half : half + length, :] = tok[r].astype(F32)
        ext[half + length :, :] = right[r].astype(F32)
        cid[...] = contigs(lens, r, positions, length * ns)

        def store(tap, a, value, r=r):
            cat[r * length : (r + 1) * length, at(tap * (width // LANES) + a, LANES)] = value

        masked_taps(ext, cid, length, taps, half, store)
    end_copies(copies)
    weights = full.reshape(taps * width, width)

    def product(r, carry):
        where = at(r, length)
        pre[where, :] = dot(cat[where, :], weights[...]) + vec[0:1, :]
        return carry

    lax.fori_loop(0, rows, product, 0)

    for r in range(rows):

        def norm(begin, carry, r=r):
            where = pl.ds(r * length + begin, 32)
            active, _ = gelu_parts(pre[where, :])
            unit, _ = normalized(active)
            after[where, :] = (
                tok[r, pl.ds(begin, 32), :].astype(F32) + unit * vec[1:2, :] + vec[2:3, :]
            )
            return carry

        loop_rows(length, 32, norm)


def ffn_kernel(nz, ns, *refs):
    after, cot, vec = refs[:3]
    wholes = refs[3:5]
    pieces = (refs[5 : 5 + ns], refs[5 + ns : 5 + 2 * ns])
    rest = refs[5 + 2 * ns :]
    layer, low, hidden, outer_grad, inner_grad, inner_full, sums, outer_full, slope, tmp, sems = rest
    seq_at, z_at, core_at = place()
    count, width = after.shape
    hid = inner_full.shape[3]
    in_rows = inner_full.shape[2]
    quarter = hid // ns
    blocks = hid // width
    inner = inner_full.reshape(width, hid)
    outer = outer_full.reshape(hid, width)
    part = outer_full.shape[3]
    pairs = []
    for i, whole in enumerate(wholes):
        core = core_at ^ i
        for q in range(ns):
            pairs.append(
                (
                    whole.at[q * in_rows : (q + 1) * in_rows],
                    inner_full.at[z_at, core, :, q * quarter : (q + 1) * quarter],
                )
            )
            pairs.append(
                (
                    whole.at[ns * in_rows + q * part : ns * in_rows + (q + 1) * part],
                    outer_full.at[z_at, core, q],
                )
            )
        for k in range(ns):
            piece = pieces[i][k]
            q = seq_at ^ k
            for j in range(1, nz):
                z = z_at ^ j
                pairs.append((piece.at[j - 1, :in_rows], inner_full.at[z, core, :, at(q, quarter)]))
                pairs.append((piece.at[j - 1, in_rows:], outer_full.at[z, core, q]))
    copies = begin_copies(pairs, sems)

    def lower(begin, carry):
        where = pl.ds(begin, 64)
        low[where, :] = after[where, :].astype(BF)
        return carry

    loop_rows(count, 64, lower)
    end_copies(copies)

    def up(b, carry):
        cols = at(b, width)
        tmp[...] = dot(low[...], inner[:, cols]) + vec[pl.ds(6 + b, 1), :]

        def act(begin, inside):
            where = pl.ds(begin, 32)
            v = tmp[where, :]
            active, cdf = gelu_parts(v)
            hidden[where, cols] = active.astype(BF)
            slope[where, cols] = gelu_slope(v, cdf)
            return inside

        loop_rows(count, 32, act)
        return carry

    lax.fori_loop(0, blocks, up, 0)
    tmp[...] = dot(hidden[...], outer[...]) + vec[3:4, :]
    zero = jnp.zeros((8, width), F32)

    def second(begin, carry):
        bias_sum, gain_sum, shift_sum = carry
        where = pl.ds(begin, 32)
        unit, scale = normalized(tmp[where, :])
        gain = vec[4:5, :]
        layer[where, :] = (after[where, :] + unit * gain + vec[5:6, :]).astype(BF)
        dy = cot[where, :].astype(F32)
        u = dy * gain
        grad = (scale * (u - mean_of(u) - unit * mean_of(u * unit))).astype(BF)
        outer_grad[where, :] = grad
        return (
            bias_sum + fold_rows(grad.astype(F32)),
            gain_sum + fold_rows(dy * unit),
            shift_sum + fold_rows(dy),
        )

    totals = loop_rows(count, 32, second, (zero, zero, zero))
    sums[...] = jnp.zeros(sums.shape, F32)
    for i, total in enumerate(totals):
        sums[3 + i : 4 + i, :] = column_sum(total)

    def down(b, carry):
        cols = at(b, width)
        tmp[...] = dot_nt(outer_grad[...], outer[cols, :])

        def act(begin, total):
            where = pl.ds(begin, 32)
            grad = (tmp[where, :] * slope[where, cols]).astype(BF)
            inner_grad[where, cols] = grad
            return total + fold_rows(grad.astype(F32))

        total = loop_rows(count, 32, act, zero)
        sums[pl.ds(6 + b, 1), :] = column_sum(total)
        return carry

    lax.fori_loop(0, blocks, down, 0)


def back_kernel(ns, rows, *refs):
    pre, cot, vec, inner_grad, inner_full, partial_sums, after_grad, conv_grad = refs[:8]
    inner = inner_full.reshape(pre.shape[1], inner_grad.shape[1])
    sends = refs[8 : 8 + ns]
    tmp, sums = refs[8 + ns :]
    seq_at = lax.axis_index("seq")
    count, width = pre.shape
    zero = jnp.zeros((8, width), F32)
    sums[...] = partial_sums[...]
    tmp[...] = dot_nt(inner_grad[...], inner[...])

    def first(begin, carry):
        bias_sum, gain_sum, shift_sum = carry
        where = pl.ds(begin, 32)
        upstream = cot[where, :].astype(F32) + tmp[where, :]
        after_grad[where, :] = upstream
        v = pre[where, :]
        active, cdf = gelu_parts(v)
        unit, scale = normalized(active)
        u = upstream * vec[1:2, :]
        grad = scale * (u - mean_of(u) - unit * mean_of(u * unit))
        grad = (grad * gelu_slope(v, cdf)).astype(BF)
        conv_grad[where, :] = grad
        return (
            bias_sum + fold_rows(grad.astype(F32)),
            gain_sum + fold_rows(upstream * unit),
            shift_sum + fold_rows(upstream),
        )

    totals = loop_rows(count, 32, first, (zero, zero, zero))
    for i, total in enumerate(totals):
        sums[i : i + 1, :] = column_sum(total)
    span = width // ns
    for k in range(ns):
        sends[k][0:count, :] = conv_grad[:, at(seq_at ^ k, span)]
        encode(sends[k], count, spread(sums[...]))
        begin = count + 2 * VEC_PAD * width // LANES
        if sends[k].shape[0] > begin:
            half = (sends[k].shape[0] - begin) // rows // (width // LANES)
            length = count // rows
            first = jnp.where((seq_at ^ k) > seq_at, length - half, 0)
            for r in range(rows):
                for a in range(width // LANES):
                    sends[k][begin : begin + half, :] = conv_grad[
                        at(r * (length // half) + first // half, half), a * LANES : (a + 1) * LANES
                    ]
                    begin += half


def spread(v):
    return jnp.concatenate(
        [v[:, a * LANES : (a + 1) * LANES] for a in range(v.shape[1] // LANES)], axis=0
    )


def gathered(v):
    return jnp.concatenate(
        [v[a * VEC_PAD : (a + 1) * VEC_PAD, :] for a in range(v.shape[0] // VEC_PAD)], axis=1
    )


def encode(ref, begin, v):
    rows = v.shape[0]
    high = v.astype(BF)
    ref[begin : begin + rows, :] = high
    ref[begin + rows : begin + 2 * rows, :] = (v - high.astype(F32)).astype(BF)


def decode(ref, begin, rows):
    high = ref[begin : begin + rows, :].astype(F32)
    return high + ref[begin + rows : begin + 2 * rows, :].astype(F32)


def tree_sum(values):
    values = list(values)
    while len(values) > 1:
        values = [values[i] + values[i + 1] for i in range(0, len(values), 2)]
    return values[0]


def ffn_weight_kernel(nz, ns, in_rows, out_rows, *refs):
    low, hidden, outer_grad, inner_grad, mine, theirs, outer_sum, inner_sum = refs
    seq_at, z_at, core_at = place()
    width = low.shape[1]
    hid = hidden.shape[1]
    part = out_rows // ns
    quarter = hid // ns

    def product(b, carry):
        cols = at(b, width)
        outer_sum[cols, :] = dot_tn(hidden[:, cols], outer_grad[...]).astype(BF)
        inner_sum[:, cols] = dot_tn(low[...], inner_grad[:, cols]).astype(BF)
        return carry

    lax.fori_loop(0, hid // width, product, 0)
    for i, out in enumerate((mine, theirs)):
        for k in range(ns):
            for j in range(nz):
                block = (z_at ^ j) * 2 + (core_at ^ i)
                out[k, j, :in_rows] = inner_sum[at(block, in_rows), at(seq_at ^ k, quarter)]
                out[k, j, in_rows:] = outer_sum[at(block * ns + (seq_at ^ k), part), :]


def conv_weight_kernel(taps, nz, ns, in_rows, *refs):
    lens = refs[0]
    far = refs[1 : 1 + ns]
    grads = refs[1 + ns : 1 + 2 * ns]
    mine, theirs, padded, cid, cat, total, toks, sems = refs[1 + 2 * ns :]
    copies = begin_copies([(far[k], toks.at[k]) for k in range(ns)], sems)
    seq_at, z_at, core_at = place()
    _, rows, length, width = toks.shape
    span = width // ns
    half = DILATION_STEP * (taps // 2)
    row_length = ns * length
    count = rows * length
    positions = lax.broadcasted_iota(jnp.int32, (row_length + 2 * half, LANES), 0) - half
    edge = jnp.zeros((half, span), F32)
    for r in range(rows):
        padded[0:half, :] = edge
        padded[half + row_length :, :] = edge
        cid[...] = contigs(lens, r, positions, row_length)
        for k in range(ns):
            padded[pl.ds(half + (seq_at ^ k) * length, length), :] = grads[k][
                r * length : (r + 1) * length, :
            ].astype(F32)
        for k in range(ns):
            base = (seq_at ^ k) * length
            centre = cid[pl.ds(pl.multiple_of(base + half, 8), length), :]
            for t in range(taps):
                begin = pl.multiple_of(base + DILATION_STEP * (taps - 1 - t), 8)
                keep = cid[pl.ds(begin, length), :] == centre
                value = jnp.where(keep, padded[pl.ds(begin, length), :], 0.0)
                low_row = k * count + r * length
                cat[low_row : low_row + length, t * span : (t + 1) * span] = value.astype(BF)
    end_copies(copies)
    for k in range(ns):
        value = tree_sum(
            [
                dot_tn(toks[k, r], cat[k * count + r * length : k * count + (r + 1) * length, :])
                for r in range(rows)
            ]
        )
        if k == 0:
            total[...] = value
        else:
            total[...] += value
    for i, out in enumerate((mine, theirs)):
        for j in range(nz):
            block = (z_at ^ j) * 2 + (core_at ^ i)
            for t in range(taps):
                begin = (j * taps + t) * in_rows
                out[begin : begin + in_rows, :] = total[
                    at(block, in_rows), t * span : (t + 1) * span
                ].astype(BF)
    vec_rows = VEC_PAD * width // LANES
    summed = tree_sum([decode(g, count, vec_rows) for g in grads])
    for out in (mine, theirs):
        encode(out, nz * taps * in_rows, summed)


def input_grad_kernel(taps, ns, rows, masks, *refs):
    lens, grad, after_grad, full_blocks = refs[:4]
    pieces = refs[4 : 4 + len(masks)]
    out, ext, cid, cat = refs[4 + len(masks) :]
    full = full_blocks.reshape(taps, grad.shape[1], grad.shape[1])
    seq_at = lax.axis_index("seq")
    half = DILATION_STEP * (taps // 2)
    width = grad.shape[1]
    length = grad.shape[0] // rows
    base = seq_at * length - half
    positions = base + lax.broadcasted_iota(jnp.int32, (length + 2 * half, LANES), 0)
    ext[0:half, :] = jnp.zeros((half, width), F32)
    ext[half + length :, :] = jnp.zeros((half, width), F32)
    for r in range(rows):
        ext[half : half + length, :] = grad[r * length : (r + 1) * length, :].astype(F32)
        for mask, piece in zip(masks, pieces):
            for step, begin in ((-1, 0), (1, half + length)):

                @pl.when((seq_at ^ mask) == seq_at + step)
                def _(r=r, piece=piece, begin=begin):
                    first = piece.shape[0] - rows * half * (width // LANES)
                    for a in range(width // LANES):
                        low = first + (r * (width // LANES) + a) * half
                        ext[begin : begin + half, a * LANES : (a + 1) * LANES] = piece[
                            low : low + half, :
                        ].astype(F32)

        cid[...] = contigs(lens, r, positions, length * ns)

        def store(tap, a, value, r=r):
            flipped = taps - 1 - tap
            cat[
                flipped, r * length : (r + 1) * length, a * LANES : (a + 1) * LANES
            ] = value

        masked_taps(ext, cid, length, taps, half, store)

    out[...] = after_grad[...]

    def product(t, carry):
        out[...] += dot_nt(cat[t], full[t])
        return carry

    lax.fori_loop(0, taps, product, 0)


def split_sum_kernel(count, *refs):
    ins, outs = refs[:count], refs[count:]
    rows = outs[0].shape[0]
    for p, out in enumerate(outs):

        def body(begin, carry, p=p, out=out):
            where = pl.ds(p * rows + begin, 64)
            out[pl.ds(begin, 64), :] = tree_sum([v[where, :].astype(F32) for v in ins]).astype(BF)
            return carry

        loop_rows(rows, 64, body)


def split_sum(ins, parts):
    rows, cols = ins[0].shape
    return vmem_call(
        functools.partial(split_sum_kernel, len(ins)),
        [((rows // parts, cols), BF)] * parts,
        slack=2,
    )(*ins)


def conv_core_kernel(rows, mine, got, *outs):
    vec_rows = (mine.shape[0] - rows * len(outs)) // 2
    begin_vec = rows * len(outs)
    summed = decode(mine, begin_vec, vec_rows) + decode(got, begin_vec, vec_rows)
    for p, out in enumerate(outs):

        def body(begin, carry, p=p, out=out):
            where = pl.ds(p * rows + begin, 64)
            out[pl.ds(begin, 64), :] = (mine[where, :].astype(F32) + got[where, :].astype(F32)).astype(
                BF
            )
            return carry

        loop_rows(rows, 64, body)
        encode(out, rows, summed)


def conv_final_kernel(count, vec_rows, *refs):
    ins, (out, square, vec_sum) = refs[:count], refs[count:]
    square[...] = summed_square(ins, out)
    vec_sum[...] = gathered(tree_sum([decode(v, out.shape[0], vec_rows) for v in ins]))


def summed_square(ins, out):
    def body(begin, carry):
        where = pl.ds(begin, 64)
        value = tree_sum([v[where, :].astype(F32) for v in ins]).astype(BF)
        out[where, :] = value
        wide = value.astype(F32)
        return carry + lane_fold(fold_rows(wide * wide))

    rows = ins[0].shape[0] // 64 * 64 if out.shape[0] % 64 else out.shape[0]
    return loop_rows(min(rows, out.shape[0]), 64, body, jnp.zeros((8, LANES), F32))


def lane_fold(v):
    return sum(v[:, a * LANES : (a + 1) * LANES] for a in range(v.shape[1] // LANES))


def ffn_final_kernel(count, *refs):
    ins, (conv_square, out) = refs[:count], refs[count:]
    rows = ins[0].shape[0]
    square = summed_square(ins, out.at[0:rows]) + conv_square[...]
    high = square.astype(BF)
    low = (square - high.astype(F32)).astype(BF)
    zero = jnp.zeros(high.shape, BF)
    tail = jnp.concatenate([high, low] + [zero] * (out.shape[1] // LANES - 2), axis=1)
    out[rows : rows + VEC_PAD, :] = jnp.concatenate([tail, jnp.zeros(tail.shape, BF)], axis=0)


def square_kernel(count, *refs):
    ins, out = refs[:count], refs[count]
    rows = ins[0].shape[0] - VEC_PAD
    parts = []
    for v in ins:
        tail = v[rows : rows + VEC_PAD, :].astype(F32)
        parts.append(tail[:8, :LANES] + tail[:8, LANES : 2 * LANES])
    out[...] = tree_sum(parts)


def small_sum_kernel(*refs):
    refs[-1][...] = tree_sum([v[...] for v in refs[:-1]])


def adam_math(weight, first, second, gradient, clip, rate, decay):
    clipped = gradient * clip
    first = beta_one * first + (1.0 - beta_one) * clipped
    second = beta_two * second + (1.0 - beta_two) * clipped * clipped
    first_hat = first / (1.0 - beta_one**step_count)
    second_hat = second / (1.0 - beta_two**step_count)
    weight = weight - rate * (first_hat / (jnp.sqrt(second_hat) + adam_eps) + decay * weight)
    return weight, first, second


def adam_kernel(taps, ns, *refs):
    conv_grads = refs[:ns]
    ffn_grads = refs[ns : 2 * ns]
    vec_sum, one, two, conv, inner, outer, vec, conv_m, inner_m, outer_m, vec_m = refs[
        2 * ns : 2 * ns + 11
    ]
    norm, new_vec, vec_first = refs[2 * ns + 11 : 2 * ns + 14]
    outs = refs[2 * ns + 14 : 2 * ns + 21]
    new_conv, conv_first, new_inner, inner_first, new_outer, outer_first, second = refs[
        2 * ns + 21 : 2 * ns + 28
    ]
    outer_second, vec_second, sems = refs[2 * ns + 28 :]
    seq_at, z_at, core_at = place()
    in_rows, width = conv.shape[1:]
    hid = inner.shape[1]
    out_rows = outer.shape[0]
    span = width // ns
    quarter = hid // ns
    part = out_rows // ns
    vec_count = vec.shape[0]
    vec_grad = vec_sum[0:vec_count, :]
    total = jnp.sum(one[...] + two[...]) + jnp.sum(vec_grad * vec_grad)
    value = jnp.sqrt(jnp.full((1, 1), total, F32))
    norm[...] = value
    clip = clip_level / jnp.maximum(value, clip_level)
    going = []

    def send(index, src, dst):
        copy = pltpu.make_async_copy(src, dst, sems.at[index])
        copy.start()
        going.append(copy)

    def conv_step(t, carry):
        for k in range(ns):
            cols = at(seq_at ^ k, span)
            w, m, v = adam_math(
                conv[t, :, cols],
                conv_m[0, t, :, cols],
                conv_m[1, t, :, cols],
                conv_grads[k][at(t, in_rows), :].astype(F32),
                clip,
                matrix_rate,
                weight_decay,
            )
            new_conv[t, :, cols] = w
            conv_first[t, :, cols] = m
            second[:, at(t * ns + (seq_at ^ k), span)] = v
        return carry

    lax.fori_loop(0, taps, conv_step, 0)
    send(0, new_conv, outs[0])
    send(1, conv_first, outs[1])
    send(2, second.at[:, : taps * width], outs[6].at[:, : taps * width])
    chunks = quarter // LANES

    for k in range(ns):

        def inner_step(a, carry, k=k):
            lanes = at((seq_at ^ k) * chunks + a, LANES)
            w, m, v = adam_math(
                inner[:, lanes],
                inner_m[0, :, lanes],
                inner_m[1, :, lanes],
                ffn_grads[k][0:in_rows, at(a, LANES)].astype(F32),
                clip,
                matrix_rate,
                weight_decay,
            )
            new_inner[:, lanes] = w
            inner_first[:, lanes] = m
            second[:, at(taps * width // LANES + (seq_at ^ k) * chunks + a, LANES)] = v
            return carry

        lax.fori_loop(0, chunks, inner_step, 0)
    send(3, new_inner, outs[2])
    send(4, inner_first, outs[3])
    for k in range(ns):
        where = at(seq_at ^ k, part)

        def outer_step(a, carry, k=k, where=where):
            lanes = at(a, LANES)
            w, m, v = adam_math(
                outer[where, lanes],
                outer_m[0, where, lanes],
                outer_m[1, where, lanes],
                ffn_grads[k][in_rows : in_rows + part, lanes].astype(F32),
                clip,
                matrix_rate,
                weight_decay,
            )
            new_outer[where, lanes] = w
            outer_first[where, lanes] = m
            outer_second[a, where, :] = v
            return carry

        lax.fori_loop(0, width // LANES, outer_step, 0)
    send(5, new_outer, outs[4])
    send(6, outer_first, outs[5])
    ratio = out_rows // in_rows
    base = taps * width + hid
    for e in range(ratio):
        for a in range(width // LANES):
            begin = base + e * width + a * LANES
            second[:, begin : begin + LANES] = outer_second[a, pl.ds(e, in_rows, stride=ratio), :]
    w, m, v = adam_math(vec[...], vec_m[0], vec_m[1], vec_grad, clip, vector_rate, 0.0)
    new_vec[...] = w
    vec_first[...] = m
    v = jnp.concatenate([v, jnp.zeros((LANES - vec_count, width), F32)], axis=0)
    vec_second[...] = jnp.transpose(v)
    begin = base + ratio * width
    block = z_at * 2 + core_at
    second[:, begin : begin + vec_count] = vec_second[at(block, in_rows), :][:, 0:vec_count]
    send(7, second.at[:, taps * width :], outs[6].at[:, taps * width :])
    end_copies(going)


def per_device(
    tokens,
    cotangent,
    contig_lengths,
    conv_weight,
    inner_weight,
    outer_weight,
    vectors,
    conv_moments,
    inner_moments,
    outer_moments,
    vector_moments,
):
    ns = lax.axis_size("seq")
    nr = lax.axis_size("row")
    nz = nr // 2
    seq_at = lax.axis_index("seq")
    rows, length, width = tokens.shape
    taps, in_rows, _ = conv_weight.shape
    hid = inner_weight.shape[1]
    out_rows = outer_weight.shape[0]
    count = rows * length
    half = DILATION_STEP * (taps // 2)
    span = width // ns
    quarter = hid // ns
    part = out_rows // ns

    ffn_rows = in_rows + part
    vec_rows = VEC_PAD * width // LANES
    conv_rows = taps * in_rows
    cot = cotangent.reshape(count, width)

    def edge_rows(k):
        near = any(abs((i ^ k) - i) == 1 for i in range(ns))
        return rows * half * (width // LANES) if near else 0

    conv_part, left_edge, right_edge, conv_own, ffn_own, ffn_part = vmem_call(
        functools.partial(round_kernel, ns),
        [
            ((taps, in_rows, span), BF),
            ((rows, half, width), BF),
            ((rows, half, width), BF),
            (conv_weight.shape, BF),
            ((ns * ffn_rows, width), BF),
            ((ffn_rows, width), BF),
        ],
        [
            pltpu.VMEM(conv_weight.shape, F32),
            pltpu.VMEM(inner_weight.shape, F32),
            pltpu.VMEM(outer_weight.shape, F32),
            pltpu.SemaphoreType.DMA((5,)),
        ],
        far=range(4),
        slack=2,
    )(conv_weight, inner_weight, outer_weight, tokens)
    got = [exchange(conv_part, "row", 2 * j) for j in range(1, nz)]
    got[0], conv_own, ffn_own = lax.optimization_barrier((got[0], conv_own, ffn_own))
    left = shift_along(right_edge, "seq", 1)
    right = shift_along(left_edge, "seq", -1)
    conv_other = exchange(conv_own, "row", 1)
    ffn_other = exchange(ffn_own, "row", 1)
    got[0], left, right = lax.optimization_barrier((got[0], left, right))
    (got,) = vmem_call(
        functools.partial(stack_kernel, nz - 1), [((nz - 1, taps, in_rows, span), BF)], slack=2
    )(*got)
    conv_pieces = [got] + [exchange(got, "seq", k) for k in range(1, ns)]
    conv_other_pieces = [exchange(got, "row", 1)]
    ffn_part, conv_other_pieces[0], conv_other, ffn_other = lax.optimization_barrier(
        (ffn_part, conv_other_pieces[0], conv_other, ffn_other)
    )
    ffn_got = [exchange(ffn_part, "row", 2 * j) for j in range(nz - 1, 0, -1)][::-1]
    late = lax.optimization_barrier((*ffn_got, *conv_pieces[1:]))
    ffn_got, conv_pieces[1:] = late[: nz - 1], late[nz - 1 :]
    conv_other_pieces += [exchange(p, "row", 1) for p in conv_pieces[1:]]
    ffn_got, vector_near = vmem_call(
        functools.partial(stack_kernel, nz - 1),
        [((nz - 1, ffn_rows, width), BF), (vector_moments.shape, F32)],
        slack=2,
    )(*ffn_got, vector_moments)
    ffn_pieces = [ffn_got] + [exchange(ffn_got, "seq", k) for k in range(1, ns)]

    pre, after, conv_full = vmem_call(
        functools.partial(conv_kernel, taps, nz, ns),
        [((count, width), F32), ((count, width), F32), ((taps, nz, 2, in_rows, width), BF)],
        [
            pltpu.VMEM((length + 2 * half, width), F32),
            pltpu.VMEM((length + 2 * half, LANES), jnp.int32),
            pltpu.VMEM((count, taps * width), BF),
            pltpu.SemaphoreType.DMA((2 * (1 + ns * (nz - 1)),)),
        ],
        smem=1,
        loose=range(5, 7 + 2 * ns),
    )(
        contig_lengths,
        vectors,
        tokens,
        left,
        right,
        conv_own,
        conv_other,
        *conv_pieces,
        *conv_other_pieces,
    )

    pre, tokens_late = lax.optimization_barrier((pre, tokens))
    token_pieces = [tokens] + [exchange(tokens_late, "seq", k) for k in range(1, ns)]
    late = lax.optimization_barrier((pre, *ffn_pieces))
    pre, ffn_pieces = late[0], late[1:]
    ffn_other_pieces = [exchange(p, "row", 1) for p in ffn_pieces]

    layer_out, low, hidden, outer_grad, inner_grad, inner_full, vec_sums = vmem_call(
        functools.partial(ffn_kernel, nz, ns),
        [
            ((count, width), BF),
            ((count, width), BF),
            ((count, hid), BF),
            ((count, width), BF),
            ((count, hid), BF),
            ((nz, 2, in_rows, hid), BF),
            ((VEC_PAD, width), F32),
        ],
        [
            pltpu.VMEM((nz, 2, ns, part, width), BF),
            pltpu.VMEM((count, hid), F32),
            pltpu.VMEM((count, width), F32),
            pltpu.SemaphoreType.DMA((4 * ns * nz,)),
        ],
        kept=(0,),
        loose=range(3, 5 + 2 * ns),
    )(after, cot, vectors, ffn_own, ffn_other, *ffn_pieces, *ffn_other_pieces)

    mine, theirs = vmem_call(
        functools.partial(ffn_weight_kernel, nz, ns, in_rows, out_rows),
        [((ns, nz, ffn_rows, width), BF)] * 2,
        [pltpu.VMEM((hid, width), BF), pltpu.VMEM((width, hid), BF)],
    )(low, hidden, outer_grad, inner_grad)

    inner_grad, mine = lax.optimization_barrier((inner_grad, mine))
    results = vmem_call(
        functools.partial(back_kernel, ns, rows),
        [((count, width), F32), ((count, width), BF)]
        + [
            ((count + 2 * vec_rows + edge_rows(k), span), BF)
            for k in range(ns)
        ],
        [pltpu.VMEM((count, width), F32), pltpu.VMEM((VEC_PAD, width), F32)],
    )(pre, cot, vectors, inner_grad, inner_full, vec_sums)
    after_grad, conv_grad = results[:2]
    grad_pieces = list(results[2:])
    late = lax.optimization_barrier((theirs, *grad_pieces, *token_pieces))
    theirs, grad_pieces, token_pieces = late[0], list(late[1 : 1 + ns]), late[1 + ns :]
    arrived = exchange(theirs, "row", 1)
    grad_pieces = grad_pieces[:1] + [exchange(grad_pieces[k], "seq", k) for k in range(1, ns)]
    mine, grad_pieces[1] = lax.optimization_barrier((mine, grad_pieces[1]))
    flat = (ns * nz * ffn_rows, width)
    ffn_sums = split_sum([mine.reshape(flat), arrived.reshape(flat)], ns)
    ffn_sums = [ffn_sums[0]] + [exchange(ffn_sums[k], "seq", k) for k in range(1, ns)]

    mine, theirs = vmem_call(
        functools.partial(conv_weight_kernel, taps, nz, ns, in_rows),
        [((nz * conv_rows + 2 * vec_rows, span), BF)] * 2,
        [
            pltpu.VMEM((ns * length + 2 * half, span), F32),
            pltpu.VMEM((ns * length + 2 * half, LANES), jnp.int32),
            pltpu.VMEM((ns * count, taps * span), BF),
            pltpu.VMEM((width, taps * span), F32),
            pltpu.VMEM((ns, rows, length, width), BF),
            pltpu.SemaphoreType.DMA((ns,)),
        ],
        smem=1,
        loose=range(1, 1 + ns),
    )(contig_lengths, *token_pieces, *grad_pieces)
    arrived = exchange(theirs, "row", 1)
    sums = vmem_call(
        functools.partial(conv_core_kernel, conv_rows),
        [((conv_rows + 2 * vec_rows, span), BF)] * nz,
        slack=2,
    )(mine, arrived)
    sums = [sums[0]] + [exchange(sums[j], "row", 2 * j) for j in range(1, nz)]

    masks = [k for k in range(ns) if edge_rows(k)]
    (input_grad,) = vmem_call(
        functools.partial(input_grad_kernel, taps, ns, rows, masks),
        [((count, width), F32)],
        [
            pltpu.VMEM((length + 2 * half, width), F32),
            pltpu.VMEM((length + 2 * half, LANES), jnp.int32),
            pltpu.VMEM((taps, count, width), BF),
        ],
        smem=1,
        kept=(0,),
    )(contig_lengths, conv_grad, after_grad, conv_full, *[grad_pieces[k] for k in masks])
    sums[0], input_grad = lax.optimization_barrier((sums[0], input_grad))

    conv_sum, conv_square, vec_sum = vmem_call(
        functools.partial(conv_final_kernel, nz, vec_rows),
        [((conv_rows, span), BF), ((8, LANES), F32), ((VEC_PAD, width), F32)],
        slack=2,
    )(*sums)
    conv_sums = [conv_sum] + [exchange(conv_sum, "seq", k) for k in range(1, ns)]

    ffn_sums = split_sum(ffn_sums, nz)
    ffn_sums = [ffn_sums[0]] + [exchange(ffn_sums[j], "row", 2 * j) for j in range(1, nz)]
    ffn_sums[0], conv_sums[-1] = lax.optimization_barrier((ffn_sums[0], conv_sums[-1]))
    (ffn_sum,) = vmem_call(
        functools.partial(ffn_final_kernel, nz), [((ffn_rows + VEC_PAD, width), BF)], slack=2
    )(*ffn_sums, conv_square)
    ffn_sums = [ffn_sum] + [exchange(ffn_sum, "seq", k) for k in range(1, ns)]
    (square,) = vmem_call(
        functools.partial(square_kernel, ns), [((8, LANES), F32)], slack=2
    )(*ffn_sums)
    squares = [square] + [exchange(square, "row", 2 * j) for j in range(1, nz)]
    (square,) = vmem_call(small_sum_kernel, [((8, LANES), F32)], slack=2)(*squares)
    squares = [square, exchange(square, "row", 1)]

    second_width = taps * width + hid + (out_rows // in_rows) * width + vectors.shape[0]
    results = [
        (conv_weight.shape, F32),
        (conv_weight.shape, F32),
        (inner_weight.shape, F32),
        (inner_weight.shape, F32),
        (outer_weight.shape, F32),
        (outer_weight.shape, F32),
        ((in_rows, second_width), F32),
    ]
    (
        norm,
        new_vectors,
        vector_first,
        new_conv,
        conv_first,
        new_inner,
        inner_first,
        new_outer,
        outer_first,
        second_moments,
    ) = vmem_call(
        functools.partial(adam_kernel, taps, ns),
        [((1, 1), F32), (vectors.shape, F32), (vectors.shape, F32), *results],
        [pltpu.VMEM(shape, dtype) for shape, dtype in results]
        + [
            pltpu.VMEM((width // LANES, out_rows, LANES), F32),
            pltpu.VMEM((width, LANES), F32),
            pltpu.SemaphoreType.DMA((8,)),
        ],
        kept=range(3),
        left=range(3, 10),
        slack=3,
    )(
        *conv_sums,
        *ffn_sums,
        vec_sum,
        *squares,
        conv_weight,
        inner_weight,
        outer_weight,
        vectors,
        conv_moments,
        inner_moments,
        outer_moments,
        vector_near,
    )
    return (
        layer_out.reshape(tokens.shape),
        input_grad.reshape(tokens.shape),
        norm.reshape(()),
        new_conv,
        conv_first,
        new_inner,
        inner_first,
        new_outer,
        outer_first,
        new_vectors,
        vector_first,
        second_moments,
    )


def solution(mesh):
    in_specs = (
        P("row", "seq", None),
        P("row", "seq", None),
        P("row", None),
        P(None, "row", None),
        P("row", None),
        P("row", None),
        P(),
        P(None, None, "row", None),
        P(None, "row", None),
        P(None, "row", None),
        P(),
    )
    out_specs = (
        P("row", "seq", None),
        P("row", "seq", None),
        P(),
        P(None, "row", None),
        P(None, "row", None),
        P("row", None),
        P("row", None),
        P("row", None),
        P("row", None),
        P(),
        P(),
        P("row", None),
    )
    return jax.shard_map(
        per_device, mesh=mesh, in_specs=in_specs, out_specs=out_specs, check_vma=False
    )
```

```python
import functools

import jax
import jax.numpy as jnp
from jax import lax
from jax.experimental import pallas as pl
from jax.experimental.pallas import tpu as pltpu
from jax.sharding import PartitionSpec as P

DILATION_STEP = 8

beta_one = 0.9
beta_two = 0.999
adam_eps = 1e-08
weight_decay = 0.1
matrix_rate = 0.03
vector_rate = 0.3
clip_level = 1.0
step_count = 10
norm_eps = 1e-05

F32 = jnp.float32
BF = jnp.bfloat16
VEC_PAD = 16
LANES = 128
SQRT_HALF = 0.7071067811865476
PDF_SCALE = 0.3989422804014327


def exchange(value, axis, mask):
    size = lax.axis_size(axis)
    return lax.ppermute(value, axis, [(i, i ^ mask) for i in range(size)])


def shift_along(value, axis, step):
    size = lax.axis_size(axis)
    pairs = [(i, i + step) for i in range(size) if 0 <= i + step < size]
    return lax.ppermute(value, axis, pairs)


def gelu_parts(v):
    cdf = 0.5 + 0.5 * lax.erf(v * SQRT_HALF)
    return v * cdf, cdf


def gelu_slope(v, cdf):
    return cdf + v * (jnp.exp(-0.5 * v * v) * PDF_SCALE)


def mean_of(v):
    return jnp.mean(v, axis=-1, keepdims=True)


def normalized(v):
    centred = v - mean_of(v)
    scale = lax.rsqrt(mean_of(centred * centred) + norm_eps)
    return centred * scale, scale


def fold_rows(v):
    rows, cols = v.shape
    return jnp.sum(v.reshape(rows // 8, 8, cols), axis=0)


def column_sum(acc):
    return jnp.sum(acc, axis=0, keepdims=True)


def loop_rows(total, step, body, init=0):
    return lax.fori_loop(
        0, total // step, lambda i, carry: body(pl.multiple_of(i * step, step), carry), init
    )


def dot(a, b):
    return jnp.dot(a, b, preferred_element_type=F32)


def dot_nt(a, b):
    return lax.dot_general(a, b, (((1,), (1,)), ((), ())), preferred_element_type=F32)


def dot_tn(a, b):
    return lax.dot_general(a, b, (((0,), (0,)), ((), ())), preferred_element_type=F32)


def place():
    seq_at = lax.axis_index("seq")
    row_at = lax.axis_index("row")
    return seq_at, row_at // 2, row_at % 2


def at(index, step):
    return pl.ds(pl.multiple_of(index * step, step), step)


def size_of(shape, dtype):
    total = jnp.dtype(dtype).itemsize
    for n in shape:
        total *= n
    return total


def vmem_call(kernel, outs, scratch=(), smem=0, loose=(), far=(), kept=(), left=(), slack=6):
    space = pl.BlockSpec(memory_space=pltpu.VMEM)
    anywhere = pl.BlockSpec(memory_space=pl.ANY)
    grant = slack * 1024 * 1024
    grant += sum(size_of(v.shape, v.dtype) for v in scratch if hasattr(v, "shape") and v.dtype in (F32, BF, jnp.int32))
    grant += sum(size_of(*outs[i]) for i in kept)

    def call(*args):
        fixed = [
            a
            if i < smem or i in loose
            else pltpu.with_memory_space_constraint(a, pltpu.HBM if i in far else pltpu.VMEM)
            for i, a in enumerate(args)
        ]
        return pl.pallas_call(
            kernel,
            out_shape=[
                jax.ShapeDtypeStruct(shape, dtype) if i in kept or i in left else pltpu.VMEM(shape, dtype)
                for i, (shape, dtype) in enumerate(outs)
            ],
            in_specs=[
                pl.BlockSpec(memory_space=pltpu.SMEM)
                if i < smem
                else pl.BlockSpec(memory_space=pltpu.HBM)
                if i in far
                else anywhere
                if i in loose
                else space
                for i in range(len(args))
            ],
            out_specs=[anywhere if i in left else space for i in range(len(outs))],
            scratch_shapes=list(scratch),
            cost_estimate=pl.CostEstimate(flops=1, bytes_accessed=1, transcendentals=0),
            compiler_params=pltpu.CompilerParams(vmem_limit_bytes=grant),
        )(*fixed)

    return call


def begin_copies(pairs, sems):
    copies = [pltpu.make_async_copy(src, dst, sems.at[i]) for i, (src, dst) in enumerate(pairs)]
    for copy in copies:
        copy.start()
    return copies


def end_copies(copies):
    for copy in copies:
        copy.wait()


def contigs(lens_ref, row, positions, row_length):
    found = jnp.zeros(positions.shape, jnp.int32)
    start = jnp.int32(0)
    for j in range(lens_ref.shape[1] - 1):
        start = start + lens_ref[row, j]
        found = found + (positions >= start).astype(jnp.int32)
    found = jnp.where(positions < 0, -1, found)
    return jnp.where(positions >= row_length, lens_ref.shape[1], found)


def masked_taps(src, cid, length, taps, half, store):
    centre = cid[pl.ds(half, length), :]

    def body(tap, carry):
        begin = pl.multiple_of(tap * DILATION_STEP, DILATION_STEP)
        keep = cid[pl.ds(begin, length), :] == centre
        for a in range(src.shape[1] // LANES):
            part = src[pl.ds(begin, length), a * LANES : (a + 1) * LANES]
            store(tap, a, jnp.where(keep, part, 0.0).astype(BF))
        return carry

    lax.fori_loop(0, taps, body, 0)


def round_kernel(ns, conv_far, inner_far, outer_far, tok_far, *refs):
    conv_part, left_edge, right_edge, conv_own, ffn_own, ffn_part = refs[:6]
    conv, inner, outer, sems = refs[6:]
    half = left_edge.shape[1]
    copies = begin_copies(
        [
            (conv_far, conv),
            (inner_far, inner),
            (outer_far, outer),
            (tok_far.at[:, :half], left_edge),
            (tok_far.at[:, tok_far.shape[1] - half :], right_edge),
        ],
        sems,
    )
    seq_at = lax.axis_index("seq")
    in_rows, hid = inner.shape
    quarter = hid // ns
    part = outer.shape[0] // ns
    span = conv.shape[2] // ns
    copies[0].wait()
    for t in range(conv.shape[0]):
        conv_own[t] = conv[t].astype(BF)
        conv_part[t] = conv[t, :, at(seq_at, span)].astype(BF)
    end_copies(copies[1:])
    for k in range(ns):
        ffn_own[k * in_rows : (k + 1) * in_rows, :] = inner[
            :, k * quarter : (k + 1) * quarter
        ].astype(BF)
    ffn_own[ns * in_rows :, :] = outer[...].astype(BF)
    ffn_part[:in_rows, :] = inner[:, at(seq_at, quarter)].astype(BF)
    ffn_part[in_rows:, :] = outer[at(seq_at, part), :].astype(BF)


def stack_kernel(count, *refs):
    ins, rest = refs[:count], refs[count:]
    out = rest[len(rest) // 2]
    for i, ref in enumerate(ins):
        out[i] = ref[...]
    if len(rest) > 1:
        rest[2][...] = rest[0][...]


def conv_kernel(taps, nz, ns, lens, vec, tok, left, right, own, other, *rest):
    pieces = (rest[:ns], rest[ns : 2 * ns])
    pre, after, full, ext, cid, cat, sems = rest[2 * ns :]
    seq_at, z_at, core_at = place()
    rows, length, width = tok.shape
    quarter = width // ns
    half = DILATION_STEP * (taps // 2)
    pairs = []
    for i, whole in enumerate((own, other)):
        core = core_at ^ i
        pairs.append((whole, full.at[:, z_at, core]))
        for k in range(ns):
            for j in range(1, nz):
                cols = at(seq_at ^ k, quarter)
                pairs.append((pieces[i][k].at[j - 1], full.at[:, z_at ^ j, core, :, cols]))
    copies = begin_copies(pairs, sems)
    span = length + 2 * half
    base = seq_at * length - half
    positions = base + lax.broadcasted_iota(jnp.int32, (span, LANES), 0)
    for r in range(rows):
        ext[0:half, :] = left[r].astype(F32)
        ext[half : half + length, :] = tok[r].astype(F32)
        ext[half + length :, :] = right[r].astype(F32)
        cid[...] = contigs(lens, r, positions, length * ns)

        def store(tap, a, value, r=r):
            cat[r * length : (r + 1) * length, at(tap * (width // LANES) + a, LANES)] = value

        masked_taps(ext, cid, length, taps, half, store)
    end_copies(copies)
    weights = full.reshape(taps * width, width)

    def product(r, carry):
        where = at(r, length)
        pre[where, :] = dot(cat[where, :], weights[...]) + vec[0:1, :]
        return carry

    lax.fori_loop(0, rows, product, 0)

    for r in range(rows):

        def norm(begin, carry, r=r):
            where = pl.ds(r * length + begin, 256)
            active, _ = gelu_parts(pre[where, :])
            unit, _ = normalized(active)
            after[where, :] = (
                tok[r, pl.ds(begin, 256), :].astype(F32) + unit * vec[1:2, :] + vec[2:3, :]
            )
            return carry

        loop_rows(length, 256, norm)


def ffn_kernel(nz, ns, *refs):
    after, cot, vec = refs[:3]
    wholes = refs[3:5]
    pieces = (refs[5 : 5 + ns], refs[5 + ns : 5 + 2 * ns])
    rest = refs[5 + 2 * ns :]
    layer, low, hidden, outer_grad, inner_grad, inner_full, sums, outer_full, slope, tmp = rest
    seq_at, z_at, core_at = place()
    count, width = after.shape
    hid = inner_full.shape[3]
    in_rows = inner_full.shape[2]
    quarter = hid // ns
    blocks = hid // width
    inner = inner_full.reshape(width, hid)
    outer = outer_full.reshape(hid, width)
    part = outer_full.shape[3]
    for i, whole in enumerate(wholes):
        core = core_at ^ i
        for q in range(ns):
            inner_full[z_at, core, :, q * quarter : (q + 1) * quarter] = whole[
                q * in_rows : (q + 1) * in_rows
            ]
            begin = ns * in_rows + q * part
            outer_full[z_at, core, q] = whole[begin : begin + part]
        for k in range(ns):
            piece = pieces[i][k]
            q = seq_at ^ k
            for j in range(1, nz):
                z = z_at ^ j
                inner_full[z, core, :, at(q, quarter)] = piece[j - 1, :in_rows]
                outer_full[z, core, q] = piece[j - 1, in_rows:]

    def lower(begin, carry):
        where = pl.ds(begin, 64)
        low[where, :] = after[where, :].astype(BF)
        return carry

    loop_rows(count, 64, lower)

    def up(b, carry):
        cols = at(b, width)
        tmp[...] = dot(low[...], inner[:, cols]) + vec[pl.ds(6 + b, 1), :]

        def act(begin, inside):
            where = pl.ds(begin, 128)
            v = tmp[where, :]
            active, cdf = gelu_parts(v)
            hidden[where, cols] = active.astype(BF)
            slope[where, cols] = gelu_slope(v, cdf)
            return inside

        loop_rows(count, 128, act)
        return carry

    lax.fori_loop(0, blocks, up, 0)
    tmp[...] = dot(hidden[...], outer[...]) + vec[3:4, :]
    zero = jnp.zeros((8, width), F32)

    def second(begin, carry):
        bias_sum, gain_sum, shift_sum = carry
        where = pl.ds(begin, 256)
        unit, scale = normalized(tmp[where, :])
        gain = vec[4:5, :]
        layer[where, :] = (after[where, :] + unit * gain + vec[5:6, :]).astype(BF)
        dy = cot[where, :].astype(F32)
        u = dy * gain
        grad = (scale * (u - mean_of(u) - unit * mean_of(u * unit))).astype(BF)
        outer_grad[where, :] = grad
        return (
            bias_sum + fold_rows(grad.astype(F32)),
            gain_sum + fold_rows(dy * unit),
            shift_sum + fold_rows(dy),
        )

    totals = loop_rows(count, 256, second, (zero, zero, zero))
    sums[...] = jnp.zeros(sums.shape, F32)
    for i, total in enumerate(totals):
        sums[3 + i : 4 + i, :] = column_sum(total)

    def down(b, carry):
        cols = at(b, width)
        tmp[...] = dot_nt(outer_grad[...], outer[cols, :])

        def act(begin, total):
            where = pl.ds(begin, 128)
            grad = (tmp[where, :] * slope[where, cols]).astype(BF)
            inner_grad[where, cols] = grad
            return total + fold_rows(grad.astype(F32))

        total = loop_rows(count, 128, act, zero)
        sums[pl.ds(6 + b, 1), :] = column_sum(total)
        return carry

    lax.fori_loop(0, blocks, down, 0)


def back_kernel(ns, rows, *refs):
    pre, cot, vec, inner_grad, inner_full, partial_sums, after_grad, conv_grad = refs[:8]
    inner = inner_full.reshape(pre.shape[1], inner_grad.shape[1])
    sends = refs[8 : 8 + ns]
    tmp, sums = refs[8 + ns :]
    seq_at = lax.axis_index("seq")
    count, width = pre.shape
    zero = jnp.zeros((8, width), F32)
    sums[...] = partial_sums[...]
    tmp[...] = dot_nt(inner_grad[...], inner[...])

    def first(begin, carry):
        bias_sum, gain_sum, shift_sum = carry
        where = pl.ds(begin, 256)
        upstream = cot[where, :].astype(F32) + tmp[where, :]
        after_grad[where, :] = upstream
        v = pre[where, :]
        active, cdf = gelu_parts(v)
        unit, scale = normalized(active)
        u = upstream * vec[1:2, :]
        grad = scale * (u - mean_of(u) - unit * mean_of(u * unit))
        grad = (grad * gelu_slope(v, cdf)).astype(BF)
        conv_grad[where, :] = grad
        return (
            bias_sum + fold_rows(grad.astype(F32)),
            gain_sum + fold_rows(upstream * unit),
            shift_sum + fold_rows(upstream),
        )

    totals = loop_rows(count, 256, first, (zero, zero, zero))
    for i, total in enumerate(totals):
        sums[i : i + 1, :] = column_sum(total)
    span = width // ns
    for k in range(ns):
        sends[k][0:count, :] = conv_grad[:, at(seq_at ^ k, span)]
        encode(sends[k], count, spread(sums[...]))
        begin = count + 2 * VEC_PAD * width // LANES
        if sends[k].shape[0] > begin:
            half = (sends[k].shape[0] - begin) // rows // (width // LANES)
            length = count // rows
            first = jnp.where((seq_at ^ k) > seq_at, length - half, 0)
            for r in range(rows):
                for a in range(width // LANES):
                    sends[k][begin : begin + half, :] = conv_grad[
                        at(r * (length // half) + first // half, half), a * LANES : (a + 1) * LANES
                    ]
                    begin += half


def spread(v):
    return jnp.concatenate(
        [v[:, a * LANES : (a + 1) * LANES] for a in range(v.shape[1] // LANES)], axis=0
    )


def gathered(v):
    return jnp.concatenate(
        [v[a * VEC_PAD : (a + 1) * VEC_PAD, :] for a in range(v.shape[0] // VEC_PAD)], axis=1
    )


def encode(ref, begin, v):
    rows = v.shape[0]
    high = v.astype(BF)
    ref[begin : begin + rows, :] = high
    ref[begin + rows : begin + 2 * rows, :] = (v - high.astype(F32)).astype(BF)


def decode(ref, begin, rows):
    high = ref[begin : begin + rows, :].astype(F32)
    return high + ref[begin + rows : begin + 2 * rows, :].astype(F32)


def tree_sum(values):
    values = list(values)
    while len(values) > 1:
        values = [values[i] + values[i + 1] for i in range(0, len(values), 2)]
    return values[0]


def ffn_weight_kernel(nz, ns, in_rows, out_rows, *refs):
    low, hidden, outer_grad, inner_grad, mine, theirs, outer_sum, inner_sum = refs
    seq_at, z_at, core_at = place()
    width = low.shape[1]
    hid = hidden.shape[1]
    part = out_rows // ns
    quarter = hid // ns

    def product(b, carry):
        cols = at(b, width)
        outer_sum[cols, :] = dot_tn(hidden[:, cols], outer_grad[...]).astype(BF)
        inner_sum[:, cols] = dot_tn(low[...], inner_grad[:, cols]).astype(BF)
        return carry

    lax.fori_loop(0, hid // width, product, 0)
    for i, out in enumerate((mine, theirs)):
        for k in range(ns):
            for j in range(nz):
                block = (z_at ^ j) * 2 + (core_at ^ i)
                out[k, j, :in_rows] = inner_sum[at(block, in_rows), at(seq_at ^ k, quarter)]
                out[k, j, in_rows:] = outer_sum[at(block * ns + (seq_at ^ k), part), :]


def conv_weight_kernel(taps, nz, ns, in_rows, *refs):
    lens = refs[0]
    far = refs[1 : 1 + ns]
    grads = refs[1 + ns : 1 + 2 * ns]
    mine, theirs, padded, cid, cat, total, toks, sems = refs[1 + 2 * ns :]
    copies = begin_copies([(far[k], toks.at[k]) for k in range(ns)], sems)
    seq_at, z_at, core_at = place()
    _, rows, length, width = toks.shape
    span = width // ns
    half = DILATION_STEP * (taps // 2)
    row_length = ns * length
    count = rows * length
    positions = lax.broadcasted_iota(jnp.int32, (row_length + 2 * half, LANES), 0) - half
    edge = jnp.zeros((half, span), F32)
    for r in range(rows):
        padded[0:half, :] = edge
        padded[half + row_length :, :] = edge
        cid[...] = contigs(lens, r, positions, row_length)
        for k in range(ns):
            padded[pl.ds(half + (seq_at ^ k) * length, length), :] = grads[k][
                r * length : (r + 1) * length, :
            ].astype(F32)
        for k in range(ns):
            base = (seq_at ^ k) * length
            centre = cid[pl.ds(pl.multiple_of(base + half, 8), length), :]
            for t in range(taps):
                begin = pl.multiple_of(base + DILATION_STEP * (taps - 1 - t), 8)
                keep = cid[pl.ds(begin, length), :] == centre
                value = jnp.where(keep, padded[pl.ds(begin, length), :], 0.0)
                low_row = k * count + r * length
                cat[low_row : low_row + length, t * span : (t + 1) * span] = value.astype(BF)
    end_copies(copies)
    for k in range(ns):
        value = tree_sum(
            [
                dot_tn(toks[k, r], cat[k * count + r * length : k * count + (r + 1) * length, :])
                for r in range(rows)
            ]
        )
        if k == 0:
            total[...] = value
        else:
            total[...] += value
    for i, out in enumerate((mine, theirs)):
        for j in range(nz):
            block = (z_at ^ j) * 2 + (core_at ^ i)
            for t in range(taps):
                begin = (j * taps + t) * in_rows
                out[begin : begin + in_rows, :] = total[
                    at(block, in_rows), t * span : (t + 1) * span
                ].astype(BF)
    vec_rows = VEC_PAD * width // LANES
    summed = tree_sum([decode(g, count, vec_rows) for g in grads])
    for out in (mine, theirs):
        encode(out, nz * taps * in_rows, summed)


def input_grad_kernel(taps, ns, rows, masks, *refs):
    lens, grad, after_grad, full_blocks = refs[:4]
    pieces = refs[4 : 4 + len(masks)]
    out, ext, cid, cat = refs[4 + len(masks) :]
    full = full_blocks.reshape(taps, grad.shape[1], grad.shape[1])
    seq_at = lax.axis_index("seq")
    half = DILATION_STEP * (taps // 2)
    width = grad.shape[1]
    length = grad.shape[0] // rows
    base = seq_at * length - half
    positions = base + lax.broadcasted_iota(jnp.int32, (length + 2 * half, LANES), 0)
    ext[0:half, :] = jnp.zeros((half, width), F32)
    ext[half + length :, :] = jnp.zeros((half, width), F32)
    for r in range(rows):
        ext[half : half + length, :] = grad[r * length : (r + 1) * length, :].astype(F32)
        for mask, piece in zip(masks, pieces):
            for step, begin in ((-1, 0), (1, half + length)):

                @pl.when((seq_at ^ mask) == seq_at + step)
                def _(r=r, piece=piece, begin=begin):
                    first = piece.shape[0] - rows * half * (width // LANES)
                    for a in range(width // LANES):
                        low = first + (r * (width // LANES) + a) * half
                        ext[begin : begin + half, a * LANES : (a + 1) * LANES] = piece[
                            low : low + half, :
                        ].astype(F32)

        cid[...] = contigs(lens, r, positions, length * ns)

        def store(tap, a, value, r=r):
            flipped = taps - 1 - tap
            cat[
                flipped, r * length : (r + 1) * length, a * LANES : (a + 1) * LANES
            ] = value

        masked_taps(ext, cid, length, taps, half, store)

    out[...] = after_grad[...]

    def product(t, carry):
        out[...] += dot_nt(cat[t], full[t])
        return carry

    lax.fori_loop(0, taps, product, 0)


def split_sum_kernel(count, *refs):
    ins, outs = refs[:count], refs[count:]
    rows = outs[0].shape[0]
    for p, out in enumerate(outs):

        def body(begin, carry, p=p, out=out):
            where = pl.ds(p * rows + begin, 64)
            out[pl.ds(begin, 64), :] = tree_sum([v[where, :].astype(F32) for v in ins]).astype(BF)
            return carry

        loop_rows(rows, 64, body)


def split_sum(ins, parts):
    rows, cols = ins[0].shape
    return vmem_call(
        functools.partial(split_sum_kernel, len(ins)),
        [((rows // parts, cols), BF)] * parts,
        slack=2,
    )(*ins)


def conv_core_kernel(rows, mine, got, *outs):
    vec_rows = (mine.shape[0] - rows * len(outs)) // 2
    begin_vec = rows * len(outs)
    summed = decode(mine, begin_vec, vec_rows) + decode(got, begin_vec, vec_rows)
    for p, out in enumerate(outs):

        def body(begin, carry, p=p, out=out):
            where = pl.ds(p * rows + begin, 64)
            out[pl.ds(begin, 64), :] = (mine[where, :].astype(F32) + got[where, :].astype(F32)).astype(
                BF
            )
            return carry

        loop_rows(rows, 64, body)
        encode(out, rows, summed)


def conv_final_kernel(count, vec_rows, *refs):
    ins, (out, square, vec_sum) = refs[:count], refs[count:]
    square[...] = summed_square(ins, out)
    vec_sum[...] = gathered(tree_sum([decode(v, out.shape[0], vec_rows) for v in ins]))


def summed_square(ins, out):
    def body(begin, carry):
        where = pl.ds(begin, 64)
        value = tree_sum([v[where, :].astype(F32) for v in ins]).astype(BF)
        out[where, :] = value
        wide = value.astype(F32)
        return carry + lane_fold(fold_rows(wide * wide))

    rows = ins[0].shape[0] // 64 * 64 if out.shape[0] % 64 else out.shape[0]
    return loop_rows(min(rows, out.shape[0]), 64, body, jnp.zeros((8, LANES), F32))


def lane_fold(v):
    return sum(v[:, a * LANES : (a + 1) * LANES] for a in range(v.shape[1] // LANES))


def ffn_final_kernel(count, *refs):
    ins, (conv_square, out) = refs[:count], refs[count:]
    rows = ins[0].shape[0]
    square = summed_square(ins, out.at[0:rows]) + conv_square[...]
    high = square.astype(BF)
    low = (square - high.astype(F32)).astype(BF)
    zero = jnp.zeros(high.shape, BF)
    tail = jnp.concatenate([high, low] + [zero] * (out.shape[1] // LANES - 2), axis=1)
    out[rows : rows + VEC_PAD, :] = jnp.concatenate([tail, jnp.zeros(tail.shape, BF)], axis=0)


def square_kernel(count, *refs):
    ins, out = refs[:count], refs[count]
    rows = ins[0].shape[0] - VEC_PAD
    parts = []
    for v in ins:
        tail = v[rows : rows + VEC_PAD, :].astype(F32)
        parts.append(tail[:8, :LANES] + tail[:8, LANES : 2 * LANES])
    out[...] = tree_sum(parts)


def small_sum_kernel(*refs):
    refs[-1][...] = tree_sum([v[...] for v in refs[:-1]])


def adam_math(weight, first, second, gradient, clip, rate, decay):
    clipped = gradient * clip
    first = beta_one * first + (1.0 - beta_one) * clipped
    second = beta_two * second + (1.0 - beta_two) * clipped * clipped
    first_hat = first / (1.0 - beta_one**step_count)
    second_hat = second / (1.0 - beta_two**step_count)
    weight = weight - rate * (first_hat / (jnp.sqrt(second_hat) + adam_eps) + decay * weight)
    return weight, first, second


def adam_kernel(taps, ns, *refs):
    conv_grads = refs[:ns]
    ffn_grads = refs[ns : 2 * ns]
    vec_sum, one, two, conv, inner, outer, vec, conv_m, inner_m, outer_m, vec_m = refs[
        2 * ns : 2 * ns + 11
    ]
    norm, new_vec, vec_first = refs[2 * ns + 11 : 2 * ns + 14]
    outs = refs[2 * ns + 14 : 2 * ns + 21]
    new_conv, conv_first, new_inner, inner_first, new_outer, outer_first, second = refs[
        2 * ns + 21 : 2 * ns + 28
    ]
    outer_second, vec_second, sems = refs[2 * ns + 28 :]
    seq_at, z_at, core_at = place()
    in_rows, width = conv.shape[1:]
    hid = inner.shape[1]
    out_rows = outer.shape[0]
    span = width // ns
    quarter = hid // ns
    part = out_rows // ns
    vec_count = vec.shape[0]
    vec_grad = vec_sum[0:vec_count, :]
    total = jnp.sum(one[...] + two[...]) + jnp.sum(vec_grad * vec_grad)
    value = jnp.sqrt(jnp.full((1, 1), total, F32))
    norm[...] = value
    clip = clip_level / jnp.maximum(value, clip_level)
    going = []

    def send(index, src, dst):
        copy = pltpu.make_async_copy(src, dst, sems.at[index])
        copy.start()
        going.append(copy)

    def conv_step(t, carry):
        for k in range(ns):
            cols = at(seq_at ^ k, span)
            w, m, v = adam_math(
                conv[t, :, cols],
                conv_m[0, t, :, cols],
                conv_m[1, t, :, cols],
                conv_grads[k][at(t, in_rows), :].astype(F32),
                clip,
                matrix_rate,
                weight_decay,
            )
            new_conv[t, :, cols] = w
            conv_first[t, :, cols] = m
            second[:, at(t * ns + (seq_at ^ k), span)] = v
        return carry

    lax.fori_loop(0, taps, conv_step, 0)
    send(0, new_conv, outs[0])
    send(1, conv_first, outs[1])
    send(2, second.at[:, : taps * width], outs[6].at[:, : taps * width])
    chunks = quarter // LANES

    for k in range(ns):

        def inner_step(a, carry, k=k):
            lanes = at((seq_at ^ k) * chunks + a, LANES)
            w, m, v = adam_math(
                inner[:, lanes],
                inner_m[0, :, lanes],
                inner_m[1, :, lanes],
                ffn_grads[k][0:in_rows, at(a, LANES)].astype(F32),
                clip,
                matrix_rate,
                weight_decay,
            )
            new_inner[:, lanes] = w
            inner_first[:, lanes] = m
            second[:, at(taps * width // LANES + (seq_at ^ k) * chunks + a, LANES)] = v
            return carry

        lax.fori_loop(0, chunks, inner_step, 0)
    send(3, new_inner, outs[2])
    send(4, inner_first, outs[3])
    for k in range(ns):
        where = at(seq_at ^ k, part)

        def outer_step(a, carry, k=k, where=where):
            lanes = at(a, LANES)
            w, m, v = adam_math(
                outer[where, lanes],
                outer_m[0, where, lanes],
                outer_m[1, where, lanes],
                ffn_grads[k][in_rows : in_rows + part, lanes].astype(F32),
                clip,
                matrix_rate,
                weight_decay,
            )
            new_outer[where, lanes] = w
            outer_first[where, lanes] = m
            outer_second[a, where, :] = v
            return carry

        lax.fori_loop(0, width // LANES, outer_step, 0)
    send(5, new_outer, outs[4])
    send(6, outer_first, outs[5])
    ratio = out_rows // in_rows
    base = taps * width + hid
    for e in range(ratio):
        for a in range(width // LANES):
            begin = base + e * width + a * LANES
            second[:, begin : begin + LANES] = outer_second[a, pl.ds(e, in_rows, stride=ratio), :]
    w, m, v = adam_math(vec[...], vec_m[0], vec_m[1], vec_grad, clip, vector_rate, 0.0)
    new_vec[...] = w
    vec_first[...] = m
    v = jnp.concatenate([v, jnp.zeros((LANES - vec_count, width), F32)], axis=0)
    vec_second[...] = jnp.transpose(v)
    begin = base + ratio * width
    block = z_at * 2 + core_at
    second[:, begin : begin + vec_count] = vec_second[at(block, in_rows), :][:, 0:vec_count]
    send(7, second.at[:, taps * width :], outs[6].at[:, taps * width :])
    end_copies(going)


def per_device(
    tokens,
    cotangent,
    contig_lengths,
    conv_weight,
    inner_weight,
    outer_weight,
    vectors,
    conv_moments,
    inner_moments,
    outer_moments,
    vector_moments,
):
    ns = lax.axis_size("seq")
    nr = lax.axis_size("row")
    nz = nr // 2
    seq_at = lax.axis_index("seq")
    rows, length, width = tokens.shape
    taps, in_rows, _ = conv_weight.shape
    hid = inner_weight.shape[1]
    out_rows = outer_weight.shape[0]
    count = rows * length
    half = DILATION_STEP * (taps // 2)
    span = width // ns
    quarter = hid // ns
    part = out_rows // ns

    ffn_rows = in_rows + part
    vec_rows = VEC_PAD * width // LANES
    conv_rows = taps * in_rows
    cot = cotangent.reshape(count, width)

    def edge_rows(k):
        near = any(abs((i ^ k) - i) == 1 for i in range(ns))
        return rows * half * (width // LANES) if near else 0

    conv_part, left_edge, right_edge, conv_own, ffn_own, ffn_part = vmem_call(
        functools.partial(round_kernel, ns),
        [
            ((taps, in_rows, span), BF),
            ((rows, half, width), BF),
            ((rows, half, width), BF),
            (conv_weight.shape, BF),
            ((ns * ffn_rows, width), BF),
            ((ffn_rows, width), BF),
        ],
        [
            pltpu.VMEM(conv_weight.shape, F32),
            pltpu.VMEM(inner_weight.shape, F32),
            pltpu.VMEM(outer_weight.shape, F32),
            pltpu.SemaphoreType.DMA((5,)),
        ],
        far=range(4),
        slack=2,
    )(conv_weight, inner_weight, outer_weight, tokens)
    got = [exchange(conv_part, "row", 2 * j) for j in range(1, nz)]
    got[0], conv_own, ffn_own = lax.optimization_barrier((got[0], conv_own, ffn_own))
    left = shift_along(right_edge, "seq", 1)
    right = shift_along(left_edge, "seq", -1)
    conv_other = exchange(conv_own, "row", 1)
    ffn_other = exchange(ffn_own, "row", 1)
    got[0], left, right = lax.optimization_barrier((got[0], left, right))
    (got,) = vmem_call(
        functools.partial(stack_kernel, nz - 1), [((nz - 1, taps, in_rows, span), BF)], slack=2
    )(*got)
    conv_pieces = [got] + [exchange(got, "seq", k) for k in range(1, ns)]
    conv_other_pieces = [exchange(got, "row", 1)]
    ffn_part, conv_other_pieces[0], conv_other, ffn_other = lax.optimization_barrier(
        (ffn_part, conv_other_pieces[0], conv_other, ffn_other)
    )
    ffn_got = [exchange(ffn_part, "row", 2 * j) for j in range(nz - 1, 0, -1)][::-1]
    late = lax.optimization_barrier((*ffn_got, *conv_pieces[1:]))
    ffn_got, conv_pieces[1:] = late[: nz - 1], late[nz - 1 :]
    conv_other_pieces += [exchange(p, "row", 1) for p in conv_pieces[1:]]
    ffn_got, vector_near = vmem_call(
        functools.partial(stack_kernel, nz - 1),
        [((nz - 1, ffn_rows, width), BF), (vector_moments.shape, F32)],
        slack=2,
    )(*ffn_got, vector_moments)
    ffn_pieces = [ffn_got] + [exchange(ffn_got, "seq", k) for k in range(1, ns)]

    pre, after, conv_full = vmem_call(
        functools.partial(conv_kernel, taps, nz, ns),
        [((count, width), F32), ((count, width), F32), ((taps, nz, 2, in_rows, width), BF)],
        [
            pltpu.VMEM((length + 2 * half, width), F32),
            pltpu.VMEM((length + 2 * half, LANES), jnp.int32),
            pltpu.VMEM((count, taps * width), BF),
            pltpu.SemaphoreType.DMA((2 * (1 + ns * (nz - 1)),)),
        ],
        smem=1,
        loose=range(5, 7 + 2 * ns),
    )(
        contig_lengths,
        vectors,
        tokens,
        left,
        right,
        conv_own,
        conv_other,
        *conv_pieces,
        *conv_other_pieces,
    )

    pre, tokens_late = lax.optimization_barrier((pre, tokens))
    token_pieces = [tokens] + [exchange(tokens_late, "seq", k) for k in range(1, ns)]
    late = lax.optimization_barrier((pre, *ffn_pieces))
    pre, ffn_pieces = late[0], late[1:]
    ffn_other_pieces = [exchange(p, "row", 1) for p in ffn_pieces]

    layer_out, low, hidden, outer_grad, inner_grad, inner_full, vec_sums = vmem_call(
        functools.partial(ffn_kernel, nz, ns),
        [
            ((count, width), BF),
            ((count, width), BF),
            ((count, hid), BF),
            ((count, width), BF),
            ((count, hid), BF),
            ((nz, 2, in_rows, hid), BF),
            ((VEC_PAD, width), F32),
        ],
        [
            pltpu.VMEM((nz, 2, ns, part, width), BF),
            pltpu.VMEM((count, hid), F32),
            pltpu.VMEM((count, width), F32),
        ],
        kept=(0,),
    )(after, cot, vectors, ffn_own, ffn_other, *ffn_pieces, *ffn_other_pieces)

    mine, theirs = vmem_call(
        functools.partial(ffn_weight_kernel, nz, ns, in_rows, out_rows),
        [((ns, nz, ffn_rows, width), BF)] * 2,
        [pltpu.VMEM((hid, width), BF), pltpu.VMEM((width, hid), BF)],
    )(low, hidden, outer_grad, inner_grad)

    inner_grad, mine = lax.optimization_barrier((inner_grad, mine))
    results = vmem_call(
        functools.partial(back_kernel, ns, rows),
        [((count, width), F32), ((count, width), BF)]
        + [
            ((count + 2 * vec_rows + edge_rows(k), span), BF)
            for k in range(ns)
        ],
        [pltpu.VMEM((count, width), F32), pltpu.VMEM((VEC_PAD, width), F32)],
    )(pre, cot, vectors, inner_grad, inner_full, vec_sums)
    after_grad, conv_grad = results[:2]
    grad_pieces = list(results[2:])
    late = lax.optimization_barrier((theirs, *grad_pieces, *token_pieces))
    theirs, grad_pieces, token_pieces = late[0], list(late[1 : 1 + ns]), late[1 + ns :]
    arrived = exchange(theirs, "row", 1)
    grad_pieces = grad_pieces[:1] + [exchange(grad_pieces[k], "seq", k) for k in range(1, ns)]
    mine, grad_pieces[1] = lax.optimization_barrier((mine, grad_pieces[1]))
    flat = (ns * nz * ffn_rows, width)
    ffn_sums = split_sum([mine.reshape(flat), arrived.reshape(flat)], ns)
    ffn_sums = [ffn_sums[0]] + [exchange(ffn_sums[k], "seq", k) for k in range(1, ns)]

    mine, theirs = vmem_call(
        functools.partial(conv_weight_kernel, taps, nz, ns, in_rows),
        [((nz * conv_rows + 2 * vec_rows, span), BF)] * 2,
        [
            pltpu.VMEM((ns * length + 2 * half, span), F32),
            pltpu.VMEM((ns * length + 2 * half, LANES), jnp.int32),
            pltpu.VMEM((ns * count, taps * span), BF),
            pltpu.VMEM((width, taps * span), F32),
            pltpu.VMEM((ns, rows, length, width), BF),
            pltpu.SemaphoreType.DMA((ns,)),
        ],
        smem=1,
        loose=range(1, 1 + ns),
    )(contig_lengths, *token_pieces, *grad_pieces)
    arrived = exchange(theirs, "row", 1)
    sums = vmem_call(
        functools.partial(conv_core_kernel, conv_rows),
        [((conv_rows + 2 * vec_rows, span), BF)] * nz,
        slack=2,
    )(mine, arrived)
    sums = [sums[0]] + [exchange(sums[j], "row", 2 * j) for j in range(1, nz)]

    masks = [k for k in range(ns) if edge_rows(k)]
    (input_grad,) = vmem_call(
        functools.partial(input_grad_kernel, taps, ns, rows, masks),
        [((count, width), F32)],
        [
            pltpu.VMEM((length + 2 * half, width), F32),
            pltpu.VMEM((length + 2 * half, LANES), jnp.int32),
            pltpu.VMEM((taps, count, width), BF),
        ],
        smem=1,
        kept=(0,),
    )(contig_lengths, conv_grad, after_grad, conv_full, *[grad_pieces[k] for k in masks])
    sums[0], input_grad = lax.optimization_barrier((sums[0], input_grad))

    conv_sum, conv_square, vec_sum = vmem_call(
        functools.partial(conv_final_kernel, nz, vec_rows),
        [((conv_rows, span), BF), ((8, LANES), F32), ((VEC_PAD, width), F32)],
        slack=2,
    )(*sums)
    conv_sums = [conv_sum] + [exchange(conv_sum, "seq", k) for k in range(1, ns)]

    ffn_sums = split_sum(ffn_sums, nz)
    ffn_sums = [ffn_sums[0]] + [exchange(ffn_sums[j], "row", 2 * j) for j in range(1, nz)]
    ffn_sums[0], conv_sums[-1] = lax.optimization_barrier((ffn_sums[0], conv_sums[-1]))
    (ffn_sum,) = vmem_call(
        functools.partial(ffn_final_kernel, nz), [((ffn_rows + VEC_PAD, width), BF)], slack=2
    )(*ffn_sums, conv_square)
    ffn_sums = [ffn_sum] + [exchange(ffn_sum, "seq", k) for k in range(1, ns)]
    (square,) = vmem_call(
        functools.partial(square_kernel, ns), [((8, LANES), F32)], slack=2
    )(*ffn_sums)
    squares = [square] + [exchange(square, "row", 2 * j) for j in range(1, nz)]
    (square,) = vmem_call(small_sum_kernel, [((8, LANES), F32)], slack=2)(*squares)
    squares = [square, exchange(square, "row", 1)]

    second_width = taps * width + hid + (out_rows // in_rows) * width + vectors.shape[0]
    results = [
        (conv_weight.shape, F32),
        (conv_weight.shape, F32),
        (inner_weight.shape, F32),
        (inner_weight.shape, F32),
        (outer_weight.shape, F32),
        (outer_weight.shape, F32),
        ((in_rows, second_width), F32),
    ]
    (
        norm,
        new_vectors,
        vector_first,
        new_conv,
        conv_first,
        new_inner,
        inner_first,
        new_outer,
        outer_first,
        second_moments,
    ) = vmem_call(
        functools.partial(adam_kernel, taps, ns),
        [((1, 1), F32), (vectors.shape, F32), (vectors.shape, F32), *results],
        [pltpu.VMEM(shape, dtype) for shape, dtype in results]
        + [
            pltpu.VMEM((width // LANES, out_rows, LANES), F32),
            pltpu.VMEM((width, LANES), F32),
            pltpu.SemaphoreType.DMA((8,)),
        ],
        kept=range(3),
        left=range(3, 10),
        slack=3,
    )(
        *conv_sums,
        *ffn_sums,
        vec_sum,
        *squares,
        conv_weight,
        inner_weight,
        outer_weight,
        vectors,
        conv_moments,
        inner_moments,
        outer_moments,
        vector_near,
    )
    return (
        layer_out.reshape(tokens.shape),
        input_grad.reshape(tokens.shape),
        norm.reshape(()),
        new_conv,
        conv_first,
        new_inner,
        inner_first,
        new_outer,
        outer_first,
        new_vectors,
        vector_first,
        second_moments,
    )


def solution(mesh):
    in_specs = (
        P("row", "seq", None),
        P("row", "seq", None),
        P("row", None),
        P(None, "row", None),
        P("row", None),
        P("row", None),
        P(),
        P(None, None, "row", None),
        P(None, "row", None),
        P(None, "row", None),
        P(),
    )
    out_specs = (
        P("row", "seq", None),
        P("row", "seq", None),
        P(),
        P(None, "row", None),
        P(None, "row", None),
        P("row", None),
        P("row", None),
        P("row", None),
        P("row", None),
        P(),
        P(),
        P("row", None),
    )
    return jax.shard_map(
        per_device, mesh=mesh, in_specs=in_specs, out_specs=out_specs, check_vma=False
    )
```

```python
import functools

import jax
import jax.numpy as jnp
from jax import lax
from jax.experimental import pallas as pl
from jax.experimental.pallas import tpu as pltpu
from jax.sharding import PartitionSpec as P

DILATION_STEP = 8

beta_one = 0.9
beta_two = 0.999
adam_eps = 1e-08
weight_decay = 0.1
matrix_rate = 0.03
vector_rate = 0.3
clip_level = 1.0
step_count = 10
norm_eps = 1e-05

F32 = jnp.float32
BF = jnp.bfloat16
VEC_PAD = 16
LANES = 128
SQRT_HALF = 0.7071067811865476
PDF_SCALE = 0.3989422804014327


def exchange(value, axis, mask):
    size = lax.axis_size(axis)
    return lax.ppermute(value, axis, [(i, i ^ mask) for i in range(size)])


def shift_along(value, axis, step):
    size = lax.axis_size(axis)
    pairs = [(i, i + step) for i in range(size) if 0 <= i + step < size]
    return lax.ppermute(value, axis, pairs)


def gelu_parts(v):
    cdf = 0.5 + 0.5 * lax.erf(v * SQRT_HALF)
    return v * cdf, cdf


def gelu_slope(v, cdf):
    return cdf + v * (jnp.exp(-0.5 * v * v) * PDF_SCALE)


def mean_of(v):
    return jnp.mean(v, axis=-1, keepdims=True)


def normalized(v):
    centred = v - mean_of(v)
    scale = lax.rsqrt(mean_of(centred * centred) + norm_eps)
    return centred * scale, scale


def fold_rows(v):
    rows, cols = v.shape
    return jnp.sum(v.reshape(rows // 8, 8, cols), axis=0)


def column_sum(acc):
    return jnp.sum(acc, axis=0, keepdims=True)


def loop_rows(total, step, body, init=0):
    return lax.fori_loop(
        0, total // step, lambda i, carry: body(pl.multiple_of(i * step, step), carry), init
    )


def dot(a, b):
    return jnp.dot(a, b, preferred_element_type=F32)


def dot_nt(a, b):
    return lax.dot_general(a, b, (((1,), (1,)), ((), ())), preferred_element_type=F32)


def dot_tn(a, b):
    return lax.dot_general(a, b, (((0,), (0,)), ((), ())), preferred_element_type=F32)


def place():
    seq_at = lax.axis_index("seq")
    row_at = lax.axis_index("row")
    return seq_at, row_at // 2, row_at % 2


def at(index, step):
    return pl.ds(pl.multiple_of(index * step, step), step)


def size_of(shape, dtype):
    total = jnp.dtype(dtype).itemsize
    for n in shape:
        total *= n
    return total


def vmem_call(kernel, outs, scratch=(), smem=0, loose=(), far=(), kept=(), left=(), slack=6):
    space = pl.BlockSpec(memory_space=pltpu.VMEM)
    anywhere = pl.BlockSpec(memory_space=pl.ANY)
    grant = slack * 1024 * 1024
    grant += sum(size_of(v.shape, v.dtype) for v in scratch if hasattr(v, "shape") and v.dtype in (F32, BF, jnp.int32))
    grant += sum(size_of(*outs[i]) for i in kept)

    def call(*args):
        fixed = [
            a
            if i < smem or i in loose
            else pltpu.with_memory_space_constraint(a, pltpu.HBM if i in far else pltpu.VMEM)
            for i, a in enumerate(args)
        ]
        return pl.pallas_call(
            kernel,
            out_shape=[
                jax.ShapeDtypeStruct(shape, dtype) if i in kept or i in left else pltpu.VMEM(shape, dtype)
                for i, (shape, dtype) in enumerate(outs)
            ],
            in_specs=[
                pl.BlockSpec(memory_space=pltpu.SMEM)
                if i < smem
                else pl.BlockSpec(memory_space=pltpu.HBM)
                if i in far
                else anywhere
                if i in loose
                else space
                for i in range(len(args))
            ],
            out_specs=[anywhere if i in left else space for i in range(len(outs))],
            scratch_shapes=list(scratch),
            cost_estimate=pl.CostEstimate(flops=1, bytes_accessed=1, transcendentals=0),
            compiler_params=pltpu.CompilerParams(vmem_limit_bytes=grant),
        )(*fixed)

    return call


def begin_copies(pairs, sems):
    copies = [pltpu.make_async_copy(src, dst, sems.at[i]) for i, (src, dst) in enumerate(pairs)]
    for copy in copies:
        copy.start()
    return copies


def end_copies(copies):
    for copy in copies:
        copy.wait()


def contigs(lens_ref, row, positions, row_length):
    found = jnp.zeros(positions.shape, jnp.int32)
    start = jnp.int32(0)
    for j in range(lens_ref.shape[1] - 1):
        start = start + lens_ref[row, j]
        found = found + (positions >= start).astype(jnp.int32)
    found = jnp.where(positions < 0, -1, found)
    return jnp.where(positions >= row_length, lens_ref.shape[1], found)


def masked_taps(src, cid, length, taps, half, store):
    centre = cid[pl.ds(half, length), :]

    def body(tap, carry):
        begin = pl.multiple_of(tap * DILATION_STEP, DILATION_STEP)
        keep = cid[pl.ds(begin, length), :] == centre
        for a in range(src.shape[1] // LANES):
            part = src[pl.ds(begin, length), a * LANES : (a + 1) * LANES]
            store(tap, a, jnp.where(keep, part, 0.0).astype(BF))
        return carry

    lax.fori_loop(0, taps, body, 0)


def round_kernel(ns, masks, conv_far, inner_far, outer_far, tok_far, *refs):
    conv_part, conv_own, ffn_own, ffn_part = refs[:4]
    edges = refs[4 : 4 + len(masks)]
    conv, inner, outer, sems = refs[4 + len(masks) :]
    seq_at = lax.axis_index("seq")
    pairs = [(conv_far, conv), (inner_far, inner), (outer_far, outer)]
    for mask, edge in zip(masks, edges):
        half = edge.shape[1]
        last = jnp.where((seq_at ^ mask) > seq_at, tok_far.shape[1] // half - 1, 0)
        pairs.append((tok_far.at[:, at(last, half)], edge))
    copies = begin_copies(pairs, sems)
    in_rows, hid = inner.shape
    quarter = hid // ns
    part = outer.shape[0] // ns
    span = conv.shape[2] // ns
    copies[0].wait()
    for t in range(conv.shape[0]):
        conv_own[t] = conv[t].astype(BF)
        conv_part[t] = conv[t, :, at(seq_at, span)].astype(BF)
    end_copies(copies[1:])
    for k in range(ns):
        ffn_own[k * in_rows : (k + 1) * in_rows, :] = inner[
            :, k * quarter : (k + 1) * quarter
        ].astype(BF)
    ffn_own[ns * in_rows :, :] = outer[...].astype(BF)
    ffn_part[:in_rows, :] = inner[:, at(seq_at, quarter)].astype(BF)
    ffn_part[in_rows:, :] = outer[at(seq_at, part), :].astype(BF)


def stack_kernel(count, *refs):
    ins, rest = refs[:count], refs[count:]
    out = rest[len(rest) // 2]
    for i, ref in enumerate(ins):
        out[i] = ref[...]
    if len(rest) > 1:
        rest[2][...] = rest[0][...]


def conv_kernel(taps, nz, ns, masks, lens, vec, tok, own, other, *rest):
    edges, rest = rest[: len(masks)], rest[len(masks) :]
    pieces = (rest[:ns], rest[ns : 2 * ns])
    pre, after, full, ext, cid, cat, sems = rest[2 * ns :]
    seq_at, z_at, core_at = place()
    rows, length, width = tok.shape
    quarter = width // ns
    half = DILATION_STEP * (taps // 2)
    pairs = []
    for i, whole in enumerate((own, other)):
        core = core_at ^ i
        pairs.append((whole, full.at[:, z_at, core]))
        for k in range(ns):
            for j in range(1, nz):
                cols = at(seq_at ^ k, quarter)
                pairs.append((pieces[i][k].at[j - 1], full.at[:, z_at ^ j, core, :, cols]))
    copies = begin_copies(pairs, sems)
    span = length + 2 * half
    base = seq_at * length - half
    positions = base + lax.broadcasted_iota(jnp.int32, (span, LANES), 0)
    ext[0:half, :] = jnp.zeros((half, width), F32)
    ext[half + length :, :] = jnp.zeros((half, width), F32)
    for r in range(rows):
        ext[half : half + length, :] = tok[r].astype(F32)
        for mask, edge in zip(masks, edges):
            for step, to, begin in ((-1, 0, edge.shape[1] - half), (1, half + length, 0)):

                @pl.when((seq_at ^ mask) == seq_at + step)
                def _(r=r, edge=edge, to=to, begin=begin):
                    ext[to : to + half, :] = edge[r, begin : begin + half, :].astype(F32)

        cid[...] = contigs(lens, r, positions, length * ns)

        def store(tap, a, value, r=r):
            cat[r * length : (r + 1) * length, at(tap * (width // LANES) + a, LANES)] = value

        masked_taps(ext, cid, length, taps, half, store)
    end_copies(copies)
    weights = full.reshape(taps * width, width)

    def product(r, carry):
        where = at(r, length)
        pre[where, :] = dot(cat[where, :], weights[...]) + vec[0:1, :]
        return carry

    lax.fori_loop(0, rows, product, 0)

    for r in range(rows):

        def norm(begin, carry, r=r):
            where = pl.ds(r * length + begin, 256)
            active, _ = gelu_parts(pre[where, :])
            unit, _ = normalized(active)
            after[where, :] = (
                tok[r, pl.ds(begin, 256), :].astype(F32) + unit * vec[1:2, :] + vec[2:3, :]
            )
            return carry

        loop_rows(length, 256, norm)


def ffn_kernel(nz, ns, *refs):
    after, cot, vec = refs[:3]
    wholes = refs[3:5]
    pieces = (refs[5 : 5 + ns], refs[5 + ns : 5 + 2 * ns])
    rest = refs[5 + 2 * ns :]
    layer, low, hidden, outer_grad, inner_grad, inner_full, sums, outer_full, slope, tmp = rest
    seq_at, z_at, core_at = place()
    count, width = after.shape
    hid = inner_full.shape[3]
    in_rows = inner_full.shape[2]
    quarter = hid // ns
    blocks = hid // width
    inner = inner_full.reshape(width, hid)
    outer = outer_full.reshape(hid, width)
    part = outer_full.shape[3]
    for i, whole in enumerate(wholes):
        core = core_at ^ i
        for q in range(ns):
            inner_full[z_at, core, :, q * quarter : (q + 1) * quarter] = whole[
                q * in_rows : (q + 1) * in_rows
            ]
            begin = ns * in_rows + q * part
            outer_full[z_at, core, q] = whole[begin : begin + part]
        for k in range(ns):
            piece = pieces[i][k]
            q = seq_at ^ k
            for j in range(1, nz):
                z = z_at ^ j
                inner_full[z, core, :, at(q, quarter)] = piece[j - 1, :in_rows]
                outer_full[z, core, q] = piece[j - 1, in_rows:]

    def lower(begin, carry):
        where = pl.ds(begin, 64)
        low[where, :] = after[where, :].astype(BF)
        return carry

    loop_rows(count, 64, lower)

    def up(b, carry):
        cols = at(b, width)
        tmp[...] = dot(low[...], inner[:, cols]) + vec[pl.ds(6 + b, 1), :]

        def act(begin, inside):
            where = pl.ds(begin, 128)
            v = tmp[where, :]
            active, cdf = gelu_parts(v)
            hidden[where, cols] = active.astype(BF)
            slope[where, cols] = gelu_slope(v, cdf)
            return inside

        loop_rows(count, 128, act)
        return carry

    lax.fori_loop(0, blocks, up, 0)
    tmp[...] = dot(hidden[...], outer[...]) + vec[3:4, :]
    zero = jnp.zeros((8, width), F32)

    def second(begin, carry):
        bias_sum, gain_sum, shift_sum = carry
        where = pl.ds(begin, 256)
        unit, scale = normalized(tmp[where, :])
        gain = vec[4:5, :]
        layer[where, :] = (after[where, :] + unit * gain + vec[5:6, :]).astype(BF)
        dy = cot[where, :].astype(F32)
        u = dy * gain
        grad = (scale * (u - mean_of(u) - unit * mean_of(u * unit))).astype(BF)
        outer_grad[where, :] = grad
        return (
            bias_sum + fold_rows(grad.astype(F32)),
            gain_sum + fold_rows(dy * unit),
            shift_sum + fold_rows(dy),
        )

    totals = loop_rows(count, 256, second, (zero, zero, zero))
    sums[...] = jnp.zeros(sums.shape, F32)
    for i, total in enumerate(totals):
        sums[3 + i : 4 + i, :] = column_sum(total)

    def down(b, carry):
        cols = at(b, width)
        tmp[...] = dot_nt(outer_grad[...], outer[cols, :])

        def act(begin, total):
            where = pl.ds(begin, 128)
            grad = (tmp[where, :] * slope[where, cols]).astype(BF)
            inner_grad[where, cols] = grad
            return total + fold_rows(grad.astype(F32))

        total = loop_rows(count, 128, act, zero)
        sums[pl.ds(6 + b, 1), :] = column_sum(total)
        return carry

    lax.fori_loop(0, blocks, down, 0)


def back_kernel(ns, rows, *refs):
    pre, cot, vec, inner_grad, inner_full, partial_sums, after_grad, conv_grad = refs[:8]
    inner = inner_full.reshape(pre.shape[1], inner_grad.shape[1])
    sends = refs[8 : 8 + ns]
    tmp, sums = refs[8 + ns :]
    seq_at = lax.axis_index("seq")
    count, width = pre.shape
    zero = jnp.zeros((8, width), F32)
    sums[...] = partial_sums[...]
    tmp[...] = dot_nt(inner_grad[...], inner[...])

    def first(begin, carry):
        bias_sum, gain_sum, shift_sum = carry
        where = pl.ds(begin, 256)
        upstream = cot[where, :].astype(F32) + tmp[where, :]
        after_grad[where, :] = upstream
        v = pre[where, :]
        active, cdf = gelu_parts(v)
        unit, scale = normalized(active)
        u = upstream * vec[1:2, :]
        grad = scale * (u - mean_of(u) - unit * mean_of(u * unit))
        grad = (grad * gelu_slope(v, cdf)).astype(BF)
        conv_grad[where, :] = grad
        return (
            bias_sum + fold_rows(grad.astype(F32)),
            gain_sum + fold_rows(upstream * unit),
            shift_sum + fold_rows(upstream),
        )

    totals = loop_rows(count, 256, first, (zero, zero, zero))
    for i, total in enumerate(totals):
        sums[i : i + 1, :] = column_sum(total)
    span = width // ns
    for k in range(ns):
        sends[k][0:count, :] = conv_grad[:, at(seq_at ^ k, span)]
        encode(sends[k], count, spread(sums[...]))
        begin = count + 2 * VEC_PAD * width // LANES
        if sends[k].shape[0] > begin:
            half = (sends[k].shape[0] - begin) // rows // (width // LANES)
            length = count // rows
            first = jnp.where((seq_at ^ k) > seq_at, length - half, 0)
            for r in range(rows):
                for a in range(width // LANES):
                    sends[k][begin : begin + half, :] = conv_grad[
                        at(r * (length // half) + first // half, half), a * LANES : (a + 1) * LANES
                    ]
                    begin += half


def spread(v):
    return jnp.concatenate(
        [v[:, a * LANES : (a + 1) * LANES] for a in range(v.shape[1] // LANES)], axis=0
    )


def gathered(v):
    return jnp.concatenate(
        [v[a * VEC_PAD : (a + 1) * VEC_PAD, :] for a in range(v.shape[0] // VEC_PAD)], axis=1
    )


def encode(ref, begin, v):
    rows = v.shape[0]
    high = v.astype(BF)
    ref[begin : begin + rows, :] = high
    ref[begin + rows : begin + 2 * rows, :] = (v - high.astype(F32)).astype(BF)


def decode(ref, begin, rows):
    high = ref[begin : begin + rows, :].astype(F32)
    return high + ref[begin + rows : begin + 2 * rows, :].astype(F32)


def tree_sum(values):
    values = list(values)
    while len(values) > 1:
        values = [values[i] + values[i + 1] for i in range(0, len(values), 2)]
    return values[0]


def ffn_weight_kernel(nz, ns, in_rows, out_rows, *refs):
    low, hidden, outer_grad, inner_grad, mine, theirs, outer_sum, inner_sum = refs
    seq_at, z_at, core_at = place()
    width = low.shape[1]
    hid = hidden.shape[1]
    part = out_rows // ns
    quarter = hid // ns

    def product(b, carry):
        cols = at(b, width)
        outer_sum[cols, :] = dot_tn(hidden[:, cols], outer_grad[...]).astype(BF)
        inner_sum[:, cols] = dot_tn(low[...], inner_grad[:, cols]).astype(BF)
        return carry

    lax.fori_loop(0, hid // width, product, 0)
    for i, out in enumerate((mine, theirs)):
        for k in range(ns):
            for j in range(nz):
                block = (z_at ^ j) * 2 + (core_at ^ i)
                out[k, j, :in_rows] = inner_sum[at(block, in_rows), at(seq_at ^ k, quarter)]
                out[k, j, in_rows:] = outer_sum[at(block * ns + (seq_at ^ k), part), :]


def conv_weight_kernel(taps, nz, ns, in_rows, *refs):
    lens = refs[0]
    far = refs[1 : 1 + ns]
    grads = refs[1 + ns : 1 + 2 * ns]
    mine, theirs, padded, cid, cat, total, toks, sems = refs[1 + 2 * ns :]
    copies = begin_copies([(far[k], toks.at[k]) for k in range(ns)], sems)
    seq_at, z_at, core_at = place()
    _, rows, length, width = toks.shape
    span = width // ns
    half = DILATION_STEP * (taps // 2)
    row_length = ns * length
    count = rows * length
    positions = lax.broadcasted_iota(jnp.int32, (row_length + 2 * half, LANES), 0) - half
    edge = jnp.zeros((half, span), F32)
    for r in range(rows):
        padded[0:half, :] = edge
        padded[half + row_length :, :] = edge
        cid[...] = contigs(lens, r, positions, row_length)
        for k in range(ns):
            padded[pl.ds(half + (seq_at ^ k) * length, length), :] = grads[k][
                r * length : (r + 1) * length, :
            ].astype(F32)
        for k in range(ns):
            base = (seq_at ^ k) * length
            centre = cid[pl.ds(pl.multiple_of(base + half, 8), length), :]
            for t in range(taps):
                begin = pl.multiple_of(base + DILATION_STEP * (taps - 1 - t), 8)
                keep = cid[pl.ds(begin, length), :] == centre
                value = jnp.where(keep, padded[pl.ds(begin, length), :], 0.0)
                low_row = k * count + r * length
                cat[low_row : low_row + length, t * span : (t + 1) * span] = value.astype(BF)
    end_copies(copies)
    for k in range(ns):
        value = tree_sum(
            [
                dot_tn(toks[k, r], cat[k * count + r * length : k * count + (r + 1) * length, :])
                for r in range(rows)
            ]
        )
        if k == 0:
            total[...] = value
        else:
            total[...] += value
    for i, out in enumerate((mine, theirs)):
        for j in range(nz):
            block = (z_at ^ j) * 2 + (core_at ^ i)
            for t in range(taps):
                begin = (j * taps + t) * in_rows
                out[begin : begin + in_rows, :] = total[
                    at(block, in_rows), t * span : (t + 1) * span
                ].astype(BF)
    vec_rows = VEC_PAD * width // LANES
    summed = tree_sum([decode(g, count, vec_rows) for g in grads])
    for out in (mine, theirs):
        encode(out, nz * taps * in_rows, summed)


def input_grad_kernel(taps, ns, rows, masks, *refs):
    lens, grad, after_grad, full_blocks = refs[:4]
    pieces = refs[4 : 4 + len(masks)]
    out, ext, cid, cat = refs[4 + len(masks) :]
    full = full_blocks.reshape(taps, grad.shape[1], grad.shape[1])
    seq_at = lax.axis_index("seq")
    half = DILATION_STEP * (taps // 2)
    width = grad.shape[1]
    length = grad.shape[0] // rows
    base = seq_at * length - half
    positions = base + lax.broadcasted_iota(jnp.int32, (length + 2 * half, LANES), 0)
    ext[0:half, :] = jnp.zeros((half, width), F32)
    ext[half + length :, :] = jnp.zeros((half, width), F32)
    for r in range(rows):
        ext[half : half + length, :] = grad[r * length : (r + 1) * length, :].astype(F32)
        for mask, piece in zip(masks, pieces):
            for step, begin in ((-1, 0), (1, half + length)):

                @pl.when((seq_at ^ mask) == seq_at + step)
                def _(r=r, piece=piece, begin=begin):
                    first = piece.shape[0] - rows * half * (width // LANES)
                    for a in range(width // LANES):
                        low = first + (r * (width // LANES) + a) * half
                        ext[begin : begin + half, a * LANES : (a + 1) * LANES] = piece[
                            low : low + half, :
                        ].astype(F32)

        cid[...] = contigs(lens, r, positions, length * ns)

        def store(tap, a, value, r=r):
            flipped = taps - 1 - tap
            cat[
                flipped, r * length : (r + 1) * length, a * LANES : (a + 1) * LANES
            ] = value

        masked_taps(ext, cid, length, taps, half, store)

    out[...] = after_grad[...]

    def product(t, carry):
        out[...] += dot_nt(cat[t], full[t])
        return carry

    lax.fori_loop(0, taps, product, 0)


def split_sum_kernel(count, *refs):
    ins, outs = refs[:count], refs[count:]
    rows = outs[0].shape[0]
    for p, out in enumerate(outs):

        def body(begin, carry, p=p, out=out):
            where = pl.ds(p * rows + begin, 64)
            out[pl.ds(begin, 64), :] = tree_sum([v[where, :].astype(F32) for v in ins]).astype(BF)
            return carry

        loop_rows(rows, 64, body)


def split_sum(ins, parts):
    rows, cols = ins[0].shape
    return vmem_call(
        functools.partial(split_sum_kernel, len(ins)),
        [((rows // parts, cols), BF)] * parts,
        slack=2,
    )(*ins)


def conv_core_kernel(rows, mine, got, *outs):
    vec_rows = (mine.shape[0] - rows * len(outs)) // 2
    begin_vec = rows * len(outs)
    summed = decode(mine, begin_vec, vec_rows) + decode(got, begin_vec, vec_rows)
    for p, out in enumerate(outs):

        def body(begin, carry, p=p, out=out):
            where = pl.ds(p * rows + begin, 64)
            out[pl.ds(begin, 64), :] = (mine[where, :].astype(F32) + got[where, :].astype(F32)).astype(
                BF
            )
            return carry

        loop_rows(rows, 64, body)
        encode(out, rows, summed)


def conv_final_kernel(count, vec_rows, *refs):
    ins, (out, square, vec_sum) = refs[:count], refs[count:]
    square[...] = summed_square(ins, out)
    vec_sum[...] = gathered(tree_sum([decode(v, out.shape[0], vec_rows) for v in ins]))


def summed_square(ins, out):
    def body(begin, carry):
        where = pl.ds(begin, 64)
        value = tree_sum([v[where, :].astype(F32) for v in ins]).astype(BF)
        out[where, :] = value
        wide = value.astype(F32)
        return carry + lane_fold(fold_rows(wide * wide))

    rows = ins[0].shape[0] // 64 * 64 if out.shape[0] % 64 else out.shape[0]
    return loop_rows(min(rows, out.shape[0]), 64, body, jnp.zeros((8, LANES), F32))


def lane_fold(v):
    return sum(v[:, a * LANES : (a + 1) * LANES] for a in range(v.shape[1] // LANES))


def ffn_final_kernel(count, *refs):
    ins, (conv_square, out) = refs[:count], refs[count:]
    rows = ins[0].shape[0]
    square = summed_square(ins, out.at[0:rows]) + conv_square[...]
    high = square.astype(BF)
    low = (square - high.astype(F32)).astype(BF)
    zero = jnp.zeros(high.shape, BF)
    tail = jnp.concatenate([high, low] + [zero] * (out.shape[1] // LANES - 2), axis=1)
    out[rows : rows + VEC_PAD, :] = jnp.concatenate([tail, jnp.zeros(tail.shape, BF)], axis=0)


def square_kernel(count, *refs):
    ins, out = refs[:count], refs[count]
    rows = ins[0].shape[0] - VEC_PAD
    parts = []
    for v in ins:
        tail = v[rows : rows + VEC_PAD, :].astype(F32)
        parts.append(tail[:8, :LANES] + tail[:8, LANES : 2 * LANES])
    out[...] = tree_sum(parts)


def small_sum_kernel(*refs):
    refs[-1][...] = tree_sum([v[...] for v in refs[:-1]])


def adam_math(weight, first, second, gradient, clip, rate, decay):
    clipped = gradient * clip
    first = beta_one * first + (1.0 - beta_one) * clipped
    second = beta_two * second + (1.0 - beta_two) * clipped * clipped
    first_hat = first * (1.0 / (1.0 - beta_one**step_count))
    second_hat = second * (1.0 / (1.0 - beta_two**step_count))
    weight = weight - rate * (first_hat / (jnp.sqrt(second_hat) + adam_eps) + decay * weight)
    return weight, first, second


def adam_kernel(taps, ns, *refs):
    conv_grads = refs[:ns]
    ffn_grads = refs[ns : 2 * ns]
    vec_sum, one, two, conv, inner, outer, vec, conv_m, inner_m, outer_m, vec_m = refs[
        2 * ns : 2 * ns + 11
    ]
    norm, new_vec, vec_first = refs[2 * ns + 11 : 2 * ns + 14]
    outs = refs[2 * ns + 14 : 2 * ns + 21]
    new_conv, conv_first, new_inner, inner_first, new_outer, outer_first, second = refs[
        2 * ns + 21 : 2 * ns + 28
    ]
    outer_second, vec_second, sems = refs[2 * ns + 28 :]
    seq_at, z_at, core_at = place()
    in_rows, width = conv.shape[1:]
    hid = inner.shape[1]
    out_rows = outer.shape[0]
    span = width // ns
    quarter = hid // ns
    part = out_rows // ns
    vec_count = vec.shape[0]
    vec_grad = vec_sum[0:vec_count, :]
    total = jnp.sum(one[...] + two[...]) + jnp.sum(vec_grad * vec_grad)
    value = jnp.sqrt(jnp.full((1, 1), total, F32))
    norm[...] = value
    clip = clip_level / jnp.maximum(value, clip_level)
    going = []

    def send(index, src, dst):
        copy = pltpu.make_async_copy(src, dst, sems.at[index])
        copy.start()
        going.append(copy)

    def conv_step(t, carry):
        for k in range(ns):
            cols = at(seq_at ^ k, span)
            w, m, v = adam_math(
                conv[t, :, cols],
                conv_m[0, t, :, cols],
                conv_m[1, t, :, cols],
                conv_grads[k][at(t, in_rows), :].astype(F32),
                clip,
                matrix_rate,
                weight_decay,
            )
            new_conv[t, :, cols] = w
            conv_first[t, :, cols] = m
            second[:, at(t * ns + (seq_at ^ k), span)] = v
        return carry

    lax.fori_loop(0, taps, conv_step, 0)
    send(0, new_conv, outs[0])
    send(1, conv_first, outs[1])
    send(2, second.at[:, : taps * width], outs[6].at[:, : taps * width])
    for k in range(ns):
        lanes = at(seq_at ^ k, quarter)
        w, m, v = adam_math(
            inner[:, lanes],
            inner_m[0, :, lanes],
            inner_m[1, :, lanes],
            ffn_grads[k][0:in_rows, :].astype(F32),
            clip,
            matrix_rate,
            weight_decay,
        )
        new_inner[:, lanes] = w
        inner_first[:, lanes] = m
        second[:, at(taps * width // quarter + (seq_at ^ k), quarter)] = v
    send(3, new_inner, outs[2])
    send(4, inner_first, outs[3])
    for k in range(ns):
        where = at(seq_at ^ k, part)
        w, m, v = adam_math(
            outer[where, :],
            outer_m[0, where, :],
            outer_m[1, where, :],
            ffn_grads[k][in_rows : in_rows + part, :].astype(F32),
            clip,
            matrix_rate,
            weight_decay,
        )
        new_outer[where, :] = w
        outer_first[where, :] = m
        for a in range(width // LANES):
            outer_second[a, where, :] = v[:, a * LANES : (a + 1) * LANES]
    send(5, new_outer, outs[4])
    send(6, outer_first, outs[5])
    ratio = out_rows // in_rows
    base = taps * width + hid
    for e in range(ratio):
        for a in range(width // LANES):
            begin = base + e * width + a * LANES
            second[:, begin : begin + LANES] = outer_second[a, pl.ds(e, in_rows, stride=ratio), :]
    w, m, v = adam_math(vec[...], vec_m[0], vec_m[1], vec_grad, clip, vector_rate, 0.0)
    new_vec[...] = w
    vec_first[...] = m
    v = jnp.concatenate([v, jnp.zeros((LANES - vec_count, width), F32)], axis=0)
    vec_second[...] = jnp.transpose(v)
    begin = base + ratio * width
    block = z_at * 2 + core_at
    second[:, begin : begin + vec_count] = vec_second[at(block, in_rows), :][:, 0:vec_count]
    send(7, second.at[:, taps * width :], outs[6].at[:, taps * width :])
    end_copies(going)


def per_device(
    tokens,
    cotangent,
    contig_lengths,
    conv_weight,
    inner_weight,
    outer_weight,
    vectors,
    conv_moments,
    inner_moments,
    outer_moments,
    vector_moments,
):
    ns = lax.axis_size("seq")
    nr = lax.axis_size("row")
    nz = nr // 2
    seq_at = lax.axis_index("seq")
    rows, length, width = tokens.shape
    taps, in_rows, _ = conv_weight.shape
    hid = inner_weight.shape[1]
    out_rows = outer_weight.shape[0]
    count = rows * length
    half = DILATION_STEP * (taps // 2)
    span = width // ns
    quarter = hid // ns
    part = out_rows // ns

    ffn_rows = in_rows + part
    vec_rows = VEC_PAD * width // LANES
    conv_rows = taps * in_rows
    cot = cotangent.reshape(count, width)

    def edge_rows(k):
        near = any(abs((i ^ k) - i) == 1 for i in range(ns))
        return rows * half * (width // LANES) if near else 0

    masks = [k for k in range(ns) if edge_rows(k)]
    far_masks = [k for k in masks if k > 1]
    rounded = vmem_call(
        functools.partial(round_kernel, ns, far_masks),
        [
            ((taps, in_rows, span), BF),
            (conv_weight.shape, BF),
            ((ns * ffn_rows, width), BF),
            ((ffn_rows, width), BF),
        ]
        + [((rows, half, width), BF)] * len(far_masks),
        [
            pltpu.VMEM(conv_weight.shape, F32),
            pltpu.VMEM(inner_weight.shape, F32),
            pltpu.VMEM(outer_weight.shape, F32),
            pltpu.SemaphoreType.DMA((3 + len(far_masks),)),
        ],
        far=range(4),
        slack=2,
    )(conv_weight, inner_weight, outer_weight, tokens)
    conv_part, conv_own, ffn_own, ffn_part = rounded[:4]
    got = [exchange(conv_part, "row", 2 * j) for j in range(1, nz)]
    edges = [exchange(rounded[4 + i], "seq", k) for i, k in enumerate(far_masks)]
    tokens_now = lax.optimization_barrier((tokens, got[0]))[0]
    token_pieces = [tokens] + [
        exchange(tokens_now, "seq", k) for k in range(1, ns) if k & (k - 1) == 0
    ]
    late = lax.optimization_barrier((got[0], *edges, *token_pieces[1:]))
    got[0], edges, token_pieces[1:] = late[0], late[1 : 1 + len(edges)], late[1 + len(edges) :]
    (got,) = vmem_call(
        functools.partial(stack_kernel, nz - 1), [((nz - 1, taps, in_rows, span), BF)], slack=2
    )(*got)
    conv_own, ffn_own = lax.optimization_barrier((conv_own, ffn_own, got))[:2]
    conv_other = exchange(conv_own, "row", 1)
    ffn_other = exchange(ffn_own, "row", 1)
    conv_pieces = [got] + [exchange(got, "seq", k) for k in range(1, ns)]
    conv_other_pieces = [exchange(got, "row", 1)]
    ffn_part, conv_other_pieces[0], conv_other, ffn_other = lax.optimization_barrier(
        (ffn_part, conv_other_pieces[0], conv_other, ffn_other)
    )
    ffn_got = [exchange(ffn_part, "row", 2 * j) for j in range(nz - 1, 0, -1)][::-1]
    late = lax.optimization_barrier((*ffn_got, *conv_pieces[1:]))
    ffn_got, conv_pieces[1:] = late[: nz - 1], late[nz - 1 :]
    conv_other_pieces += [exchange(p, "row", 1) for p in conv_pieces[1:]]
    ffn_got, vector_near = vmem_call(
        functools.partial(stack_kernel, nz - 1),
        [((nz - 1, ffn_rows, width), BF), (vector_moments.shape, F32)],
        slack=2,
    )(*ffn_got, vector_moments)
    ffn_pieces = [ffn_got] + [exchange(ffn_got, "seq", k) for k in range(1, ns)]

    pre, after, conv_full = vmem_call(
        functools.partial(conv_kernel, taps, nz, ns, masks),
        [((count, width), F32), ((count, width), F32), ((taps, nz, 2, in_rows, width), BF)],
        [
            pltpu.VMEM((length + 2 * half, width), F32),
            pltpu.VMEM((length + 2 * half, LANES), jnp.int32),
            pltpu.VMEM((count, taps * width), BF),
            pltpu.SemaphoreType.DMA((2 * (1 + ns * (nz - 1)),)),
        ],
        smem=1,
        loose=[i for i in range(3, 6 + len(far_masks) + 2 * ns) if not 5 <= i < 6 + len(far_masks)],
    )(
        contig_lengths,
        vectors,
        tokens,
        conv_own,
        conv_other,
        token_pieces[1],
        *edges,
        *conv_pieces,
        *conv_other_pieces,
    )

    tokens_late = lax.optimization_barrier((tokens, pre, *ffn_pieces))[0]
    near = [k for k in range(1, ns) if k & (k - 1) == 0]
    token_pieces = [tokens] + [
        token_pieces[1 + near.index(k)] if k in near else exchange(tokens_late, "seq", k)
        for k in range(1, ns)
    ]
    late = lax.optimization_barrier((pre, *ffn_pieces))
    pre, ffn_pieces = late[0], late[1:]
    ffn_other_pieces = [exchange(p, "row", 1) for p in ffn_pieces]

    layer_out, low, hidden, outer_grad, inner_grad, inner_full, vec_sums = vmem_call(
        functools.partial(ffn_kernel, nz, ns),
        [
            ((count, width), BF),
            ((count, width), BF),
            ((count, hid), BF),
            ((count, width), BF),
            ((count, hid), BF),
            ((nz, 2, in_rows, hid), BF),
            ((VEC_PAD, width), F32),
        ],
        [
            pltpu.VMEM((nz, 2, ns, part, width), BF),
            pltpu.VMEM((count, hid), F32),
            pltpu.VMEM((count, width), F32),
        ],
        kept=(0,),
    )(after, cot, vectors, ffn_own, ffn_other, *ffn_pieces, *ffn_other_pieces)

    mine, theirs = vmem_call(
        functools.partial(ffn_weight_kernel, nz, ns, in_rows, out_rows),
        [((ns, nz, ffn_rows, width), BF)] * 2,
        [pltpu.VMEM((hid, width), BF), pltpu.VMEM((width, hid), BF)],
    )(low, hidden, outer_grad, inner_grad)

    inner_grad, mine = lax.optimization_barrier((inner_grad, mine))
    results = vmem_call(
        functools.partial(back_kernel, ns, rows),
        [((count, width), F32), ((count, width), BF)]
        + [
            ((count + 2 * vec_rows + edge_rows(k), span), BF)
            for k in range(ns)
        ],
        [pltpu.VMEM((count, width), F32), pltpu.VMEM((VEC_PAD, width), F32)],
    )(pre, cot, vectors, inner_grad, inner_full, vec_sums)
    after_grad, conv_grad = results[:2]
    grad_pieces = list(results[2:])
    late = lax.optimization_barrier((theirs, *grad_pieces, *token_pieces))
    theirs, grad_pieces, token_pieces = late[0], list(late[1 : 1 + ns]), late[1 + ns :]
    arrived = exchange(theirs, "row", 1)
    grad_pieces = grad_pieces[:1] + [exchange(grad_pieces[k], "seq", k) for k in range(1, ns)]
    mine, grad_pieces[1] = lax.optimization_barrier((mine, grad_pieces[1]))
    flat = (ns * nz * ffn_rows, width)
    ffn_sums = split_sum([mine.reshape(flat), arrived.reshape(flat)], ns)
    ffn_sums = [ffn_sums[0]] + [exchange(ffn_sums[k], "seq", k) for k in range(1, ns)]

    mine, theirs = vmem_call(
        functools.partial(conv_weight_kernel, taps, nz, ns, in_rows),
        [((nz * conv_rows + 2 * vec_rows, span), BF)] * 2,
        [
            pltpu.VMEM((ns * length + 2 * half, span), F32),
            pltpu.VMEM((ns * length + 2 * half, LANES), jnp.int32),
            pltpu.VMEM((ns * count, taps * span), BF),
            pltpu.VMEM((width, taps * span), F32),
            pltpu.VMEM((ns, rows, length, width), BF),
            pltpu.SemaphoreType.DMA((ns,)),
        ],
        smem=1,
        loose=range(1, 1 + ns),
    )(contig_lengths, *token_pieces, *grad_pieces)
    arrived = exchange(theirs, "row", 1)
    sums = vmem_call(
        functools.partial(conv_core_kernel, conv_rows),
        [((conv_rows + 2 * vec_rows, span), BF)] * nz,
        slack=2,
    )(mine, arrived)
    sums = [sums[0]] + [exchange(sums[j], "row", 2 * j) for j in range(1, nz)]

    masks = [k for k in range(ns) if edge_rows(k)]
    (input_grad,) = vmem_call(
        functools.partial(input_grad_kernel, taps, ns, rows, masks),
        [((count, width), F32)],
        [
            pltpu.VMEM((length + 2 * half, width), F32),
            pltpu.VMEM((length + 2 * half, LANES), jnp.int32),
            pltpu.VMEM((taps, count, width), BF),
        ],
        smem=1,
        kept=(0,),
    )(contig_lengths, conv_grad, after_grad, conv_full, *[grad_pieces[k] for k in masks])
    sums[0], input_grad = lax.optimization_barrier((sums[0], input_grad))

    conv_sum, conv_square, vec_sum = vmem_call(
        functools.partial(conv_final_kernel, nz, vec_rows),
        [((conv_rows, span), BF), ((8, LANES), F32), ((VEC_PAD, width), F32)],
        slack=2,
    )(*sums)
    conv_sums = [conv_sum] + [exchange(conv_sum, "seq", k) for k in range(1, ns)]

    ffn_sums = split_sum(ffn_sums, nz)
    ffn_sums = [ffn_sums[0]] + [exchange(ffn_sums[j], "row", 2 * j) for j in range(1, nz)]
    ffn_sums[0], conv_sums[-1] = lax.optimization_barrier((ffn_sums[0], conv_sums[-1]))
    (ffn_sum,) = vmem_call(
        functools.partial(ffn_final_kernel, nz), [((ffn_rows + VEC_PAD, width), BF)], slack=2
    )(*ffn_sums, conv_square)
    ffn_sums = [ffn_sum] + [exchange(ffn_sum, "seq", k) for k in range(1, ns)]
    (square,) = vmem_call(
        functools.partial(square_kernel, ns), [((8, LANES), F32)], slack=2
    )(*ffn_sums)
    squares = [square] + [exchange(square, "row", 2 * j) for j in range(1, nz)]
    (square,) = vmem_call(small_sum_kernel, [((8, LANES), F32)], slack=2)(*squares)
    squares = [square, exchange(square, "row", 1)]

    second_width = taps * width + hid + (out_rows // in_rows) * width + vectors.shape[0]
    results = [
        (conv_weight.shape, F32),
        (conv_weight.shape, F32),
        (inner_weight.shape, F32),
        (inner_weight.shape, F32),
        (outer_weight.shape, F32),
        (outer_weight.shape, F32),
        ((in_rows, second_width), F32),
    ]
    (
        norm,
        new_vectors,
        vector_first,
        new_conv,
        conv_first,
        new_inner,
        inner_first,
        new_outer,
        outer_first,
        second_moments,
    ) = vmem_call(
        functools.partial(adam_kernel, taps, ns),
        [((1, 1), F32), (vectors.shape, F32), (vectors.shape, F32), *results],
        [pltpu.VMEM(shape, dtype) for shape, dtype in results]
        + [
            pltpu.VMEM((width // LANES, out_rows, LANES), F32),
            pltpu.VMEM((width, LANES), F32),
            pltpu.SemaphoreType.DMA((8,)),
        ],
        kept=range(3),
        left=range(3, 10),
        slack=3,
    )(
        *conv_sums,
        *ffn_sums,
        vec_sum,
        *squares,
        conv_weight,
        inner_weight,
        outer_weight,
        vectors,
        conv_moments,
        inner_moments,
        outer_moments,
        vector_near,
    )
    return (
        layer_out.reshape(tokens.shape),
        input_grad.reshape(tokens.shape),
        norm.reshape(()),
        new_conv,
        conv_first,
        new_inner,
        inner_first,
        new_outer,
        outer_first,
        new_vectors,
        vector_first,
        second_moments,
    )


def solution(mesh):
    in_specs = (
        P("row", "seq", None),
        P("row", "seq", None),
        P("row", None),
        P(None, "row", None),
        P("row", None),
        P("row", None),
        P(),
        P(None, None, "row", None),
        P(None, "row", None),
        P(None, "row", None),
        P(),
    )
    out_specs = (
        P("row", "seq", None),
        P("row", "seq", None),
        P(),
        P(None, "row", None),
        P(None, "row", None),
        P("row", None),
        P("row", None),
        P("row", None),
        P("row", None),
        P(),
        P(),
        P("row", None),
    )
    return jax.shard_map(
        per_device, mesh=mesh, in_specs=in_specs, out_specs=out_specs, check_vma=False
    )
```

```python
import functools

import jax
import jax.numpy as jnp
from jax import lax
from jax.experimental import pallas as pl
from jax.experimental.pallas import tpu as pltpu
from jax.sharding import PartitionSpec as P

DILATION_STEP = 8

beta_one = 0.9
beta_two = 0.999
adam_eps = 1e-08
weight_decay = 0.1
matrix_rate = 0.03
vector_rate = 0.3
clip_level = 1.0
step_count = 10
norm_eps = 1e-05

F32 = jnp.float32
BF = jnp.bfloat16
VEC_PAD = 16
LANES = 128
SQRT_HALF = 0.7071067811865476
PDF_SCALE = 0.3989422804014327


def exchange(value, axis, mask):
    size = lax.axis_size(axis)
    return lax.ppermute(value, axis, [(i, i ^ mask) for i in range(size)])


def shift_along(value, axis, step):
    size = lax.axis_size(axis)
    pairs = [(i, i + step) for i in range(size) if 0 <= i + step < size]
    return lax.ppermute(value, axis, pairs)


def gelu_parts(v):
    cdf = 0.5 + 0.5 * lax.erf(v * SQRT_HALF)
    return v * cdf, cdf


def gelu_slope(v, cdf):
    return cdf + v * (jnp.exp(-0.5 * v * v) * PDF_SCALE)


def mean_of(v):
    return jnp.mean(v, axis=-1, keepdims=True)


def normalized(v):
    centred = v - mean_of(v)
    scale = lax.rsqrt(mean_of(centred * centred) + norm_eps)
    return centred * scale, scale


def fold_rows(v):
    rows, cols = v.shape
    return jnp.sum(v.reshape(rows // 8, 8, cols), axis=0)


def column_sum(acc):
    return jnp.sum(acc, axis=0, keepdims=True)


def loop_rows(total, step, body, init=0):
    return lax.fori_loop(
        0, total // step, lambda i, carry: body(pl.multiple_of(i * step, step), carry), init
    )


def dot(a, b):
    return jnp.dot(a, b, preferred_element_type=F32)


def dot_nt(a, b):
    return lax.dot_general(a, b, (((1,), (1,)), ((), ())), preferred_element_type=F32)


def dot_tn(a, b):
    return lax.dot_general(a, b, (((0,), (0,)), ((), ())), preferred_element_type=F32)


def place():
    seq_at = lax.axis_index("seq")
    row_at = lax.axis_index("row")
    return seq_at, row_at // 2, row_at % 2


def at(index, step):
    return pl.ds(pl.multiple_of(index * step, step), step)


def size_of(shape, dtype):
    total = jnp.dtype(dtype).itemsize
    for n in shape:
        total *= n
    return total


def vmem_call(kernel, outs, scratch=(), smem=0, loose=(), far=(), kept=(), left=(), slack=6):
    space = pl.BlockSpec(memory_space=pltpu.VMEM)
    anywhere = pl.BlockSpec(memory_space=pl.ANY)
    grant = slack * 1024 * 1024
    grant += sum(size_of(v.shape, v.dtype) for v in scratch if hasattr(v, "shape") and v.dtype in (F32, BF, jnp.int32))
    grant += sum(size_of(*outs[i]) for i in kept)

    def call(*args):
        fixed = [
            a
            if i < smem or i in loose
            else pltpu.with_memory_space_constraint(a, pltpu.HBM if i in far else pltpu.VMEM)
            for i, a in enumerate(args)
        ]
        return pl.pallas_call(
            kernel,
            out_shape=[
                jax.ShapeDtypeStruct(shape, dtype) if i in kept or i in left else pltpu.VMEM(shape, dtype)
                for i, (shape, dtype) in enumerate(outs)
            ],
            in_specs=[
                pl.BlockSpec(memory_space=pltpu.SMEM)
                if i < smem
                else pl.BlockSpec(memory_space=pltpu.HBM)
                if i in far
                else anywhere
                if i in loose
                else space
                for i in range(len(args))
            ],
            out_specs=[anywhere if i in left else space for i in range(len(outs))],
            scratch_shapes=list(scratch),
            cost_estimate=pl.CostEstimate(flops=1, bytes_accessed=1, transcendentals=0),
            compiler_params=pltpu.CompilerParams(vmem_limit_bytes=grant),
        )(*fixed)

    return call


def begin_copies(pairs, sems):
    copies = [pltpu.make_async_copy(src, dst, sems.at[i]) for i, (src, dst) in enumerate(pairs)]
    for copy in copies:
        copy.start()
    return copies


def end_copies(copies):
    for copy in copies:
        copy.wait()


def contigs(lens_ref, row, positions, row_length):
    found = jnp.zeros(positions.shape, jnp.int32)
    start = jnp.int32(0)
    for j in range(lens_ref.shape[1] - 1):
        start = start + lens_ref[row, j]
        found = found + (positions >= start).astype(jnp.int32)
    found = jnp.where(positions < 0, -1, found)
    return jnp.where(positions >= row_length, lens_ref.shape[1], found)


def masked_taps(src, cid, length, taps, half, store):
    centre = cid[pl.ds(half, length), :]

    def body(tap, carry):
        begin = pl.multiple_of(tap * DILATION_STEP, DILATION_STEP)
        keep = cid[pl.ds(begin, length), :] == centre
        for a in range(src.shape[1] // LANES):
            part = src[pl.ds(begin, length), a * LANES : (a + 1) * LANES]
            store(tap, a, jnp.where(keep, part, 0.0).astype(BF))
        return carry

    lax.fori_loop(0, taps, body, 0)


def round_kernel(ns, masks, conv_far, inner_far, outer_far, tok_far, *refs):
    conv_part, conv_own, ffn_own, ffn_part = refs[:4]
    edges = refs[4 : 4 + len(masks)]
    conv, inner, outer, sems = refs[4 + len(masks) :]
    seq_at = lax.axis_index("seq")
    pairs = [(conv_far, conv), (inner_far, inner), (outer_far, outer)]
    for mask, edge in zip(masks, edges):
        half = edge.shape[1]
        last = jnp.where((seq_at ^ mask) > seq_at, tok_far.shape[1] // half - 1, 0)
        pairs.append((tok_far.at[:, at(last, half)], edge))
    copies = begin_copies(pairs, sems)
    in_rows, hid = inner.shape
    quarter = hid // ns
    part = outer.shape[0] // ns
    span = conv.shape[2] // ns
    copies[0].wait()
    for t in range(conv.shape[0]):
        conv_own[t] = conv[t].astype(BF)
        conv_part[t] = conv[t, :, at(seq_at, span)].astype(BF)
    end_copies(copies[1:])
    for k in range(ns):
        ffn_own[k * in_rows : (k + 1) * in_rows, :] = inner[
            :, k * quarter : (k + 1) * quarter
        ].astype(BF)
    ffn_own[ns * in_rows :, :] = outer[...].astype(BF)
    ffn_part[:in_rows, :] = inner[:, at(seq_at, quarter)].astype(BF)
    ffn_part[in_rows:, :] = outer[at(seq_at, part), :].astype(BF)


def stack_kernel(count, *refs):
    ins, rest = refs[:count], refs[count:]
    out = rest[len(rest) // 2]
    for i, ref in enumerate(ins):
        out[i] = ref[...]
    if len(rest) > 1:
        rest[2][...] = rest[0][...]


def conv_kernel(taps, nz, ns, masks, lens, vec, tok, own, other, *rest):
    edges, rest = rest[: len(masks)], rest[len(masks) :]
    pieces = (rest[:ns], rest[ns : 2 * ns])
    pre, after, full, ext, cid, cat, sems = rest[2 * ns :]
    seq_at, z_at, core_at = place()
    rows, length, width = tok.shape
    quarter = width // ns
    half = DILATION_STEP * (taps // 2)
    pairs = []
    for i, whole in enumerate((own, other)):
        core = core_at ^ i
        pairs.append((whole, full.at[:, z_at, core]))
        for k in range(ns):
            for j in range(1, nz):
                cols = at(seq_at ^ k, quarter)
                pairs.append((pieces[i][k].at[j - 1], full.at[:, z_at ^ j, core, :, cols]))
    copies = begin_copies(pairs, sems)
    span = length + 2 * half
    base = seq_at * length - half
    positions = base + lax.broadcasted_iota(jnp.int32, (span, LANES), 0)
    ext[0:half, :] = jnp.zeros((half, width), F32)
    ext[half + length :, :] = jnp.zeros((half, width), F32)
    for r in range(rows):
        ext[half : half + length, :] = tok[r].astype(F32)
        for mask, edge in zip(masks, edges):
            for step, to, begin in ((-1, 0, edge.shape[1] - half), (1, half + length, 0)):

                @pl.when((seq_at ^ mask) == seq_at + step)
                def _(r=r, edge=edge, to=to, begin=begin):
                    ext[to : to + half, :] = edge[r, begin : begin + half, :].astype(F32)

        cid[...] = contigs(lens, r, positions, length * ns)

        def store(tap, a, value, r=r):
            cat[r * length : (r + 1) * length, at(tap * (width // LANES) + a, LANES)] = value

        masked_taps(ext, cid, length, taps, half, store)
    end_copies(copies)
    weights = full.reshape(taps * width, width)

    def product(r, carry):
        where = at(r, length)
        pre[where, :] = dot(cat[where, :], weights[...]) + vec[0:1, :]
        return carry

    lax.fori_loop(0, rows, product, 0)

    for r in range(rows):

        def norm(begin, carry, r=r):
            where = pl.ds(r * length + begin, 256)
            active, _ = gelu_parts(pre[where, :])
            unit, _ = normalized(active)
            after[where, :] = (
                tok[r, pl.ds(begin, 256), :].astype(F32) + unit * vec[1:2, :] + vec[2:3, :]
            )
            return carry

        loop_rows(length, 256, norm)


def ffn_kernel(nz, ns, *refs):
    after, cot, vec = refs[:3]
    wholes = refs[3:5]
    pieces = (refs[5 : 5 + ns], refs[5 + ns : 5 + 2 * ns])
    rest = refs[5 + 2 * ns :]
    layer, low, hidden, outer_grad, inner_grad, inner_full, sums, outer_full, slope, tmp = rest
    seq_at, z_at, core_at = place()
    count, width = after.shape
    hid = inner_full.shape[3]
    in_rows = inner_full.shape[2]
    quarter = hid // ns
    blocks = hid // width
    inner = inner_full.reshape(width, hid)
    outer = outer_full.reshape(hid, width)
    part = outer_full.shape[3]
    for i, whole in enumerate(wholes):
        core = core_at ^ i
        for q in range(ns):
            inner_full[z_at, core, :, q * quarter : (q + 1) * quarter] = whole[
                q * in_rows : (q + 1) * in_rows
            ]
            begin = ns * in_rows + q * part
            outer_full[z_at, core, q] = whole[begin : begin + part]
        for k in range(ns):
            piece = pieces[i][k]
            q = seq_at ^ k
            for j in range(1, nz):
                z = z_at ^ j
                inner_full[z, core, :, at(q, quarter)] = piece[j - 1, :in_rows]
                outer_full[z, core, q] = piece[j - 1, in_rows:]

    def lower(begin, carry):
        where = pl.ds(begin, 64)
        low[where, :] = after[where, :].astype(BF)
        return carry

    loop_rows(count, 64, lower)

    def up(b, carry):
        cols = at(b, width)
        tmp[...] = dot(low[...], inner[:, cols]) + vec[pl.ds(6 + b, 1), :]

        def act(begin, inside):
            where = pl.ds(begin, 128)
            v = tmp[where, :]
            active, cdf = gelu_parts(v)
            hidden[where, cols] = active.astype(BF)
            slope[where, cols] = gelu_slope(v, cdf)
            return inside

        loop_rows(count, 128, act)
        return carry

    lax.fori_loop(0, blocks, up, 0)
    tmp[...] = dot(hidden[...], outer[...]) + vec[3:4, :]
    zero = jnp.zeros((8, width), F32)

    def second(begin, carry):
        bias_sum, gain_sum, shift_sum = carry
        where = pl.ds(begin, 256)
        unit, scale = normalized(tmp[where, :])
        gain = vec[4:5, :]
        layer[where, :] = (after[where, :] + unit * gain + vec[5:6, :]).astype(BF)
        dy = cot[where, :].astype(F32)
        u = dy * gain
        grad = (scale * (u - mean_of(u) - unit * mean_of(u * unit))).astype(BF)
        outer_grad[where, :] = grad
        return (
            bias_sum + fold_rows(grad.astype(F32)),
            gain_sum + fold_rows(dy * unit),
            shift_sum + fold_rows(dy),
        )

    totals = loop_rows(count, 256, second, (zero, zero, zero))
    sums[...] = jnp.zeros(sums.shape, F32)
    for i, total in enumerate(totals):
        sums[3 + i : 4 + i, :] = column_sum(total)

    def down(b, carry):
        cols = at(b, width)
        tmp[...] = dot_nt(outer_grad[...], outer[cols, :])

        def act(begin, total):
            where = pl.ds(begin, 128)
            grad = (tmp[where, :] * slope[where, cols]).astype(BF)
            inner_grad[where, cols] = grad
            return total + fold_rows(grad.astype(F32))

        total = loop_rows(count, 128, act, zero)
        sums[pl.ds(6 + b, 1), :] = column_sum(total)
        return carry

    lax.fori_loop(0, blocks, down, 0)


def back_kernel(ns, rows, *refs):
    pre, cot, vec, inner_grad, inner_full, partial_sums, after_grad, conv_grad = refs[:8]
    inner = inner_full.reshape(pre.shape[1], inner_grad.shape[1])
    sends = refs[8 : 8 + ns]
    tmp, sums = refs[8 + ns :]
    seq_at = lax.axis_index("seq")
    count, width = pre.shape
    zero = jnp.zeros((8, width), F32)
    sums[...] = partial_sums[...]
    tmp[...] = dot_nt(inner_grad[...], inner[...])

    def first(begin, carry):
        bias_sum, gain_sum, shift_sum = carry
        where = pl.ds(begin, 256)
        upstream = cot[where, :].astype(F32) + tmp[where, :]
        after_grad[where, :] = upstream
        v = pre[where, :]
        active, cdf = gelu_parts(v)
        unit, scale = normalized(active)
        u = upstream * vec[1:2, :]
        grad = scale * (u - mean_of(u) - unit * mean_of(u * unit))
        grad = (grad * gelu_slope(v, cdf)).astype(BF)
        conv_grad[where, :] = grad
        return (
            bias_sum + fold_rows(grad.astype(F32)),
            gain_sum + fold_rows(upstream * unit),
            shift_sum + fold_rows(upstream),
        )

    totals = loop_rows(count, 256, first, (zero, zero, zero))
    for i, total in enumerate(totals):
        sums[i : i + 1, :] = column_sum(total)
    span = width // ns
    for k in range(ns):
        sends[k][0:count, :] = conv_grad[:, at(seq_at ^ k, span)]
        encode(sends[k], count, spread(sums[...]))
        begin = count + 2 * VEC_PAD * width // LANES
        if sends[k].shape[0] > begin:
            half = (sends[k].shape[0] - begin) // rows // (width // LANES)
            length = count // rows
            first = jnp.where((seq_at ^ k) > seq_at, length - half, 0)
            for r in range(rows):
                for a in range(width // LANES):
                    sends[k][begin : begin + half, :] = conv_grad[
                        at(r * (length // half) + first // half, half), a * LANES : (a + 1) * LANES
                    ]
                    begin += half


def spread(v):
    return jnp.concatenate(
        [v[:, a * LANES : (a + 1) * LANES] for a in range(v.shape[1] // LANES)], axis=0
    )


def gathered(v):
    return jnp.concatenate(
        [v[a * VEC_PAD : (a + 1) * VEC_PAD, :] for a in range(v.shape[0] // VEC_PAD)], axis=1
    )


def encode(ref, begin, v):
    rows = v.shape[0]
    high = v.astype(BF)
    ref[begin : begin + rows, :] = high
    ref[begin + rows : begin + 2 * rows, :] = (v - high.astype(F32)).astype(BF)


def decode(ref, begin, rows):
    high = ref[begin : begin + rows, :].astype(F32)
    return high + ref[begin + rows : begin + 2 * rows, :].astype(F32)


def tree_sum(values):
    values = list(values)
    while len(values) > 1:
        values = [values[i] + values[i + 1] for i in range(0, len(values), 2)]
    return values[0]


def ffn_weight_kernel(nz, ns, in_rows, out_rows, *refs):
    low, hidden, outer_grad, inner_grad, mine, theirs, outer_sum, inner_sum = refs
    seq_at, z_at, core_at = place()
    width = low.shape[1]
    hid = hidden.shape[1]
    part = out_rows // ns
    quarter = hid // ns

    def product(b, carry):
        cols = at(b, width)
        outer_sum[cols, :] = dot_tn(hidden[:, cols], outer_grad[...]).astype(BF)
        inner_sum[:, cols] = dot_tn(low[...], inner_grad[:, cols]).astype(BF)
        return carry

    lax.fori_loop(0, hid // width, product, 0)
    for i, out in enumerate((mine, theirs)):
        for k in range(ns):
            for j in range(nz):
                block = (z_at ^ j) * 2 + (core_at ^ i)
                out[k, j, :in_rows] = inner_sum[at(block, in_rows), at(seq_at ^ k, quarter)]
                out[k, j, in_rows:] = outer_sum[at(block * ns + (seq_at ^ k), part), :]


def conv_weight_kernel(taps, nz, ns, in_rows, *refs):
    lens = refs[0]
    far = refs[1 : 1 + ns]
    grads = refs[1 + ns : 1 + 2 * ns]
    mine, theirs, padded, cid, cat, total, toks, sems = refs[1 + 2 * ns :]
    copies = begin_copies([(far[k], toks.at[k]) for k in range(ns)], sems)
    seq_at, z_at, core_at = place()
    _, rows, length, width = toks.shape
    span = width // ns
    half = DILATION_STEP * (taps // 2)
    row_length = ns * length
    count = rows * length
    positions = lax.broadcasted_iota(jnp.int32, (row_length + 2 * half, LANES), 0) - half
    edge = jnp.zeros((half, span), F32)
    for r in range(rows):
        padded[0:half, :] = edge
        padded[half + row_length :, :] = edge
        cid[...] = contigs(lens, r, positions, row_length)
        for k in range(ns):
            padded[pl.ds(half + (seq_at ^ k) * length, length), :] = grads[k][
                r * length : (r + 1) * length, :
            ].astype(F32)
        for k in range(ns):
            base = (seq_at ^ k) * length
            centre = cid[pl.ds(pl.multiple_of(base + half, 8), length), :]
            for t in range(taps):
                begin = pl.multiple_of(base + DILATION_STEP * (taps - 1 - t), 8)
                keep = cid[pl.ds(begin, length), :] == centre
                value = jnp.where(keep, padded[pl.ds(begin, length), :], 0.0)
                low_row = k * count + r * length
                cat[low_row : low_row + length, t * span : (t + 1) * span] = value.astype(BF)
    end_copies(copies)
    for k in range(ns):
        value = tree_sum(
            [
                dot_tn(toks[k, r], cat[k * count + r * length : k * count + (r + 1) * length, :])
                for r in range(rows)
            ]
        )
        if k == 0:
            total[...] = value
        else:
            total[...] += value
    for i, out in enumerate((mine, theirs)):
        for j in range(nz):
            block = (z_at ^ j) * 2 + (core_at ^ i)
            for t in range(taps):
                begin = (j * taps + t) * in_rows
                out[begin : begin + in_rows, :] = total[
                    at(block, in_rows), t * span : (t + 1) * span
                ].astype(BF)
    vec_rows = VEC_PAD * width // LANES
    summed = tree_sum([decode(g, count, vec_rows) for g in grads])
    for out in (mine, theirs):
        encode(out, nz * taps * in_rows, summed)


def input_grad_kernel(taps, ns, rows, masks, *refs):
    lens, grad, after_grad, full_blocks = refs[:4]
    pieces = refs[4 : 4 + len(masks)]
    out, ext, cid, cat = refs[4 + len(masks) :]
    full = full_blocks.reshape(taps, grad.shape[1], grad.shape[1])
    seq_at = lax.axis_index("seq")
    half = DILATION_STEP * (taps // 2)
    width = grad.shape[1]
    length = grad.shape[0] // rows
    base = seq_at * length - half
    positions = base + lax.broadcasted_iota(jnp.int32, (length + 2 * half, LANES), 0)
    ext[0:half, :] = jnp.zeros((half, width), F32)
    ext[half + length :, :] = jnp.zeros((half, width), F32)
    for r in range(rows):
        ext[half : half + length, :] = grad[r * length : (r + 1) * length, :].astype(F32)
        for mask, piece in zip(masks, pieces):
            for step, begin in ((-1, 0), (1, half + length)):

                @pl.when((seq_at ^ mask) == seq_at + step)
                def _(r=r, piece=piece, begin=begin):
                    first = piece.shape[0] - rows * half * (width // LANES)
                    for a in range(width // LANES):
                        low = first + (r * (width // LANES) + a) * half
                        ext[begin : begin + half, a * LANES : (a + 1) * LANES] = piece[
                            low : low + half, :
                        ].astype(F32)

        cid[...] = contigs(lens, r, positions, length * ns)

        def store(tap, a, value, r=r):
            flipped = taps - 1 - tap
            cat[
                flipped, r * length : (r + 1) * length, a * LANES : (a + 1) * LANES
            ] = value

        masked_taps(ext, cid, length, taps, half, store)

    out[...] = after_grad[...]

    def product(t, carry):
        out[...] += dot_nt(cat[t], full[t])
        return carry

    lax.fori_loop(0, taps, product, 0)


def split_sum_kernel(count, *refs):
    ins, outs = refs[:count], refs[count:]
    rows = outs[0].shape[0]
    for p, out in enumerate(outs):

        def body(begin, carry, p=p, out=out):
            where = pl.ds(p * rows + begin, 64)
            out[pl.ds(begin, 64), :] = tree_sum([v[where, :].astype(F32) for v in ins]).astype(BF)
            return carry

        loop_rows(rows, 64, body)


def split_sum(ins, parts):
    rows, cols = ins[0].shape
    return vmem_call(
        functools.partial(split_sum_kernel, len(ins)),
        [((rows // parts, cols), BF)] * parts,
        slack=2,
    )(*ins)


def conv_core_kernel(rows, mine, got, *outs):
    vec_rows = (mine.shape[0] - rows * len(outs)) // 2
    begin_vec = rows * len(outs)
    summed = decode(mine, begin_vec, vec_rows) + decode(got, begin_vec, vec_rows)
    for p, out in enumerate(outs):

        def body(begin, carry, p=p, out=out):
            where = pl.ds(p * rows + begin, 64)
            out[pl.ds(begin, 64), :] = (mine[where, :].astype(F32) + got[where, :].astype(F32)).astype(
                BF
            )
            return carry

        loop_rows(rows, 64, body)
        encode(out, rows, summed)


def conv_final_kernel(count, vec_rows, *refs):
    ins, (out, square, vec_sum) = refs[:count], refs[count:]
    square[...] = summed_square(ins, out)
    vec_sum[...] = gathered(tree_sum([decode(v, out.shape[0], vec_rows) for v in ins]))


def summed_square(ins, out):
    def body(begin, carry):
        where = pl.ds(begin, 64)
        value = tree_sum([v[where, :].astype(F32) for v in ins]).astype(BF)
        out[where, :] = value
        wide = value.astype(F32)
        return carry + lane_fold(fold_rows(wide * wide))

    rows = ins[0].shape[0] // 64 * 64 if out.shape[0] % 64 else out.shape[0]
    return loop_rows(min(rows, out.shape[0]), 64, body, jnp.zeros((8, LANES), F32))


def lane_fold(v):
    return sum(v[:, a * LANES : (a + 1) * LANES] for a in range(v.shape[1] // LANES))


def ffn_final_kernel(count, *refs):
    ins, (conv_square, out) = refs[:count], refs[count:]
    rows = ins[0].shape[0]
    square = summed_square(ins, out.at[0:rows]) + conv_square[...]
    high = square.astype(BF)
    low = (square - high.astype(F32)).astype(BF)
    zero = jnp.zeros(high.shape, BF)
    tail = jnp.concatenate([high, low] + [zero] * (out.shape[1] // LANES - 2), axis=1)
    out[rows : rows + VEC_PAD, :] = jnp.concatenate([tail, jnp.zeros(tail.shape, BF)], axis=0)


def square_kernel(count, *refs):
    ins, out = refs[:count], refs[count]
    rows = ins[0].shape[0] - VEC_PAD
    parts = []
    for v in ins:
        tail = v[rows : rows + VEC_PAD, :].astype(F32)
        parts.append(tail[:8, :LANES] + tail[:8, LANES : 2 * LANES])
    out[...] = tree_sum(parts)


def small_sum_kernel(*refs):
    refs[-1][...] = tree_sum([v[...] for v in refs[:-1]])


def adam_math(weight, first, second, gradient, clip, rate, decay):
    clipped = gradient * clip
    first = beta_one * first + (1.0 - beta_one) * clipped
    second = beta_two * second + (1.0 - beta_two) * clipped * clipped
    first_hat = first * (1.0 / (1.0 - beta_one**step_count))
    second_hat = second * (1.0 / (1.0 - beta_two**step_count))
    weight = weight - rate * (first_hat / (jnp.sqrt(second_hat) + adam_eps) + decay * weight)
    return weight, first, second


def adam_kernel(taps, ns, *refs):
    conv_grads = refs[:ns]
    ffn_grads = refs[ns : 2 * ns]
    vec_sum, one, two, conv, inner, outer, vec, conv_m, inner_m, outer_m, vec_m = refs[
        2 * ns : 2 * ns + 11
    ]
    norm, new_vec, vec_first = refs[2 * ns + 11 : 2 * ns + 14]
    outs = refs[2 * ns + 14 : 2 * ns + 21]
    new_conv, conv_first, new_inner, inner_first, new_outer, outer_first, second = refs[
        2 * ns + 21 : 2 * ns + 28
    ]
    outer_second, vec_second, sems = refs[2 * ns + 28 :]
    seq_at, z_at, core_at = place()
    in_rows, width = conv.shape[1:]
    hid = inner.shape[1]
    out_rows = outer.shape[0]
    span = width // ns
    quarter = hid // ns
    part = out_rows // ns
    vec_count = vec.shape[0]
    vec_grad = vec_sum[0:vec_count, :]
    total = jnp.sum(one[...] + two[...]) + jnp.sum(vec_grad * vec_grad)
    value = jnp.sqrt(jnp.full((1, 1), total, F32))
    norm[...] = value
    clip = clip_level / jnp.maximum(value, clip_level)
    going = []

    def send(index, src, dst):
        copy = pltpu.make_async_copy(src, dst, sems.at[index])
        copy.start()
        going.append(copy)

    def conv_step(t, carry):
        for k in range(ns):
            cols = at(seq_at ^ k, span)
            w, m, v = adam_math(
                conv[t, :, cols],
                conv_m[0, t, :, cols],
                conv_m[1, t, :, cols],
                conv_grads[k][at(t, in_rows), :].astype(F32),
                clip,
                matrix_rate,
                weight_decay,
            )
            new_conv[t, :, cols] = w
            conv_first[t, :, cols] = m
            second[:, at(t * ns + (seq_at ^ k), span)] = v
        return carry

    lax.fori_loop(0, taps, conv_step, 0)
    send(0, new_conv, outs[0])
    send(1, conv_first, outs[1])
    send(2, second.at[:, : taps * width], outs[6].at[:, : taps * width])
    for k in range(ns):
        lanes = at(seq_at ^ k, quarter)
        w, m, v = adam_math(
            inner[:, lanes],
            inner_m[0, :, lanes],
            inner_m[1, :, lanes],
            ffn_grads[k][0:in_rows, :].astype(F32),
            clip,
            matrix_rate,
            weight_decay,
        )
        new_inner[:, lanes] = w
        inner_first[:, lanes] = m
        second[:, at(taps * width // quarter + (seq_at ^ k), quarter)] = v
    send(3, new_inner, outs[2])
    send(4, inner_first, outs[3])
    for k in range(ns):
        where = at(seq_at ^ k, part)
        w, m, v = adam_math(
            outer[where, :],
            outer_m[0, where, :],
            outer_m[1, where, :],
            ffn_grads[k][in_rows : in_rows + part, :].astype(F32),
            clip,
            matrix_rate,
            weight_decay,
        )
        new_outer[where, :] = w
        outer_first[where, :] = m
        for a in range(width // LANES):
            outer_second[a, where, :] = v[:, a * LANES : (a + 1) * LANES]
    send(5, new_outer, outs[4])
    send(6, outer_first, outs[5])
    ratio = out_rows // in_rows
    base = taps * width + hid
    for e in range(ratio):
        for a in range(width // LANES):
            begin = base + e * width + a * LANES
            second[:, begin : begin + LANES] = outer_second[a, pl.ds(e, in_rows, stride=ratio), :]
    w, m, v = adam_math(vec[...], vec_m[0], vec_m[1], vec_grad, clip, vector_rate, 0.0)
    new_vec[...] = w
    vec_first[...] = m
    v = jnp.concatenate([v, jnp.zeros((LANES - vec_count, width), F32)], axis=0)
    vec_second[...] = jnp.transpose(v)
    begin = base + ratio * width
    block = z_at * 2 + core_at
    second[:, begin : begin + vec_count] = vec_second[at(block, in_rows), :][:, 0:vec_count]
    send(7, second.at[:, taps * width :], outs[6].at[:, taps * width :])
    end_copies(going)


def per_device(
    tokens,
    cotangent,
    contig_lengths,
    conv_weight,
    inner_weight,
    outer_weight,
    vectors,
    conv_moments,
    inner_moments,
    outer_moments,
    vector_moments,
):
    ns = lax.axis_size("seq")
    nr = lax.axis_size("row")
    nz = nr // 2
    seq_at = lax.axis_index("seq")
    rows, length, width = tokens.shape
    taps, in_rows, _ = conv_weight.shape
    hid = inner_weight.shape[1]
    out_rows = outer_weight.shape[0]
    count = rows * length
    half = DILATION_STEP * (taps // 2)
    span = width // ns
    quarter = hid // ns
    part = out_rows // ns

    ffn_rows = in_rows + part
    vec_rows = VEC_PAD * width // LANES
    conv_rows = taps * in_rows
    cot = cotangent.reshape(count, width)

    def edge_rows(k):
        near = any(abs((i ^ k) - i) == 1 for i in range(ns))
        return rows * half * (width // LANES) if near else 0

    masks = [k for k in range(ns) if edge_rows(k)]
    far_masks = [k for k in masks if k > 1]
    rounded = vmem_call(
        functools.partial(round_kernel, ns, far_masks),
        [
            ((taps, in_rows, span), BF),
            (conv_weight.shape, BF),
            ((ns * ffn_rows, width), BF),
            ((ffn_rows, width), BF),
        ]
        + [((rows, half, width), BF)] * len(far_masks),
        [
            pltpu.VMEM(conv_weight.shape, F32),
            pltpu.VMEM(inner_weight.shape, F32),
            pltpu.VMEM(outer_weight.shape, F32),
            pltpu.SemaphoreType.DMA((3 + len(far_masks),)),
        ],
        far=range(4),
        slack=2,
    )(conv_weight, inner_weight, outer_weight, tokens)
    conv_part, conv_own, ffn_own, ffn_part = rounded[:4]
    got = [exchange(conv_part, "row", 2 * j) for j in range(1, nz)]
    edges = [
        exchange(lax.optimization_barrier((rounded[4 + i], got[0]))[0], "seq", k)
        for i, k in enumerate(far_masks)
    ]
    tokens_now = lax.optimization_barrier((tokens, conv_part))[0]
    token_pieces = [tokens] + [
        exchange(tokens_now, "seq", k) for k in range(1, ns) if k & (k - 1) == 0
    ]
    late = lax.optimization_barrier((got[0], *edges, *token_pieces[1:]))
    got[0], edges, token_pieces[1:] = late[0], late[1 : 1 + len(edges)], late[1 + len(edges) :]
    (got,) = vmem_call(
        functools.partial(stack_kernel, nz - 1), [((nz - 1, taps, in_rows, span), BF)], slack=2
    )(*got)
    conv_own, ffn_own = lax.optimization_barrier((conv_own, ffn_own, got))[:2]
    conv_other = exchange(conv_own, "row", 1)
    ffn_other = exchange(ffn_own, "row", 1)
    conv_pieces = [got] + [exchange(got, "seq", k) for k in range(1, ns)]
    conv_other_pieces = [exchange(got, "row", 1)]
    ffn_part, conv_other_pieces[0], conv_other, ffn_other = lax.optimization_barrier(
        (ffn_part, conv_other_pieces[0], conv_other, ffn_other)
    )
    ffn_got = [exchange(ffn_part, "row", 2 * j) for j in range(nz - 1, 0, -1)][::-1]
    late = lax.optimization_barrier((*ffn_got, *conv_pieces[1:]))
    ffn_got, conv_pieces[1:] = late[: nz - 1], late[nz - 1 :]
    conv_other_pieces += [exchange(p, "row", 1) for p in conv_pieces[1:]]
    ffn_got, vector_near = vmem_call(
        functools.partial(stack_kernel, nz - 1),
        [((nz - 1, ffn_rows, width), BF), (vector_moments.shape, F32)],
        slack=2,
    )(*ffn_got, vector_moments)
    ffn_pieces = [ffn_got] + [exchange(ffn_got, "seq", k) for k in range(1, ns)]

    pre, after, conv_full = vmem_call(
        functools.partial(conv_kernel, taps, nz, ns, masks),
        [((count, width), F32), ((count, width), F32), ((taps, nz, 2, in_rows, width), BF)],
        [
            pltpu.VMEM((length + 2 * half, width), F32),
            pltpu.VMEM((length + 2 * half, LANES), jnp.int32),
            pltpu.VMEM((count, taps * width), BF),
            pltpu.SemaphoreType.DMA((2 * (1 + ns * (nz - 1)),)),
        ],
        smem=1,
        loose=[i for i in range(3, 6 + len(far_masks) + 2 * ns) if not 5 <= i < 6 + len(far_masks)],
    )(
        contig_lengths,
        vectors,
        tokens,
        conv_own,
        conv_other,
        token_pieces[1],
        *edges,
        *conv_pieces,
        *conv_other_pieces,
    )

    tokens_late = lax.optimization_barrier((tokens, pre, *ffn_pieces))[0]
    near = [k for k in range(1, ns) if k & (k - 1) == 0]
    token_pieces = [tokens] + [
        token_pieces[1 + near.index(k)] if k in near else exchange(tokens_late, "seq", k)
        for k in range(1, ns)
    ]
    late = lax.optimization_barrier((pre, *ffn_pieces))
    pre, ffn_pieces = late[0], late[1:]
    ffn_other_pieces = [exchange(p, "row", 1) for p in ffn_pieces]

    layer_out, low, hidden, outer_grad, inner_grad, inner_full, vec_sums = vmem_call(
        functools.partial(ffn_kernel, nz, ns),
        [
            ((count, width), BF),
            ((count, width), BF),
            ((count, hid), BF),
            ((count, width), BF),
            ((count, hid), BF),
            ((nz, 2, in_rows, hid), BF),
            ((VEC_PAD, width), F32),
        ],
        [
            pltpu.VMEM((nz, 2, ns, part, width), BF),
            pltpu.VMEM((count, hid), F32),
            pltpu.VMEM((count, width), F32),
        ],
        kept=(0,),
    )(after, cot, vectors, ffn_own, ffn_other, *ffn_pieces, *ffn_other_pieces)

    mine, theirs = vmem_call(
        functools.partial(ffn_weight_kernel, nz, ns, in_rows, out_rows),
        [((ns, nz, ffn_rows, width), BF)] * 2,
        [pltpu.VMEM((hid, width), BF), pltpu.VMEM((width, hid), BF)],
    )(low, hidden, outer_grad, inner_grad)

    inner_grad, mine = lax.optimization_barrier((inner_grad, mine))
    results = vmem_call(
        functools.partial(back_kernel, ns, rows),
        [((count, width), F32), ((count, width), BF)]
        + [
            ((count + 2 * vec_rows + edge_rows(k), span), BF)
            for k in range(ns)
        ],
        [pltpu.VMEM((count, width), F32), pltpu.VMEM((VEC_PAD, width), F32)],
    )(pre, cot, vectors, inner_grad, inner_full, vec_sums)
    after_grad, conv_grad = results[:2]
    grad_pieces = list(results[2:])
    late = lax.optimization_barrier((theirs, *grad_pieces, *token_pieces))
    theirs, grad_pieces, token_pieces = late[0], list(late[1 : 1 + ns]), late[1 + ns :]
    arrived = exchange(theirs, "row", 1)
    grad_pieces = grad_pieces[:1] + [exchange(grad_pieces[k], "seq", k) for k in range(1, ns)]
    mine, grad_pieces[1] = lax.optimization_barrier((mine, grad_pieces[1]))
    flat = (ns * nz * ffn_rows, width)
    ffn_sums = split_sum([mine.reshape(flat), arrived.reshape(flat)], ns)
    ffn_sums = [ffn_sums[0]] + [exchange(ffn_sums[k], "seq", k) for k in range(1, ns)]

    mine, theirs = vmem_call(
        functools.partial(conv_weight_kernel, taps, nz, ns, in_rows),
        [((nz * conv_rows + 2 * vec_rows, span), BF)] * 2,
        [
            pltpu.VMEM((ns * length + 2 * half, span), F32),
            pltpu.VMEM((ns * length + 2 * half, LANES), jnp.int32),
            pltpu.VMEM((ns * count, taps * span), BF),
            pltpu.VMEM((width, taps * span), F32),
            pltpu.VMEM((ns, rows, length, width), BF),
            pltpu.SemaphoreType.DMA((ns,)),
        ],
        smem=1,
        loose=range(1, 1 + ns),
    )(contig_lengths, *token_pieces, *grad_pieces)
    arrived = exchange(theirs, "row", 1)
    sums = vmem_call(
        functools.partial(conv_core_kernel, conv_rows),
        [((conv_rows + 2 * vec_rows, span), BF)] * nz,
        slack=2,
    )(mine, arrived)
    sums = [sums[0]] + [exchange(sums[j], "row", 2 * j) for j in range(1, nz)]

    masks = [k for k in range(ns) if edge_rows(k)]
    (input_grad,) = vmem_call(
        functools.partial(input_grad_kernel, taps, ns, rows, masks),
        [((count, width), F32)],
        [
            pltpu.VMEM((length + 2 * half, width), F32),
            pltpu.VMEM((length + 2 * half, LANES), jnp.int32),
            pltpu.VMEM((taps, count, width), BF),
        ],
        smem=1,
        kept=(0,),
    )(contig_lengths, conv_grad, after_grad, conv_full, *[grad_pieces[k] for k in masks])
    sums[0], input_grad = lax.optimization_barrier((sums[0], input_grad))

    conv_sum, conv_square, vec_sum = vmem_call(
        functools.partial(conv_final_kernel, nz, vec_rows),
        [((conv_rows, span), BF), ((8, LANES), F32), ((VEC_PAD, width), F32)],
        slack=2,
    )(*sums)
    conv_sums = [conv_sum] + [exchange(conv_sum, "seq", k) for k in range(1, ns)]

    ffn_sums = split_sum(ffn_sums, nz)
    ffn_sums = [ffn_sums[0]] + [exchange(ffn_sums[j], "row", 2 * j) for j in range(1, nz)]
    ffn_sums[0], conv_sums[-1] = lax.optimization_barrier((ffn_sums[0], conv_sums[-1]))
    (ffn_sum,) = vmem_call(
        functools.partial(ffn_final_kernel, nz), [((ffn_rows + VEC_PAD, width), BF)], slack=2
    )(*ffn_sums, conv_square)
    ffn_sums = [ffn_sum] + [exchange(ffn_sum, "seq", k) for k in range(1, ns)]
    (square,) = vmem_call(
        functools.partial(square_kernel, ns), [((8, LANES), F32)], slack=2
    )(*ffn_sums)
    squares = [square] + [exchange(square, "row", 2 * j) for j in range(1, nz)]
    (square,) = vmem_call(small_sum_kernel, [((8, LANES), F32)], slack=2)(*squares)
    squares = [square, exchange(square, "row", 1)]

    second_width = taps * width + hid + (out_rows // in_rows) * width + vectors.shape[0]
    results = [
        (conv_weight.shape, F32),
        (conv_weight.shape, F32),
        (inner_weight.shape, F32),
        (inner_weight.shape, F32),
        (outer_weight.shape, F32),
        (outer_weight.shape, F32),
        ((in_rows, second_width), F32),
    ]
    (
        norm,
        new_vectors,
        vector_first,
        new_conv,
        conv_first,
        new_inner,
        inner_first,
        new_outer,
        outer_first,
        second_moments,
    ) = vmem_call(
        functools.partial(adam_kernel, taps, ns),
        [((1, 1), F32), (vectors.shape, F32), (vectors.shape, F32), *results],
        [pltpu.VMEM(shape, dtype) for shape, dtype in results]
        + [
            pltpu.VMEM((width // LANES, out_rows, LANES), F32),
            pltpu.VMEM((width, LANES), F32),
            pltpu.SemaphoreType.DMA((8,)),
        ],
        kept=range(3),
        left=range(3, 10),
        slack=3,
    )(
        *conv_sums,
        *ffn_sums,
        vec_sum,
        *squares,
        conv_weight,
        inner_weight,
        outer_weight,
        vectors,
        conv_moments,
        inner_moments,
        outer_moments,
        vector_near,
    )
    return (
        layer_out.reshape(tokens.shape),
        input_grad.reshape(tokens.shape),
        norm.reshape(()),
        new_conv,
        conv_first,
        new_inner,
        inner_first,
        new_outer,
        outer_first,
        new_vectors,
        vector_first,
        second_moments,
    )


def solution(mesh):
    in_specs = (
        P("row", "seq", None),
        P("row", "seq", None),
        P("row", None),
        P(None, "row", None),
        P("row", None),
        P("row", None),
        P(),
        P(None, None, "row", None),
        P(None, "row", None),
        P(None, "row", None),
        P(),
    )
    out_specs = (
        P("row", "seq", None),
        P("row", "seq", None),
        P(),
        P(None, "row", None),
        P(None, "row", None),
        P("row", None),
        P("row", None),
        P("row", None),
        P("row", None),
        P(),
        P(),
        P("row", None),
    )
    return jax.shard_map(
        per_device, mesh=mesh, in_specs=in_specs, out_specs=out_specs, check_vma=False
    )
```

```python
import functools

import jax
import jax.numpy as jnp
from jax import lax
from jax.experimental import pallas as pl
from jax.experimental.pallas import tpu as pltpu
from jax.sharding import PartitionSpec as P

DILATION_STEP = 8

beta_one = 0.9
beta_two = 0.999
adam_eps = 1e-08
weight_decay = 0.1
matrix_rate = 0.03
vector_rate = 0.3
clip_level = 1.0
step_count = 10
norm_eps = 1e-05

F32 = jnp.float32
BF = jnp.bfloat16
VEC_PAD = 16
VEC_ROWS = 10
LANES = 128
SQRT_HALF = 0.7071067811865476
PDF_SCALE = 0.3989422804014327


def exchange(value, axis, mask):
    size = lax.axis_size(axis)
    return lax.ppermute(value, axis, [(i, i ^ mask) for i in range(size)])


def shift_along(value, axis, step):
    size = lax.axis_size(axis)
    pairs = [(i, i + step) for i in range(size) if 0 <= i + step < size]
    return lax.ppermute(value, axis, pairs)


def gelu_parts(v):
    cdf = 0.5 + 0.5 * lax.erf(v * SQRT_HALF)
    return v * cdf, cdf


def gelu_slope(v, cdf):
    return cdf + v * (jnp.exp(-0.5 * v * v) * PDF_SCALE)


def mean_of(v):
    return jnp.mean(v, axis=-1, keepdims=True)


def normalized(v):
    centred = v - mean_of(v)
    scale = lax.rsqrt(mean_of(centred * centred) + norm_eps)
    return centred * scale, scale


def fold_rows(v):
    rows, cols = v.shape
    return jnp.sum(v.reshape(rows // 8, 8, cols), axis=0)


def column_sum(acc):
    return jnp.sum(acc, axis=0, keepdims=True)


def loop_rows(total, step, body, init=0):
    return lax.fori_loop(
        0, total // step, lambda i, carry: body(pl.multiple_of(i * step, step), carry), init
    )


def dot(a, b):
    return jnp.dot(a, b, preferred_element_type=F32)


def dot_nt(a, b):
    return lax.dot_general(a, b, (((1,), (1,)), ((), ())), preferred_element_type=F32)


def dot_tn(a, b):
    return lax.dot_general(a, b, (((0,), (0,)), ((), ())), preferred_element_type=F32)


def place():
    seq_at = lax.axis_index("seq")
    row_at = lax.axis_index("row")
    return seq_at, row_at // 2, row_at % 2


def at(index, step):
    return pl.ds(pl.multiple_of(index * step, step), step)


def size_of(shape, dtype):
    total = jnp.dtype(dtype).itemsize
    for n in shape:
        total *= n
    return total


def vmem_call(kernel, outs, scratch=(), smem=0, loose=(), far=(), kept=(), left=(), slack=6):
    space = pl.BlockSpec(memory_space=pltpu.VMEM)
    anywhere = pl.BlockSpec(memory_space=pl.ANY)
    grant = slack * 1024 * 1024
    grant += sum(size_of(v.shape, v.dtype) for v in scratch if hasattr(v, "shape") and v.dtype in (F32, BF, jnp.int32))
    grant += sum(size_of(*outs[i]) for i in kept)

    def call(*args):
        fixed = [
            a
            if i < smem or i in loose
            else pltpu.with_memory_space_constraint(a, pltpu.HBM if i in far else pltpu.VMEM)
            for i, a in enumerate(args)
        ]
        return pl.pallas_call(
            kernel,
            out_shape=[
                jax.ShapeDtypeStruct(shape, dtype) if i in kept or i in left else pltpu.VMEM(shape, dtype)
                for i, (shape, dtype) in enumerate(outs)
            ],
            in_specs=[
                pl.BlockSpec(memory_space=pltpu.SMEM)
                if i < smem
                else pl.BlockSpec(memory_space=pltpu.HBM)
                if i in far
                else anywhere
                if i in loose
                else space
                for i in range(len(args))
            ],
            out_specs=[anywhere if i in left else space for i in range(len(outs))],
            scratch_shapes=list(scratch),
            cost_estimate=pl.CostEstimate(flops=1, bytes_accessed=1, transcendentals=0),
            compiler_params=pltpu.CompilerParams(vmem_limit_bytes=grant),
        )(*fixed)

    return call


def begin_copies(pairs, sems):
    copies = [pltpu.make_async_copy(src, dst, sems.at[i]) for i, (src, dst) in enumerate(pairs)]
    for copy in copies:
        copy.start()
    return copies


def end_copies(copies):
    for copy in copies:
        copy.wait()


def contigs(lens_ref, row, positions, row_length):
    found = jnp.zeros(positions.shape, jnp.int32)
    start = jnp.int32(0)
    for j in range(lens_ref.shape[1] - 1):
        start = start + lens_ref[row, j]
        found = found + (positions >= start).astype(jnp.int32)
    found = jnp.where(positions < 0, -1, found)
    return jnp.where(positions >= row_length, lens_ref.shape[1], found)


def masked_taps(src, cid, length, taps, half, store):
    centre = cid[pl.ds(half, length), :]

    def body(tap, carry):
        begin = pl.multiple_of(tap * DILATION_STEP, DILATION_STEP)
        keep = cid[pl.ds(begin, length), :] == centre
        for a in range(src.shape[1] // LANES):
            part = src[pl.ds(begin, length), a * LANES : (a + 1) * LANES]
            store(tap, a, jnp.where(keep, part, 0.0).astype(BF))
        return carry

    lax.fori_loop(0, taps, body, 0)


def round_kernel(ns, masks, conv_far, inner_far, outer_far, tok_far, *refs):
    conv_part, conv_own, ffn_own, ffn_part = refs[:4]
    edges = refs[4 : 4 + len(masks)]
    conv, inner, outer, sems = refs[4 + len(masks) :]
    seq_at = lax.axis_index("seq")
    pairs = [(conv_far, conv), (inner_far, inner), (outer_far, outer)]
    for mask, edge in zip(masks, edges):
        half = edge.shape[1]
        last = jnp.where((seq_at ^ mask) > seq_at, tok_far.shape[1] // half - 1, 0)
        pairs.append((tok_far.at[:, at(last, half)], edge))
    copies = begin_copies(pairs, sems)
    in_rows, hid = inner.shape
    quarter = hid // ns
    part = outer.shape[0] // ns
    span = conv.shape[2] // ns
    copies[0].wait()
    for t in range(conv.shape[0]):
        conv_own[t] = conv[t].astype(BF)
        conv_part[t] = conv[t, :, at(seq_at, span)].astype(BF)
    end_copies(copies[1:])
    for k in range(ns):
        ffn_own[k * in_rows : (k + 1) * in_rows, :] = inner[
            :, k * quarter : (k + 1) * quarter
        ].astype(BF)
    ffn_own[ns * in_rows :, :] = outer[...].astype(BF)
    ffn_part[:in_rows, :] = inner[:, at(seq_at, quarter)].astype(BF)
    ffn_part[in_rows:, :] = outer[at(seq_at, part), :].astype(BF)


def stack_kernel(count, *refs):
    ins, rest = refs[:count], refs[count:]
    out = rest[len(rest) // 2]
    for i, ref in enumerate(ins):
        out[i] = ref[...]
    if len(rest) > 1:
        rest[2][...] = rest[0][...]


def conv_kernel(taps, nz, ns, masks, lens, vec, tok, own, other, *rest):
    edges, rest = rest[: len(masks)], rest[len(masks) :]
    pieces = (rest[:ns], rest[ns : 2 * ns])
    pre, after, full, ext, cid, cat, sems = rest[2 * ns :]
    seq_at, z_at, core_at = place()
    rows, length, width = tok.shape
    quarter = width // ns
    half = DILATION_STEP * (taps // 2)
    pairs = []
    for i, whole in enumerate((own, other)):
        core = core_at ^ i
        pairs.append((whole, full.at[:, z_at, core]))
        for k in range(ns):
            for j in range(1, nz):
                cols = at(seq_at ^ k, quarter)
                pairs.append((pieces[i][k].at[j - 1], full.at[:, z_at ^ j, core, :, cols]))
    copies = begin_copies(pairs, sems)
    span = length + 2 * half
    base = seq_at * length - half
    positions = base + lax.broadcasted_iota(jnp.int32, (span, LANES), 0)
    ext[0:half, :] = jnp.zeros((half, width), F32)
    ext[half + length :, :] = jnp.zeros((half, width), F32)
    for r in range(rows):
        ext[half : half + length, :] = tok[r].astype(F32)
        for mask, edge in zip(masks, edges):
            for step, to, begin in ((-1, 0, edge.shape[1] - half), (1, half + length, 0)):

                @pl.when((seq_at ^ mask) == seq_at + step)
                def _(r=r, edge=edge, to=to, begin=begin):
                    ext[to : to + half, :] = edge[r, begin : begin + half, :].astype(F32)

        cid[...] = contigs(lens, r, positions, length * ns)

        def store(tap, a, value, r=r):
            cat[r * length : (r + 1) * length, at(tap * (width // LANES) + a, LANES)] = value

        masked_taps(ext, cid, length, taps, half, store)
    end_copies(copies)
    weights = full.reshape(taps * width, width)

    def product(r, carry):
        where = at(r, length)
        pre[where, :] = dot(cat[where, :], weights[...]) + vec[0:1, :]
        return carry

    lax.fori_loop(0, rows, product, 0)

    for r in range(rows):

        def norm(begin, carry, r=r):
            where = pl.ds(r * length + begin, 256)
            active, _ = gelu_parts(pre[where, :])
            unit, _ = normalized(active)
            after[where, :] = (
                tok[r, pl.ds(begin, 256), :].astype(F32) + unit * vec[1:2, :] + vec[2:3, :]
            )
            return carry

        loop_rows(length, 256, norm)


def ffn_kernel(nz, ns, *refs):
    after, cot, vec = refs[:3]
    wholes = refs[3:5]
    pieces = (refs[5 : 5 + ns], refs[5 + ns : 5 + 2 * ns])
    rest = refs[5 + 2 * ns :]
    layer, low, hidden, outer_grad, inner_grad, inner_full, sums, outer_full, slope, tmp = rest
    seq_at, z_at, core_at = place()
    count, width = after.shape
    hid = inner_full.shape[3]
    in_rows = inner_full.shape[2]
    quarter = hid // ns
    blocks = hid // width
    inner = inner_full.reshape(width, hid)
    outer = outer_full.reshape(hid, width)
    part = outer_full.shape[3]
    for i, whole in enumerate(wholes):
        core = core_at ^ i
        for q in range(ns):
            inner_full[z_at, core, :, q * quarter : (q + 1) * quarter] = whole[
                q * in_rows : (q + 1) * in_rows
            ]
            begin = ns * in_rows + q * part
            outer_full[z_at, core, q] = whole[begin : begin + part]
        for k in range(ns):
            piece = pieces[i][k]
            q = seq_at ^ k
            for j in range(1, nz):
                z = z_at ^ j
                inner_full[z, core, :, at(q, quarter)] = piece[j - 1, :in_rows]
                outer_full[z, core, q] = piece[j - 1, in_rows:]

    def lower(begin, carry):
        where = pl.ds(begin, 64)
        low[where, :] = after[where, :].astype(BF)
        return carry

    loop_rows(count, 64, lower)

    def up(b, carry):
        cols = at(b, width)
        tmp[...] = dot(low[...], inner[:, cols]) + vec[pl.ds(6 + b, 1), :]

        def act(begin, inside):
            where = pl.ds(begin, 128)
            v = tmp[where, :]
            active, cdf = gelu_parts(v)
            hidden[where, cols] = active.astype(BF)
            slope[where, cols] = gelu_slope(v, cdf)
            return inside

        loop_rows(count, 128, act)
        return carry

    lax.fori_loop(0, blocks, up, 0)
    tmp[...] = dot(hidden[...], outer[...]) + vec[3:4, :]
    zero = jnp.zeros((8, width), F32)

    def second(begin, carry):
        bias_sum, gain_sum, shift_sum = carry
        where = pl.ds(begin, 256)
        unit, scale = normalized(tmp[where, :])
        gain = vec[4:5, :]
        layer[where, :] = (after[where, :] + unit * gain + vec[5:6, :]).astype(BF)
        dy = cot[where, :].astype(F32)
        u = dy * gain
        grad = (scale * (u - mean_of(u) - unit * mean_of(u * unit))).astype(BF)
        outer_grad[where, :] = grad
        return (
            bias_sum + fold_rows(grad.astype(F32)),
            gain_sum + fold_rows(dy * unit),
            shift_sum + fold_rows(dy),
        )

    totals = loop_rows(count, 256, second, (zero, zero, zero))
    sums[...] = jnp.zeros(sums.shape, F32)
    for i, total in enumerate(totals):
        sums[3 + i : 4 + i, :] = column_sum(total)

    def down(b, carry):
        cols = at(b, width)
        tmp[...] = dot_nt(outer_grad[...], outer[cols, :])

        def act(begin, total):
            where = pl.ds(begin, 128)
            grad = (tmp[where, :] * slope[where, cols]).astype(BF)
            inner_grad[where, cols] = grad
            return total + fold_rows(grad.astype(F32))

        total = loop_rows(count, 128, act, zero)
        sums[pl.ds(6 + b, 1), :] = column_sum(total)
        return carry

    lax.fori_loop(0, blocks, down, 0)


def back_kernel(ns, rows, *refs):
    pre, cot, vec, inner_grad, inner_full, partial_sums, after_grad, conv_grad = refs[:8]
    inner = inner_full.reshape(pre.shape[1], inner_grad.shape[1])
    sends = refs[8 : 8 + ns]
    tmp, sums = refs[8 + ns :]
    seq_at = lax.axis_index("seq")
    count, width = pre.shape
    zero = jnp.zeros((8, width), F32)
    sums[...] = partial_sums[...]
    tmp[...] = dot_nt(inner_grad[...], inner[...])

    def first(begin, carry):
        bias_sum, gain_sum, shift_sum = carry
        where = pl.ds(begin, 256)
        upstream = cot[where, :].astype(F32) + tmp[where, :]
        after_grad[where, :] = upstream
        v = pre[where, :]
        active, cdf = gelu_parts(v)
        unit, scale = normalized(active)
        u = upstream * vec[1:2, :]
        grad = scale * (u - mean_of(u) - unit * mean_of(u * unit))
        grad = (grad * gelu_slope(v, cdf)).astype(BF)
        conv_grad[where, :] = grad
        return (
            bias_sum + fold_rows(grad.astype(F32)),
            gain_sum + fold_rows(upstream * unit),
            shift_sum + fold_rows(upstream),
        )

    totals = loop_rows(count, 256, first, (zero, zero, zero))
    for i, total in enumerate(totals):
        sums[i : i + 1, :] = column_sum(total)
    span = width // ns
    for k in range(ns):
        sends[k][0:count, :] = conv_grad[:, at(seq_at ^ k, span)]
        encode(sends[k], count, spread(sums[...]))
        begin = count + 2 * VEC_ROWS * width // LANES
        if sends[k].shape[0] > begin:
            half = (sends[k].shape[0] - begin) // rows // (width // LANES)
            length = count // rows
            first = jnp.where((seq_at ^ k) > seq_at, length - half, 0)
            for r in range(rows):
                for a in range(width // LANES):
                    sends[k][begin : begin + half, :] = conv_grad[
                        at(r * (length // half) + first // half, half), a * LANES : (a + 1) * LANES
                    ]
                    begin += half


def spread(v):
    v = v[:VEC_ROWS]
    return jnp.concatenate(
        [v[:, a * LANES : (a + 1) * LANES] for a in range(v.shape[1] // LANES)], axis=0
    )


def gathered(v):
    return jnp.concatenate(
        [v[a * VEC_ROWS : (a + 1) * VEC_ROWS, :] for a in range(v.shape[0] // VEC_ROWS)], axis=1
    )


def encode(ref, begin, v):
    rows = v.shape[0]
    high = v.astype(BF)
    ref[begin : begin + rows, :] = high
    ref[begin + rows : begin + 2 * rows, :] = (v - high.astype(F32)).astype(BF)


def decode(ref, begin, rows):
    high = ref[begin : begin + rows, :].astype(F32)
    return high + ref[begin + rows : begin + 2 * rows, :].astype(F32)


def tree_sum(values):
    values = list(values)
    while len(values) > 1:
        values = [values[i] + values[i + 1] for i in range(0, len(values), 2)]
    return values[0]


def ffn_weight_kernel(nz, ns, in_rows, out_rows, *refs):
    low, hidden, outer_grad, inner_grad, mine, theirs, outer_sum, inner_sum = refs
    seq_at, z_at, core_at = place()
    width = low.shape[1]
    hid = hidden.shape[1]
    part = out_rows // ns
    quarter = hid // ns

    def product(b, carry):
        cols = at(b, width)
        outer_sum[cols, :] = dot_tn(hidden[:, cols], outer_grad[...]).astype(BF)
        inner_sum[:, cols] = dot_tn(low[...], inner_grad[:, cols]).astype(BF)
        return carry

    lax.fori_loop(0, hid // width, product, 0)
    for i, out in enumerate((mine, theirs)):
        for k in range(ns):
            for j in range(nz):
                block = (z_at ^ j) * 2 + (core_at ^ i)
                out[k, j, :in_rows] = inner_sum[at(block, in_rows), at(seq_at ^ k, quarter)]
                out[k, j, in_rows:] = outer_sum[at(block * ns + (seq_at ^ k), part), :]


def conv_weight_kernel(taps, nz, ns, in_rows, *refs):
    lens = refs[0]
    far = refs[1 : 1 + ns]
    grads = refs[1 + ns : 1 + 2 * ns]
    mine, theirs, padded, cid, cat, total, toks, sems = refs[1 + 2 * ns :]
    copies = begin_copies([(far[k], toks.at[k]) for k in range(ns)], sems)
    seq_at, z_at, core_at = place()
    _, rows, length, width = toks.shape
    span = width // ns
    half = DILATION_STEP * (taps // 2)
    row_length = ns * length
    count = rows * length
    positions = lax.broadcasted_iota(jnp.int32, (row_length + 2 * half, LANES), 0) - half
    edge = jnp.zeros((half, span), F32)
    for r in range(rows):
        padded[0:half, :] = edge
        padded[half + row_length :, :] = edge
        cid[...] = contigs(lens, r, positions, row_length)
        for k in range(ns):
            padded[pl.ds(half + (seq_at ^ k) * length, length), :] = grads[k][
                r * length : (r + 1) * length, :
            ].astype(F32)
        for k in range(ns):
            base = (seq_at ^ k) * length
            centre = cid[pl.ds(pl.multiple_of(base + half, 8), length), :]
            for t in range(taps):
                begin = pl.multiple_of(base + DILATION_STEP * (taps - 1 - t), 8)
                keep = cid[pl.ds(begin, length), :] == centre
                value = jnp.where(keep, padded[pl.ds(begin, length), :], 0.0)
                low_row = k * count + r * length
                cat[low_row : low_row + length, t * span : (t + 1) * span] = value.astype(BF)
    end_copies(copies)
    for k in range(ns):
        value = tree_sum(
            [
                dot_tn(toks[k, r], cat[k * count + r * length : k * count + (r + 1) * length, :])
                for r in range(rows)
            ]
        )
        if k == 0:
            total[...] = value
        else:
            total[...] += value
    for i, out in enumerate((mine, theirs)):
        for j in range(nz):
            block = (z_at ^ j) * 2 + (core_at ^ i)
            for t in range(taps):
                begin = (j * taps + t) * in_rows
                out[begin : begin + in_rows, :] = total[
                    at(block, in_rows), t * span : (t + 1) * span
                ].astype(BF)
    vec_rows = VEC_ROWS * width // LANES
    summed = tree_sum([decode(g, count, vec_rows) for g in grads])
    for out in (mine, theirs):
        encode(out, nz * taps * in_rows, summed)


def input_grad_kernel(taps, ns, rows, masks, *refs):
    lens, grad, after_grad, full_blocks = refs[:4]
    pieces = refs[4 : 4 + len(masks)]
    out, ext, cid, cat = refs[4 + len(masks) :]
    full = full_blocks.reshape(taps, grad.shape[1], grad.shape[1])
    seq_at = lax.axis_index("seq")
    half = DILATION_STEP * (taps // 2)
    width = grad.shape[1]
    length = grad.shape[0] // rows
    base = seq_at * length - half
    positions = base + lax.broadcasted_iota(jnp.int32, (length + 2 * half, LANES), 0)
    ext[0:half, :] = jnp.zeros((half, width), F32)
    ext[half + length :, :] = jnp.zeros((half, width), F32)
    for r in range(rows):
        ext[half : half + length, :] = grad[r * length : (r + 1) * length, :].astype(F32)
        for mask, piece in zip(masks, pieces):
            for step, begin in ((-1, 0), (1, half + length)):

                @pl.when((seq_at ^ mask) == seq_at + step)
                def _(r=r, piece=piece, begin=begin):
                    first = piece.shape[0] - rows * half * (width // LANES)
                    for a in range(width // LANES):
                        low = first + (r * (width // LANES) + a) * half
                        ext[begin : begin + half, a * LANES : (a + 1) * LANES] = piece[
                            low : low + half, :
                        ].astype(F32)

        cid[...] = contigs(lens, r, positions, length * ns)

        def store(tap, a, value, r=r):
            flipped = taps - 1 - tap
            cat[
                flipped, r * length : (r + 1) * length, a * LANES : (a + 1) * LANES
            ] = value

        masked_taps(ext, cid, length, taps, half, store)

    out[...] = after_grad[...]

    def product(t, carry):
        out[...] += dot_nt(cat[t], full[t])
        return carry

    lax.fori_loop(0, taps, product, 0)


def split_sum_kernel(count, *refs):
    ins, outs = refs[:count], refs[count:]
    rows = outs[0].shape[0]
    for p, out in enumerate(outs):

        def body(begin, carry, p=p, out=out):
            where = pl.ds(p * rows + begin, 64)
            out[pl.ds(begin, 64), :] = tree_sum([v[where, :].astype(F32) for v in ins]).astype(BF)
            return carry

        loop_rows(rows, 64, body)


def split_sum(ins, parts):
    rows, cols = ins[0].shape
    return vmem_call(
        functools.partial(split_sum_kernel, len(ins)),
        [((rows // parts, cols), BF)] * parts,
        slack=2,
    )(*ins)


def conv_core_kernel(rows, mine, got, *outs):
    vec_rows = (mine.shape[0] - rows * len(outs)) // 2
    begin_vec = rows * len(outs)
    summed = decode(mine, begin_vec, vec_rows) + decode(got, begin_vec, vec_rows)
    for p, out in enumerate(outs):

        def body(begin, carry, p=p, out=out):
            where = pl.ds(p * rows + begin, 64)
            out[pl.ds(begin, 64), :] = (mine[where, :].astype(F32) + got[where, :].astype(F32)).astype(
                BF
            )
            return carry

        loop_rows(rows, 64, body)
        encode(out, rows, summed)


def conv_final_kernel(count, vec_rows, *refs):
    ins, (out, square, vec_sum) = refs[:count], refs[count:]
    square[...] = summed_square(ins, out)
    vec_sum[...] = gathered(tree_sum([decode(v, out.shape[0], vec_rows) for v in ins]))


def summed_square(ins, out):
    def body(begin, carry):
        where = pl.ds(begin, 64)
        value = tree_sum([v[where, :].astype(F32) for v in ins]).astype(BF)
        out[where, :] = value
        wide = value.astype(F32)
        return carry + lane_fold(fold_rows(wide * wide))

    rows = ins[0].shape[0] // 64 * 64 if out.shape[0] % 64 else out.shape[0]
    return loop_rows(min(rows, out.shape[0]), 64, body, jnp.zeros((8, LANES), F32))


def lane_fold(v):
    return sum(v[:, a * LANES : (a + 1) * LANES] for a in range(v.shape[1] // LANES))


def ffn_final_kernel(count, *refs):
    ins, (conv_square, out) = refs[:count], refs[count:]
    rows = ins[0].shape[0]
    square = summed_square(ins, out.at[0:rows]) + conv_square[...]
    high = square.astype(BF)
    low = (square - high.astype(F32)).astype(BF)
    zero = jnp.zeros(high.shape, BF)
    tail = jnp.concatenate([high, low] + [zero] * (out.shape[1] // LANES - 2), axis=1)
    out[rows : rows + VEC_PAD, :] = jnp.concatenate([tail, jnp.zeros(tail.shape, BF)], axis=0)


def square_kernel(count, *refs):
    ins, out = refs[:count], refs[count]
    rows = ins[0].shape[0] - VEC_PAD
    parts = []
    for v in ins:
        tail = v[rows : rows + VEC_PAD, :].astype(F32)
        parts.append(tail[:8, :LANES] + tail[:8, LANES : 2 * LANES])
    out[...] = tree_sum(parts)


def small_sum_kernel(*refs):
    refs[-1][...] = tree_sum([v[...] for v in refs[:-1]])


def adam_math(weight, first, second, gradient, clip, rate, decay):
    clipped = gradient * clip
    first = beta_one * first + (1.0 - beta_one) * clipped
    second = beta_two * second + (1.0 - beta_two) * clipped * clipped
    first_hat = first * (1.0 / (1.0 - beta_one**step_count))
    second_hat = second * (1.0 / (1.0 - beta_two**step_count))
    weight = weight - rate * (first_hat / (jnp.sqrt(second_hat) + adam_eps) + decay * weight)
    return weight, first, second


def adam_kernel(taps, ns, *refs):
    conv_grads = refs[:ns]
    ffn_grads = refs[ns : 2 * ns]
    vec_sum, one, two, conv, inner, outer, vec, conv_m, inner_m, outer_m, vec_m = refs[
        2 * ns : 2 * ns + 11
    ]
    norm, new_vec, vec_first = refs[2 * ns + 11 : 2 * ns + 14]
    outs = refs[2 * ns + 14 : 2 * ns + 21]
    new_conv, conv_first, new_inner, inner_first, new_outer, outer_first, second = refs[
        2 * ns + 21 : 2 * ns + 28
    ]
    outer_second, vec_second, sems = refs[2 * ns + 28 :]
    seq_at, z_at, core_at = place()
    in_rows, width = conv.shape[1:]
    hid = inner.shape[1]
    out_rows = outer.shape[0]
    span = width // ns
    quarter = hid // ns
    part = out_rows // ns
    vec_count = vec.shape[0]
    vec_grad = vec_sum[0:vec_count, :]
    total = jnp.sum(one[...] + two[...]) + jnp.sum(vec_grad * vec_grad)
    value = jnp.sqrt(jnp.full((1, 1), total, F32))
    norm[...] = value
    clip = clip_level / jnp.maximum(value, clip_level)
    going = []

    def send(index, src, dst):
        copy = pltpu.make_async_copy(src, dst, sems.at[index])
        copy.start()
        going.append(copy)

    def conv_step(t, carry):
        for k in range(ns):
            cols = at(seq_at ^ k, span)
            w, m, v = adam_math(
                conv[t, :, cols],
                conv_m[0, t, :, cols],
                conv_m[1, t, :, cols],
                conv_grads[k][at(t, in_rows), :].astype(F32),
                clip,
                matrix_rate,
                weight_decay,
            )
            new_conv[t, :, cols] = w
            conv_first[t, :, cols] = m
            second[:, at(t * ns + (seq_at ^ k), span)] = v
        return carry

    for k in range(ns):
        lanes = at(seq_at ^ k, quarter)
        w, m, v = adam_math(
            inner[:, lanes],
            inner_m[0, :, lanes],
            inner_m[1, :, lanes],
            ffn_grads[k][0:in_rows, :].astype(F32),
            clip,
            matrix_rate,
            weight_decay,
        )
        new_inner[:, lanes] = w
        inner_first[:, lanes] = m
        second[:, at(taps * width // quarter + (seq_at ^ k), quarter)] = v
    send(0, new_inner, outs[2])
    send(1, inner_first, outs[3])
    for k in range(ns):
        where = at(seq_at ^ k, part)
        w, m, v = adam_math(
            outer[where, :],
            outer_m[0, where, :],
            outer_m[1, where, :],
            ffn_grads[k][in_rows : in_rows + part, :].astype(F32),
            clip,
            matrix_rate,
            weight_decay,
        )
        new_outer[where, :] = w
        outer_first[where, :] = m
        for a in range(width // LANES):
            outer_second[a, where, :] = v[:, a * LANES : (a + 1) * LANES]
    send(2, new_outer, outs[4])
    send(3, outer_first, outs[5])
    ratio = out_rows // in_rows
    base = taps * width + hid
    for e in range(ratio):
        for a in range(width // LANES):
            begin = base + e * width + a * LANES
            second[:, begin : begin + LANES] = outer_second[a, pl.ds(e, in_rows, stride=ratio), :]
    w, m, v = adam_math(vec[...], vec_m[0], vec_m[1], vec_grad, clip, vector_rate, 0.0)
    new_vec[...] = w
    vec_first[...] = m
    v = jnp.concatenate([v, jnp.zeros((LANES - vec_count, width), F32)], axis=0)
    vec_second[...] = jnp.transpose(v)
    begin = base + ratio * width
    block = z_at * 2 + core_at
    second[:, begin : begin + vec_count] = vec_second[at(block, in_rows), :][:, 0:vec_count]
    send(4, second.at[:, taps * width :], outs[6].at[:, taps * width :])
    parts = 3
    for p in range(parts):
        low, high = taps * p // parts, taps * (p + 1) // parts
        lax.fori_loop(low, high, conv_step, 0)
        send(5 + 3 * p, new_conv.at[low:high], outs[0].at[low:high])
        send(6 + 3 * p, conv_first.at[low:high], outs[1].at[low:high])
        cols = slice(low * width, high * width)
        send(7 + 3 * p, second.at[:, cols], outs[6].at[:, cols])
    end_copies(going)


def per_device(
    tokens,
    cotangent,
    contig_lengths,
    conv_weight,
    inner_weight,
    outer_weight,
    vectors,
    conv_moments,
    inner_moments,
    outer_moments,
    vector_moments,
):
    ns = lax.axis_size("seq")
    nr = lax.axis_size("row")
    nz = nr // 2
    seq_at = lax.axis_index("seq")
    rows, length, width = tokens.shape
    taps, in_rows, _ = conv_weight.shape
    hid = inner_weight.shape[1]
    out_rows = outer_weight.shape[0]
    count = rows * length
    half = DILATION_STEP * (taps // 2)
    span = width // ns
    quarter = hid // ns
    part = out_rows // ns

    ffn_rows = in_rows + part
    vec_rows = VEC_ROWS * width // LANES
    conv_rows = taps * in_rows
    cot = cotangent.reshape(count, width)

    def edge_rows(k):
        near = any(abs((i ^ k) - i) == 1 for i in range(ns))
        return rows * half * (width // LANES) if near else 0

    masks = [k for k in range(ns) if edge_rows(k)]
    far_masks = [k for k in masks if k > 1]
    rounded = vmem_call(
        functools.partial(round_kernel, ns, far_masks),
        [
            ((taps, in_rows, span), BF),
            (conv_weight.shape, BF),
            ((ns * ffn_rows, width), BF),
            ((ffn_rows, width), BF),
        ]
        + [((rows, half, width), BF)] * len(far_masks),
        [
            pltpu.VMEM(conv_weight.shape, F32),
            pltpu.VMEM(inner_weight.shape, F32),
            pltpu.VMEM(outer_weight.shape, F32),
            pltpu.SemaphoreType.DMA((3 + len(far_masks),)),
        ],
        far=range(4),
        slack=2,
    )(conv_weight, inner_weight, outer_weight, tokens)
    conv_part, conv_own, ffn_own, ffn_part = rounded[:4]
    got = [exchange(conv_part, "row", 2 * j) for j in range(1, nz)]
    edges = [
        exchange(lax.optimization_barrier((rounded[4 + i], got[0]))[0], "seq", k)
        for i, k in enumerate(far_masks)
    ]
    tokens_now = lax.optimization_barrier((tokens, conv_part))[0]
    token_pieces = [tokens] + [
        exchange(tokens_now, "seq", k) for k in range(1, ns) if k & (k - 1) == 0
    ]
    late = lax.optimization_barrier((got[0], *edges, *token_pieces[1:]))
    got[0], edges, token_pieces[1:] = late[0], late[1 : 1 + len(edges)], late[1 + len(edges) :]
    (got,) = vmem_call(
        functools.partial(stack_kernel, nz - 1), [((nz - 1, taps, in_rows, span), BF)], slack=2
    )(*got)
    conv_own, ffn_own = lax.optimization_barrier((conv_own, ffn_own, got))[:2]
    conv_other = exchange(conv_own, "row", 1)
    ffn_other = exchange(ffn_own, "row", 1)
    conv_pieces = [got] + [exchange(got, "seq", k) for k in range(1, ns)]
    conv_other_pieces = [exchange(got, "row", 1)]
    ffn_part, conv_other_pieces[0], conv_other, ffn_other = lax.optimization_barrier(
        (ffn_part, conv_other_pieces[0], conv_other, ffn_other)
    )
    ffn_got = [exchange(ffn_part, "row", 2 * j) for j in range(nz - 1, 0, -1)][::-1]
    late = lax.optimization_barrier((*ffn_got, *conv_pieces[1:]))
    ffn_got, conv_pieces[1:] = late[: nz - 1], late[nz - 1 :]
    conv_other_pieces += [exchange(p, "row", 1) for p in conv_pieces[1:]]
    ffn_got, vector_near = vmem_call(
        functools.partial(stack_kernel, nz - 1),
        [((nz - 1, ffn_rows, width), BF), (vector_moments.shape, F32)],
        slack=2,
    )(*ffn_got, vector_moments)
    ffn_pieces = [ffn_got] + [exchange(ffn_got, "seq", k) for k in range(1, ns)]

    ffn_near, conv_own = lax.optimization_barrier((exchange(ffn_got, "row", 1), conv_own))
    pre, after, conv_full = vmem_call(
        functools.partial(conv_kernel, taps, nz, ns, masks),
        [((count, width), F32), ((count, width), F32), ((taps, nz, 2, in_rows, width), BF)],
        [
            pltpu.VMEM((length + 2 * half, width), F32),
            pltpu.VMEM((length + 2 * half, LANES), jnp.int32),
            pltpu.VMEM((count, taps * width), BF),
            pltpu.SemaphoreType.DMA((2 * (1 + ns * (nz - 1)),)),
        ],
        smem=1,
        loose=[i for i in range(3, 6 + len(far_masks) + 2 * ns) if not 5 <= i < 6 + len(far_masks)],
    )(
        contig_lengths,
        vectors,
        tokens,
        conv_own,
        conv_other,
        token_pieces[1],
        *edges,
        *conv_pieces,
        *conv_other_pieces,
    )

    tokens_late = lax.optimization_barrier((tokens, pre, *ffn_pieces))[0]
    near = [k for k in range(1, ns) if k & (k - 1) == 0]
    token_pieces = [tokens] + [
        token_pieces[1 + near.index(k)] if k in near else exchange(tokens_late, "seq", k)
        for k in range(1, ns)
    ]
    late = lax.optimization_barrier((pre, *ffn_pieces[1:]))
    pre, ffn_pieces = late[0], [ffn_got, *late[1:]]
    ffn_other_pieces = [ffn_near] + [exchange(p, "row", 1) for p in ffn_pieces[1:]]

    layer_out, low, hidden, outer_grad, inner_grad, inner_full, vec_sums = vmem_call(
        functools.partial(ffn_kernel, nz, ns),
        [
            ((count, width), BF),
            ((count, width), BF),
            ((count, hid), BF),
            ((count, width), BF),
            ((count, hid), BF),
            ((nz, 2, in_rows, hid), BF),
            ((VEC_PAD, width), F32),
        ],
        [
            pltpu.VMEM((nz, 2, ns, part, width), BF),
            pltpu.VMEM((count, hid), F32),
            pltpu.VMEM((count, width), F32),
        ],
        kept=(0,),
    )(after, cot, vectors, ffn_own, ffn_other, *ffn_pieces, *ffn_other_pieces)

    mine, theirs = vmem_call(
        functools.partial(ffn_weight_kernel, nz, ns, in_rows, out_rows),
        [((ns, nz, ffn_rows, width), BF)] * 2,
        [pltpu.VMEM((hid, width), BF), pltpu.VMEM((width, hid), BF)],
    )(low, hidden, outer_grad, inner_grad)

    inner_grad, mine = lax.optimization_barrier((inner_grad, mine))
    results = vmem_call(
        functools.partial(back_kernel, ns, rows),
        [((count, width), F32), ((count, width), BF)]
        + [
            ((count + 2 * vec_rows + edge_rows(k), span), BF)
            for k in range(ns)
        ],
        [pltpu.VMEM((count, width), F32), pltpu.VMEM((VEC_PAD, width), F32)],
    )(pre, cot, vectors, inner_grad, inner_full, vec_sums)
    after_grad, conv_grad = results[:2]
    grad_pieces = list(results[2:])
    late = lax.optimization_barrier((theirs, *grad_pieces, *token_pieces))
    theirs, grad_pieces, token_pieces = late[0], list(late[1 : 1 + ns]), late[1 + ns :]
    arrived = exchange(theirs, "row", 1)
    grad_pieces = grad_pieces[:1] + [exchange(grad_pieces[k], "seq", k) for k in range(1, ns)]
    mine, grad_pieces[1] = lax.optimization_barrier((mine, grad_pieces[1]))
    flat = (ns * nz * ffn_rows, width)
    ffn_sums = split_sum([mine.reshape(flat), arrived.reshape(flat)], ns)
    ffn_sums = [ffn_sums[0]] + [exchange(ffn_sums[k], "seq", k) for k in range(1, ns)]

    mine, theirs = vmem_call(
        functools.partial(conv_weight_kernel, taps, nz, ns, in_rows),
        [((nz * conv_rows + 2 * vec_rows, span), BF)] * 2,
        [
            pltpu.VMEM((ns * length + 2 * half, span), F32),
            pltpu.VMEM((ns * length + 2 * half, LANES), jnp.int32),
            pltpu.VMEM((ns * count, taps * span), BF),
            pltpu.VMEM((width, taps * span), F32),
            pltpu.VMEM((ns, rows, length, width), BF),
            pltpu.SemaphoreType.DMA((ns,)),
        ],
        smem=1,
        loose=range(1, 1 + ns),
    )(contig_lengths, *token_pieces, *grad_pieces)
    arrived = exchange(theirs, "row", 1)
    sums = vmem_call(
        functools.partial(conv_core_kernel, conv_rows),
        [((conv_rows + 2 * vec_rows, span), BF)] * nz,
        slack=2,
    )(mine, arrived)
    sums = [sums[0]] + [exchange(sums[j], "row", 2 * j) for j in range(1, nz)]

    masks = [k for k in range(ns) if edge_rows(k)]
    (input_grad,) = vmem_call(
        functools.partial(input_grad_kernel, taps, ns, rows, masks),
        [((count, width), F32)],
        [
            pltpu.VMEM((length + 2 * half, width), F32),
            pltpu.VMEM((length + 2 * half, LANES), jnp.int32),
            pltpu.VMEM((taps, count, width), BF),
        ],
        smem=1,
        kept=(0,),
    )(contig_lengths, conv_grad, after_grad, conv_full, *[grad_pieces[k] for k in masks])
    sums[0], input_grad = lax.optimization_barrier((sums[0], input_grad))

    conv_sum, conv_square, vec_sum = vmem_call(
        functools.partial(conv_final_kernel, nz, vec_rows),
        [((conv_rows, span), BF), ((8, LANES), F32), ((VEC_ROWS, width), F32)],
        slack=2,
    )(*sums)
    conv_sums = [conv_sum] + [exchange(conv_sum, "seq", k) for k in range(1, ns)]

    ffn_sums = split_sum(ffn_sums, nz)
    ffn_sums = [ffn_sums[0]] + [exchange(ffn_sums[j], "row", 2 * j) for j in range(1, nz)]
    ffn_sums[0], conv_sums[-1] = lax.optimization_barrier((ffn_sums[0], conv_sums[-1]))
    (ffn_sum,) = vmem_call(
        functools.partial(ffn_final_kernel, nz), [((ffn_rows + VEC_PAD, width), BF)], slack=2
    )(*ffn_sums, conv_square)
    ffn_sums = [ffn_sum] + [exchange(ffn_sum, "seq", k) for k in range(1, ns)]
    (square,) = vmem_call(
        functools.partial(square_kernel, ns), [((8, LANES), F32)], slack=2
    )(*ffn_sums)
    squares = [square] + [exchange(square, "row", 2 * j) for j in range(1, nz)]
    (square,) = vmem_call(small_sum_kernel, [((8, LANES), F32)], slack=2)(*squares)
    squares = [square, exchange(square, "row", 1)]

    second_width = taps * width + hid + (out_rows // in_rows) * width + vectors.shape[0]
    results = [
        (conv_weight.shape, F32),
        (conv_weight.shape, F32),
        (inner_weight.shape, F32),
        (inner_weight.shape, F32),
        (outer_weight.shape, F32),
        (outer_weight.shape, F32),
        ((in_rows, second_width), F32),
    ]
    (
        norm,
        new_vectors,
        vector_first,
        new_conv,
        conv_first,
        new_inner,
        inner_first,
        new_outer,
        outer_first,
        second_moments,
    ) = vmem_call(
        functools.partial(adam_kernel, taps, ns),
        [((1, 1), F32), (vectors.shape, F32), (vectors.shape, F32), *results],
        [pltpu.VMEM(shape, dtype) for shape, dtype in results]
        + [
            pltpu.VMEM((width // LANES, out_rows, LANES), F32),
            pltpu.VMEM((width, LANES), F32),
            pltpu.SemaphoreType.DMA((14,)),
        ],
        kept=range(3),
        left=range(3, 10),
        slack=3,
    )(
        *conv_sums,
        *ffn_sums,
        vec_sum,
        *squares,
        conv_weight,
        inner_weight,
        outer_weight,
        vectors,
        conv_moments,
        inner_moments,
        outer_moments,
        vector_near,
    )
    return (
        layer_out.reshape(tokens.shape),
        input_grad.reshape(tokens.shape),
        norm.reshape(()),
        new_conv,
        conv_first,
        new_inner,
        inner_first,
        new_outer,
        outer_first,
        new_vectors,
        vector_first,
        second_moments,
    )


def solution(mesh):
    in_specs = (
        P("row", "seq", None),
        P("row", "seq", None),
        P("row", None),
        P(None, "row", None),
        P("row", None),
        P("row", None),
        P(),
        P(None, None, "row", None),
        P(None, "row", None),
        P(None, "row", None),
        P(),
    )
    out_specs = (
        P("row", "seq", None),
        P("row", "seq", None),
        P(),
        P(None, "row", None),
        P(None, "row", None),
        P("row", None),
        P("row", None),
        P("row", None),
        P("row", None),
        P(),
        P(),
        P("row", None),
    )
    return jax.shard_map(
        per_device, mesh=mesh, in_specs=in_specs, out_specs=out_specs, check_vma=False
    )
```
